128 devices in a mesh: row: 8 (over y, x_lo), col: 16 (over z, x_hi, core).
Axes of the slice: x: 4 (x_hi: 2, x_lo: 2; x = x_hi * 2 + x_lo), y: 4, z: 4, core: 2. Of those that a mesh axis runs over, the one named last changes fastest.
Arguments:
- teacher_feats: bfloat16 [64, 128, 4096], P(None, 'row', 'col'), may hold values from -6 to 6
- teacher_probs: float32 [8, 128, 4096], P(None, 'row', 'col'), may hold values from 0 to 1, as said below
- student_feats: bfloat16 [256, 128, 4096], P(None, 'row', 'col'), may hold values from 0 to 8
- conv_weight: bfloat16 [9, 256, 256], replicated, may hold values from -0.125 to 0.125
- class_weight: bfloat16 [256, 8], replicated, may hold values from -3 to 3
Outputs:
- refined: float32 [8, 128, 4096], P(None, 'row', 'col')
- feature_grad: bfloat16 [256, 128, 4096], P(None, 'row', 'col')
- grad_conv: float32 [9, 256, 256], replicated
- grad_class: float32 [256, 8], replicated
The draws below stay inside these ranges and needn't reach their ends.
Inputs may be any that keep to these rules, and one draw needn't show every extreme that they name: `teacher_probs`: at every pixel the 8 values are positive and sum to one.
All inputs are finite; a program needn't handle non-finite values.
Results may differ from the reference program's by a relative error of at most 0.002.
The reference program's roundings to bfloat16 on the way (of `hidden`, `error_term` and `back_error`) count: a program that leaves them out, or rounds other values in their place, can miss the bound.
Values may be sent and summed in bfloat16 or wider, within the bound.
No kernel may reach another device: no remote copies, remote signals or barrier semaphores. Data moves between devices by JAX's collectives and lax.ppermute only.
A program may use at most 128 MiB of HBM per device.

```python
import jax
import jax.numpy as jnp

TEACHER_CH = 64
STUDENT_CH = 256
HIDDEN_SIZE = 256
CLASSES = 8
ITERS = 4
ROWS_DEV = 16
COLS_DEV = 256
HEIGHT = 128
WIDTH = 4096


def draw_teacher_feats(key, part):
    value_key, scale_key = jax.random.split(jax.random.fold_in(key, 11))
    values = jax.random.truncated_normal(value_key, -4.0, 4.0, (TEACHER_CH, HEIGHT, WIDTH), jnp.float32)
    scales = jnp.exp(jax.random.uniform(scale_key, (1, HEIGHT, WIDTH), jnp.float32, jnp.log(0.3), jnp.log(1.5)))
    return (values * scales).astype(jnp.bfloat16)


def draw_teacher_probs(key, part):
    region_key, pixel_key = jax.random.split(jax.random.fold_in(key, 23))
    blocks = 2.0 * jax.random.normal(region_key, (CLASSES, 2 * HEIGHT // ROWS_DEV, 2 * WIDTH // COLS_DEV), jnp.float32)
    coarse = jnp.repeat(jnp.repeat(blocks, ROWS_DEV // 2, axis=1), COLS_DEV // 2, axis=2)
    logits = coarse + jax.random.normal(pixel_key, (CLASSES, HEIGHT, WIDTH), jnp.float32)
    return jax.nn.softmax(logits, axis=0).astype(jnp.float32)


def draw_student_feats(key, part):
    region_key, pixel_key = jax.random.split(jax.random.fold_in(key, 37))
    low_scale = 0.01
    low_value = 0.0
    block_scale = jnp.exp(jax.random.uniform(region_key, (1, 2 * HEIGHT // ROWS_DEV, 2 * WIDTH // COLS_DEV), jnp.float32, jnp.log(low_scale), jnp.log(10.0)))
    coarse = jnp.repeat(jnp.repeat(block_scale, ROWS_DEV // 2, axis=1), COLS_DEV // 2, axis=2)
    values = jax.random.uniform(pixel_key, (STUDENT_CH, HEIGHT, WIDTH), jnp.float32, low_value, 0.8)
    return (values * coarse).astype(jnp.bfloat16)


def noise(own_key, dims, spread, reach, kind=jnp.bfloat16):
    array = jax.random.normal(own_key, dims, jnp.float32) * spread
    return jnp.minimum(jnp.maximum(array, -reach), reach).astype(kind)


def setup_inputs(seed: int = 0) -> dict:
    streams_of = jax.random.split(jax.random.key(seed), 6)
    return {
        "teacher_feats": draw_teacher_feats(jax.random.fold_in(streams_of[5], 71), 0),
        "teacher_probs": draw_teacher_probs(jax.random.fold_in(streams_of[5], 71), 0),
        "student_feats": draw_student_feats(jax.random.fold_in(streams_of[5], 71), 0),
        "conv_weight": noise(streams_of[3], (9, STUDENT_CH, HIDDEN_SIZE), (9 * STUDENT_CH) ** -0.5, 0.125),
        "class_weight": noise(streams_of[4], (HIDDEN_SIZE, CLASSES), 0.5, 3.0),
    }


def tap_list():
    offsets = [(0, 0)]
    for radius in (1, 2, 4):
        for step_y in (-1, 0, 1):
            for step_x in (-1, 0, 1):
                if step_y != 0 or step_x != 0:
                    offsets.append((step_y * radius, step_x * radius))
    return offsets


def conv_taps():
    return [(off_y, off_x) for off_y in (-1, 0, 1) for off_x in (-1, 0, 1)]


def window(padded, margin, off_y, off_x, rows_here, cols_here):
    return padded[:, margin + off_y:margin + off_y + rows_here, margin + off_x:margin + off_x + cols_here]


def silu_slope(pre_act):
    logistic = jax.nn.sigmoid(pre_act)
    return logistic * (1.0 + pre_act * (1.0 - logistic))


def reference(teacher_feats, teacher_probs, student_feats, conv_weight, class_weight):
    rows_here, cols_here = teacher_probs.shape[1], teacher_probs.shape[2]
    margin = 4
    pad_spec = ((0, 0), (margin, margin), (margin, margin))
    features = jnp.pad(teacher_feats.astype(jnp.float32), pad_spec)
    inside = jnp.pad(jnp.ones((1, rows_here, cols_here), jnp.float32), pad_spec)
    center = window(features, margin, 0, 0, rows_here, cols_here)
    tap_terms = []
    for off_y, off_x in tap_list():
        neighbour = window(features, margin, off_y, off_x, rows_here, cols_here)
        distance = jnp.sum((center - neighbour) ** 2, axis=0)
        present = window(inside, margin, off_y, off_x, rows_here, cols_here)[0]
        tap_terms.append(present * jnp.exp(-distance / teacher_feats.shape[0]))
    stacked = jnp.stack(tap_terms)
    weights = stacked / jnp.sum(stacked, axis=0)
    current = teacher_probs
    for sweep_index in range(ITERS):
        padded = jnp.pad(current, pad_spec)
        running = jnp.zeros(current.shape, jnp.float32)
        for position, (off_y, off_x) in enumerate(tap_list()):
            running = running + weights[position][None] * window(padded, margin, off_y, off_x, rows_here, cols_here)
        current = running
    refined = current

    channels = student_feats.shape[0]
    pixels = rows_here * cols_here
    unit_pad = ((0, 0), (1, 1), (1, 1))
    student_pad = jnp.pad(student_feats, unit_pad)
    pre_act = jnp.zeros((conv_weight.shape[2], pixels), jnp.float32)
    for tap_index, (off_y, off_x) in enumerate(conv_taps()):
        shifted = window(student_pad, 1, off_y, off_x, rows_here, cols_here).reshape(channels, pixels)
        pre_act = pre_act + jnp.dot(conv_weight[tap_index].T, shifted, preferred_element_type=jnp.float32)
    hidden = jax.nn.silu(pre_act).astype(jnp.bfloat16)
    class_logit = jnp.dot(class_weight.T, hidden, preferred_element_type=jnp.float32)
    error_term = (jax.nn.sigmoid(class_logit) - refined.reshape(-1, pixels)).astype(jnp.bfloat16)
    back_sum = jnp.dot(class_weight, error_term, preferred_element_type=jnp.float32)
    back_error = (back_sum * silu_slope(pre_act)).astype(jnp.bfloat16)
    pixel_count = float(ROWS_DEV * COLS_DEV)
    grad_class = jnp.dot(hidden, error_term.T, preferred_element_type=jnp.float32) / pixel_count
    error_pad = jnp.pad(back_error.reshape(-1, rows_here, cols_here), unit_pad)
    conv_grads = []
    feature_sum = jnp.zeros((channels, pixels), jnp.float32)
    for tap_index, (off_y, off_x) in enumerate(conv_taps()):
        shifted = window(student_pad, 1, off_y, off_x, rows_here, cols_here).reshape(channels, pixels)
        conv_grads.append(jnp.dot(shifted, back_error.T, preferred_element_type=jnp.float32) / pixel_count)
        moved = window(error_pad, 1, -off_y, -off_x, rows_here, cols_here).reshape(-1, pixels)
        feature_sum = feature_sum + jnp.dot(conv_weight[tap_index], moved, preferred_element_type=jnp.float32)
    feature_grad = feature_sum.astype(jnp.bfloat16).reshape(channels, rows_here, cols_here)
    return refined, feature_grad, jnp.stack(conv_grads), grad_class
```

```python
import jax
import jax.numpy as jnp
from jax import lax
from jax.sharding import PartitionSpec as P

ITERS = 4


def with_halo(cells, sides, width):
    for axis, dim in sides:
        count = lax.axis_size(axis)
        ends = count - 1
        head = lax.slice_in_dim(cells, 0, width, axis=dim)
        tail = lax.slice_in_dim(cells, cells.shape[dim] - width, cells.shape[dim], axis=dim)
        cells = jnp.concatenate(
            [
                lax.ppermute(tail, axis, [(i, (i + 1) % count) for i in range(ends)]),
                cells,
                lax.ppermute(head, axis, [((i + 1) % count, i) for i in range(ends)]),
            ],
            axis=dim,
        )
    return cells


def tap_list():
    offsets = [(0, 0)]
    for radius in (1, 2, 4):
        for step_y in (-1, 0, 1):
            for step_x in (-1, 0, 1):
                if step_y != 0 or step_x != 0:
                    offsets.append((step_y * radius, step_x * radius))
    return offsets


def conv_taps():
    return [(off_y, off_x) for off_y in (-1, 0, 1) for off_x in (-1, 0, 1)]


def window(padded, margin, off_y, off_x, rows_here, cols_here):
    return padded[
        :, margin + off_y : margin + off_y + rows_here, margin + off_x : margin + off_x + cols_here
    ]


def silu_slope(pre_act):
    logistic = jax.nn.sigmoid(pre_act)
    return logistic * (1.0 + pre_act * (1.0 - logistic))


def line_inside(start, count, extend, full):
    places = start - extend + jnp.arange(count + 2 * extend, dtype=jnp.int32)
    return ((places >= 0) & (places < full)).astype(jnp.float32)


def affinity_weights(features, inside, extend, rows_here, cols_here):
    margin = 4
    span_y = rows_here + 2 * extend
    span_x = cols_here + 2 * extend
    center = features[:, margin : margin + span_y, margin : margin + span_x].astype(jnp.float32)
    tap_terms = []
    for position, (off_y, off_x) in enumerate(tap_list()):
        if position == 0:
            tap_terms.append(jnp.ones((span_y, span_x), jnp.float32))
        else:
            neighbour = features[
                :,
                margin + off_y : margin + off_y + span_y,
                margin + off_x : margin + off_x + span_x,
            ].astype(jnp.float32)
            distance = jnp.sum((center - neighbour) ** 2, axis=0)
            present = inside[
                margin + off_y : margin + off_y + span_y, margin + off_x : margin + off_x + span_x
            ]
            tap_terms.append(present * jnp.exp(-distance / features.shape[0]))
    stacked = jnp.stack(tap_terms)
    return stacked / jnp.sum(stacked, axis=0)


def propagate(weights, padded, span_y, span_x):
    running = jnp.zeros((padded.shape[0], span_y, span_x), jnp.float32)
    for position, (off_y, off_x) in enumerate(tap_list()):
        running = running + weights[position][None] * window(
            padded, 4, off_y, off_x, span_y, span_x
        )
    return running


def split_chunks(conv_part, class_part, devices):
    taps, channels, hidden = conv_part.shape
    tiles = conv_part.reshape(taps, channels // 8, 8, hidden // 128, 128).transpose(0, 1, 3, 2, 4)
    tiles = tiles.reshape(-1, 8, 128)
    whole = (tiles.shape[0] // devices) * devices
    head = tiles[:whole].reshape(devices, -1, 128)
    rest = tiles[whole:].reshape(devices, -1, 128)
    small = class_part.reshape(devices, -1)
    small = jnp.pad(small, ((0, 0), (0, 128 - small.shape[1])))[:, None, :]
    return head, rest, small


def join_chunks(chunks, shapes, devices):
    conv_shape, class_shape = shapes
    taps, channels, hidden = conv_shape
    n_tiles = taps * channels * hidden // 1024
    head_rows = (n_tiles // devices) * 8
    conv_rows = n_tiles * 8 // devices
    head = chunks[:, :head_rows].reshape(-1, 8, 128)
    rest = chunks[:, head_rows:conv_rows].reshape(-1, 8, 128)
    tiles = jnp.concatenate([head, rest], axis=0)
    tiles = tiles.reshape(taps, channels // 8, hidden // 128, 8, 128).transpose(0, 1, 3, 2, 4)
    small = chunks[:, conv_rows, : class_shape[0] * class_shape[1] // devices]
    return tiles.reshape(conv_shape), small.reshape(class_shape)


def shift_of(largest):
    return jnp.clip(jnp.ceil(jnp.log2(jnp.maximum(largest, 1e-30))), -100.0, 120.0)


def pack_half(values, exponent):
    scaled = (values * jnp.exp2(14.0 - exponent)).astype(jnp.float16)
    marks = jnp.broadcast_to(exponent, values.shape[:-2] + (1, 128)).astype(jnp.float16)
    rows = values.shape[-2]
    fill = -(-(rows + 1) // 8) * 8 - rows - 1
    zeros = jnp.zeros(values.shape[:-2] + (fill, 128), jnp.float16)
    return jnp.concatenate([scaled, marks, zeros], axis=-2)


def unpack_half(packed, rows):
    exponent = packed[..., rows : rows + 1, :1].astype(jnp.float32)
    return packed[..., :rows, :].astype(jnp.float32) * jnp.exp2(exponent - 14.0)


def sum_everywhere(conv_part, class_part, axes):
    devices = 1
    for axis in axes:
        devices = devices * lax.axis_size(axis)
    head, rest, small = split_chunks(conv_part, class_part, devices)
    values = jnp.concatenate([head, rest, small], axis=1)
    rows = values.shape[1]
    largest = jnp.maximum(jnp.max(jnp.abs(conv_part)), jnp.max(jnp.abs(class_part)))
    sent = pack_half(values, shift_of(largest))
    got = lax.all_to_all(sent, axes, split_axis=0, concat_axis=0, tiled=True)
    total = jnp.sum(unpack_half(got, rows), axis=0)
    mine = pack_half(total, shift_of(jnp.max(jnp.abs(total))))
    spread = jnp.broadcast_to(mine[None], (devices,) + mine.shape)
    everyone = lax.all_to_all(spread, axes, split_axis=0, concat_axis=0, tiled=True)
    return join_chunks(unpack_half(everyone, rows), (conv_part.shape, class_part.shape), devices)


def shards(teacher_feats, teacher_probs, student_feats, conv_weight, class_weight):
    rows_here, cols_here = (teacher_probs.shape[1], teacher_probs.shape[2])
    row_start = lax.axis_index("row") * rows_here
    col_start = lax.axis_index("col") * cols_here
    full_rows = rows_here * lax.axis_size("row")
    full_cols = cols_here * lax.axis_size("col")
    features = with_halo(teacher_feats, (("row", 1), ("col", 2)), 4)
    inside = (
        line_inside(row_start, rows_here, 4, full_rows)[:, None]
        * line_inside(col_start, cols_here, 4, full_cols)[None, :]
    )
    weights = affinity_weights(features, inside, 0, rows_here, cols_here)
    current = teacher_probs
    for sweep_index in range(ITERS):
        padded = with_halo(current, (("row", 1), ("col", 2)), 4)
        current = propagate(weights, padded, rows_here, cols_here)
    channels = student_feats.shape[0]
    pixels = rows_here * cols_here
    pixel_count = float(rows_here * cols_here)
    student_pad = with_halo(student_feats, (("row", 1), ("col", 2)), 1)
    pre_act = jnp.zeros((conv_weight.shape[2], pixels), jnp.float32)
    for tap_index, (off_y, off_x) in enumerate(conv_taps()):
        shifted = window(student_pad, 1, off_y, off_x, rows_here, cols_here).reshape(
            channels, pixels
        )
        pre_act = pre_act + jnp.einsum(
            "ch,cp->hp", conv_weight[tap_index], shifted, preferred_element_type=jnp.float32
        )
    hidden = jax.nn.silu(pre_act).astype(jnp.bfloat16)
    class_logit = jnp.einsum("hk,hp->kp", class_weight, hidden, preferred_element_type=jnp.float32)
    error_term = (jax.nn.sigmoid(class_logit) - current.reshape(-1, pixels)).astype(jnp.bfloat16)
    back_sum = jnp.einsum("hk,kp->hp", class_weight, error_term, preferred_element_type=jnp.float32)
    back_error = (back_sum * silu_slope(pre_act)).astype(jnp.bfloat16)
    class_part = jnp.einsum("hp,kp->hk", hidden, error_term, preferred_element_type=jnp.float32)
    error_pad = with_halo(back_error.reshape(-1, rows_here, cols_here), (("row", 1), ("col", 2)), 1)
    conv_parts = []
    feature_sum = jnp.zeros((channels, pixels), jnp.float32)
    for tap_index, (off_y, off_x) in enumerate(conv_taps()):
        shifted = window(student_pad, 1, off_y, off_x, rows_here, cols_here).reshape(
            channels, pixels
        )
        tap_part = jnp.einsum("cp,hp->ch", shifted, back_error, preferred_element_type=jnp.float32)
        conv_parts.append(tap_part)
        moved = window(error_pad, 1, -off_y, -off_x, rows_here, cols_here).reshape(-1, pixels)
        feature_sum = feature_sum + jnp.einsum(
            "ch,hp->cp", conv_weight[tap_index], moved, preferred_element_type=jnp.float32
        )
    feature_grad = feature_sum.astype(jnp.bfloat16).reshape(channels, rows_here, cols_here)
    summed_conv, summed_class = sum_everywhere(
        jnp.stack(conv_parts), class_part, ("row", "col")
    )
    grad_conv = summed_conv / pixel_count
    grad_class = summed_class / pixel_count
    return (current, feature_grad, grad_conv, grad_class)


def solution(mesh):
    in_specs = (P(None, "row", "col"), P(None, "row", "col"), P(None, "row", "col"), P(), P())
    out_specs = (P(None, "row", "col"), P(None, "row", "col"), P(), P())
    return jax.shard_map(shards, mesh=mesh, in_specs=in_specs, out_specs=out_specs, check_vma=False)
```

```python
import functools

import jax
import jax.numpy as jnp
from jax import lax
from jax.experimental import pallas as pl
from jax.experimental.pallas import tpu as pltpu
from jax.sharding import PartitionSpec as P


def with_halo(cells, sides, width):
    for axis, dim in sides:
        count = lax.axis_size(axis)
        ends = count - 1
        head = lax.slice_in_dim(cells, 0, width, axis=dim)
        tail = lax.slice_in_dim(cells, cells.shape[dim] - width, cells.shape[dim], axis=dim)
        cells = jnp.concatenate(
            [
                lax.ppermute(tail, axis, [(i, (i + 1) % count) for i in range(ends)]),
                cells,
                lax.ppermute(head, axis, [((i + 1) % count, i) for i in range(ends)]),
            ],
            axis=dim,
        )
    return cells


def conv_taps():
    return [(off_y, off_x) for off_y in (-1, 0, 1) for off_x in (-1, 0, 1)]


def window(padded, margin, off_y, off_x, rows_here, cols_here):
    return padded[
        :, margin + off_y : margin + off_y + rows_here, margin + off_x : margin + off_x + cols_here
    ]


def silu_slope(pre_act):
    logistic = jax.nn.sigmoid(pre_act)
    return logistic * (1.0 + pre_act * (1.0 - logistic))


EDGE_ROWS = 8
EDGE_COLS = 16
SPAN = 384
PAIR_TAPS = [tap for s in (1, 2, 4) for tap in ((0, s), (s, -s), (s, 0), (s, s))]


def shifted_by(cells, off_x):
    return cells if off_x == 0 else pltpu.roll(cells, (-off_x) % cells.shape[-1], cells.ndim - 1)


def lane_of(shape):
    return lax.broadcasted_iota(jnp.int32, shape, len(shape) - 1)


def edges_kernel(up_ref, mid_ref, down_ref, left_ref, right_ref):
    channels = mid_ref.shape[1]
    group = lane_of((channels, 128)) // EDGE_COLS
    sources = [up_ref] + [mid_ref.at[pl.ds(8 * g, 8)] for g in range(mid_ref.shape[0] // 8)] + [down_ref]
    for g, source in enumerate(sources):
        left = jnp.zeros((channels, 128), jnp.float32)
        right = jnp.zeros((channels, 128), jnp.float32)
        for i in range(8):
            first = source[i, :, :128].astype(jnp.float32)
            last = source[i, :, -128:].astype(jnp.float32)
            left = jnp.where(group == i, pltpu.roll(first, EDGE_COLS * i, 1), left)
            right = jnp.where(group == i, pltpu.roll(last, (EDGE_COLS * (i + 1)) % 128, 1), right)
        left_ref[g] = left.astype(left_ref.dtype)
        right_ref[g] = right.astype(right_ref.dtype)


def sweep_row(weights, center_row, read_row):
    total = weights(0) * read_row(center_row)
    for index, (off_y, off_x) in enumerate(PAIR_TAPS):
        total += weights(1 + index) * shifted_by(read_row(center_row + off_y), off_x)
        total += weights(13 + index) * shifted_by(read_row(center_row - off_y), -off_x)
    return total


def affinity_kernel(
    place_ref, up_ref, mid_ref, down_ref, left_ref, right_ref, current_ref, weights_ref,
    feats, probs, next_probs, pairs, *, full_rows, full_cols, feat_channels, classes,
):
    rows = mid_ref.shape[0]
    cols = mid_ref.shape[2]
    tall = rows + 2 * EDGE_ROWS
    channels = mid_ref.shape[1]
    lanes = lane_of((channels, 128))

    def gather(i, carry):
        for g in range(tall // 8):
            if g == 0:
                body = up_ref[i]
            elif g == tall // 8 - 1:
                body = down_ref[i]
            else:
                body = mid_ref[8 * (g - 1) + i]
            from_right = pltpu.roll(right_ref[g].astype(jnp.float32), (128 - EDGE_COLS * i) % 128, 1)
            from_left = pltpu.roll(left_ref[g].astype(jnp.float32), (240 - EDGE_COLS * i) % 128, 1)
            side = jnp.where(lanes < EDGE_COLS, from_right, jnp.where(lanes >= 128 - EDGE_COLS, from_left, 0.0))
            body = body.astype(jnp.float32)
            row = 8 * g + i
            high, low = feat_channels, feat_channels + classes
            feats[row, :, :cols] = body[:high]
            feats[row, :, cols:] = side[:high]
            probs[row, :, :cols] = body[high:low] + body[low:]
            probs[row, :, cols:] = side[high:low] + side[low:]
        return carry

    lax.fori_loop(0, 8, gather, 0)
    pairs[:, tall - 8 :, :] = jnp.zeros((len(PAIR_TAPS), 8, SPAN), jnp.float32)

    def distances(row, carry):
        sums = [jnp.zeros((8, SPAN), jnp.float32) for _ in PAIR_TAPS]
        for c in range(feat_channels // 8):
            here = feats[row, 8 * c : 8 * c + 8, :]
            there = {0: here}
            for index, (off_y, off_x) in enumerate(PAIR_TAPS):
                if off_y not in there:
                    there[off_y] = feats[row + off_y, 8 * c : 8 * c + 8, :]
                gap = here - shifted_by(there[off_y], off_x)
                sums[index] += gap * gap
        for index in range(len(PAIR_TAPS)):
            pairs[index, pl.ds(row, 1), :] = jnp.sum(sums[index], axis=0, keepdims=True)
        return carry

    lax.fori_loop(0, tall - 4, distances, 0)

    shape = (tall, SPAN)
    lane = lane_of(shape)
    row_at = place_ref[0] - EDGE_ROWS + lax.broadcasted_iota(jnp.int32, shape, 0)
    col_at = place_ref[1] + jnp.where(lane < cols + EDGE_COLS, lane, lane - SPAN)

    def inside(off_y, off_x):
        y, x = row_at + off_y, col_at + off_x
        return (y >= 0) & (y < full_rows) & (x >= 0) & (x < full_cols)

    here_inside = inside(0, 0)
    for index, (off_y, off_x) in enumerate(PAIR_TAPS):
        present = here_inside & inside(off_y, off_x)
        pairs[index] = jnp.where(present, jnp.exp(pairs[index] * (-1.0 / feat_channels)), 0.0)
    wide = rows + EDGE_ROWS
    total = jnp.ones((wide, SPAN), jnp.float32)
    for index, (off_y, off_x) in enumerate(PAIR_TAPS):
        ahead = pairs[index, 4 : 4 + wide, :]
        behind = shifted_by(pairs[index, 4 - off_y : 4 - off_y + wide, :], -off_x)
        weights_ref[1 + index] = ahead
        weights_ref[13 + index] = behind
        total = total + (ahead + behind)
    scale = 1.0 / total
    weights_ref[0] = scale
    for index in range(1, 25):
        weights_ref[index] = weights_ref[index] * scale
    two_sweeps(weights_ref, lambda row: probs[row], next_probs, current_ref, rows)


def two_sweeps(weights_ref, read_row, middle, out_ref, rows):
    def first(row, carry):
        middle[row] = sweep_row(lambda o: weights_ref[o, pl.ds(row, 1), :], row + 4, read_row)
        return carry

    lax.fori_loop(0, rows + 8, first, 0)

    def second(row, carry):
        value = sweep_row(lambda o: weights_ref[o, pl.ds(row + 4, 1), :], row + 4, lambda r: middle[r])
        out_ref[row] = value[:, : out_ref.shape[2]]
        return carry

    lax.fori_loop(0, rows, second, 0)


def finish_kernel(weights_ref, up_ref, mid_ref, down_ref, out_ref, probs, next_probs):
    rows = mid_ref.shape[0]
    probs[:EDGE_ROWS] = up_ref[...]
    probs[EDGE_ROWS : EDGE_ROWS + rows] = mid_ref[...]
    probs[EDGE_ROWS + rows :] = down_ref[...]
    two_sweeps(weights_ref, lambda row: probs[row], next_probs, out_ref, rows)


def pass_on(cells, axis, step):
    ends = lax.axis_size(axis) - 1
    if step > 0:
        return lax.ppermute(cells, axis, [(i, i + 1) for i in range(ends)])
    return lax.ppermute(cells, axis, [(i + 1, i) for i in range(ends)])


def refine(teacher_feats, teacher_probs):
    feat_channels, rows, cols = teacher_feats.shape
    classes = teacher_probs.shape[0]
    high = lax.reduce_precision(teacher_probs, 8, 7)
    low = teacher_probs - high
    mid = jnp.concatenate(
        [teacher_feats, high.astype(jnp.bfloat16), low.astype(jnp.bfloat16)], axis=0
    ).transpose(1, 0, 2)
    up = pass_on(mid[rows - EDGE_ROWS :], "row", 1)
    down = pass_on(mid[:EDGE_ROWS], "row", -1)
    channels = mid.shape[1]
    groups = (rows + 2 * EDGE_ROWS) // 8
    edge = jax.ShapeDtypeStruct((groups, channels, 128), jnp.bfloat16)
    to_left, to_right = pl.pallas_call(edges_kernel, out_shape=(edge, edge), name="edges")(up, mid, down)
    left = pass_on(to_right, "col", 1)
    right = pass_on(to_left, "col", -1)
    place = jnp.stack([lax.axis_index("row") * rows, lax.axis_index("col") * cols]).astype(jnp.int32)
    tall = rows + 2 * EDGE_ROWS
    vmem = pl.BlockSpec(memory_space=pltpu.VMEM)
    current, weights = pl.pallas_call(
        functools.partial(
            affinity_kernel,
            full_rows=rows * lax.axis_size("row"),
            full_cols=cols * lax.axis_size("col"),
            feat_channels=feat_channels,
            classes=classes,
        ),
        out_shape=(
            jax.ShapeDtypeStruct((rows, classes, SPAN), jnp.float32),
            jax.ShapeDtypeStruct((25, rows + EDGE_ROWS, SPAN), jnp.float32),
        ),
        in_specs=[pl.BlockSpec(memory_space=pltpu.SMEM)] + [vmem] * 5,
        out_specs=(vmem, vmem),
        scratch_shapes=[
            pltpu.VMEM((tall, feat_channels, SPAN), jnp.float32),
            pltpu.VMEM((tall, classes, SPAN), jnp.float32),
            pltpu.VMEM((rows + 8, classes, SPAN), jnp.float32),
            pltpu.VMEM((len(PAIR_TAPS), tall, SPAN), jnp.float32),
        ],
        name="affinity",
    )(place, up, mid, down, left, right)
    up = pass_on(current[rows - EDGE_ROWS :], "row", 1)
    down = pass_on(current[:EDGE_ROWS], "row", -1)
    refined = pl.pallas_call(
        finish_kernel,
        out_shape=jax.ShapeDtypeStruct((rows, classes, cols), jnp.float32),
        scratch_shapes=[
            pltpu.VMEM((tall, classes, SPAN), jnp.float32),
            pltpu.VMEM((rows + 8, classes, SPAN), jnp.float32),
        ],
        name="finish",
    )(weights, up, current, down)
    return refined.transpose(1, 0, 2)


def split_chunks(conv_part, class_part, devices):
    taps, channels, hidden = conv_part.shape
    tiles = conv_part.reshape(taps, channels // 8, 8, hidden // 128, 128).transpose(0, 1, 3, 2, 4)
    tiles = tiles.reshape(-1, 8, 128)
    whole = (tiles.shape[0] // devices) * devices
    head = tiles[:whole].reshape(devices, -1, 128)
    rest = tiles[whole:].reshape(devices, -1, 128)
    small = class_part.reshape(devices, -1)
    small = jnp.pad(small, ((0, 0), (0, 128 - small.shape[1])))[:, None, :]
    return head, rest, small


def join_chunks(chunks, shapes, devices):
    conv_shape, class_shape = shapes
    taps, channels, hidden = conv_shape
    n_tiles = taps * channels * hidden // 1024
    head_rows = (n_tiles // devices) * 8
    conv_rows = n_tiles * 8 // devices
    head = chunks[:, :head_rows].reshape(-1, 8, 128)
    rest = chunks[:, head_rows:conv_rows].reshape(-1, 8, 128)
    tiles = jnp.concatenate([head, rest], axis=0)
    tiles = tiles.reshape(taps, channels // 8, hidden // 128, 8, 128).transpose(0, 1, 3, 2, 4)
    small = chunks[:, conv_rows, : class_shape[0] * class_shape[1] // devices]
    return tiles.reshape(conv_shape), small.reshape(class_shape)


def shift_of(largest):
    return jnp.clip(jnp.ceil(jnp.log2(jnp.maximum(largest, 1e-30))), -100.0, 120.0)


def pack_half(values, exponent):
    scaled = (values * jnp.exp2(14.0 - exponent)).astype(jnp.float16)
    marks = jnp.broadcast_to(exponent, values.shape[:-2] + (1, 128)).astype(jnp.float16)
    rows = values.shape[-2]
    fill = -(-(rows + 1) // 8) * 8 - rows - 1
    zeros = jnp.zeros(values.shape[:-2] + (fill, 128), jnp.float16)
    return jnp.concatenate([scaled, marks, zeros], axis=-2)


def unpack_half(packed, rows):
    exponent = packed[..., rows : rows + 1, :1].astype(jnp.float32)
    return packed[..., :rows, :].astype(jnp.float32) * jnp.exp2(exponent - 14.0)


def sum_everywhere(conv_part, class_part, axes):
    devices = 1
    for axis in axes:
        devices = devices * lax.axis_size(axis)
    head, rest, small = split_chunks(conv_part, class_part, devices)
    values = jnp.concatenate([head, rest, small], axis=1)
    rows = values.shape[1]
    largest = jnp.maximum(jnp.max(jnp.abs(conv_part)), jnp.max(jnp.abs(class_part)))
    sent = pack_half(values, shift_of(largest))
    got = lax.all_to_all(sent, axes, split_axis=0, concat_axis=0, tiled=True)
    total = jnp.sum(unpack_half(got, rows), axis=0)
    mine = pack_half(total, shift_of(jnp.max(jnp.abs(total))))
    spread = jnp.broadcast_to(mine[None], (devices,) + mine.shape)
    everyone = lax.all_to_all(spread, axes, split_axis=0, concat_axis=0, tiled=True)
    return join_chunks(unpack_half(everyone, rows), (conv_part.shape, class_part.shape), devices)


def shards(teacher_feats, teacher_probs, student_feats, conv_weight, class_weight):
    rows_here, cols_here = (teacher_probs.shape[1], teacher_probs.shape[2])
    current = refine(teacher_feats, teacher_probs)
    channels = student_feats.shape[0]
    pixels = rows_here * cols_here
    pixel_count = float(rows_here * cols_here)
    student_pad = with_halo(student_feats, (("row", 1), ("col", 2)), 1)
    pre_act = jnp.zeros((conv_weight.shape[2], pixels), jnp.float32)
    for tap_index, (off_y, off_x) in enumerate(conv_taps()):
        shifted = window(student_pad, 1, off_y, off_x, rows_here, cols_here).reshape(
            channels, pixels
        )
        pre_act = pre_act + jnp.einsum(
            "ch,cp->hp", conv_weight[tap_index], shifted, preferred_element_type=jnp.float32
        )
    hidden = jax.nn.silu(pre_act).astype(jnp.bfloat16)
    class_logit = jnp.einsum("hk,hp->kp", class_weight, hidden, preferred_element_type=jnp.float32)
    error_term = (jax.nn.sigmoid(class_logit) - current.reshape(-1, pixels)).astype(jnp.bfloat16)
    back_sum = jnp.einsum("hk,kp->hp", class_weight, error_term, preferred_element_type=jnp.float32)
    back_error = (back_sum * silu_slope(pre_act)).astype(jnp.bfloat16)
    class_part = jnp.einsum("hp,kp->hk", hidden, error_term, preferred_element_type=jnp.float32)
    error_pad = with_halo(back_error.reshape(-1, rows_here, cols_here), (("row", 1), ("col", 2)), 1)
    conv_parts = []
    feature_sum = jnp.zeros((channels, pixels), jnp.float32)
    for tap_index, (off_y, off_x) in enumerate(conv_taps()):
        shifted = window(student_pad, 1, off_y, off_x, rows_here, cols_here).reshape(
            channels, pixels
        )
        tap_part = jnp.einsum("cp,hp->ch", shifted, back_error, preferred_element_type=jnp.float32)
        conv_parts.append(tap_part)
        moved = window(error_pad, 1, -off_y, -off_x, rows_here, cols_here).reshape(-1, pixels)
        feature_sum = feature_sum + jnp.einsum(
            "ch,hp->cp", conv_weight[tap_index], moved, preferred_element_type=jnp.float32
        )
    feature_grad = feature_sum.astype(jnp.bfloat16).reshape(channels, rows_here, cols_here)
    summed_conv, summed_class = sum_everywhere(
        jnp.stack(conv_parts), class_part, ("row", "col")
    )
    grad_conv = summed_conv / pixel_count
    grad_class = summed_class / pixel_count
    return (current, feature_grad, grad_conv, grad_class)


def solution(mesh):
    in_specs = (P(None, "row", "col"), P(None, "row", "col"), P(None, "row", "col"), P(), P())
    out_specs = (P(None, "row", "col"), P(None, "row", "col"), P(), P())
    return jax.shard_map(shards, mesh=mesh, in_specs=in_specs, out_specs=out_specs, check_vma=False)
```

```python
import functools

import jax
import jax.numpy as jnp
from jax import lax
from jax.experimental import pallas as pl
from jax.experimental.pallas import tpu as pltpu
from jax.sharding import PartitionSpec as P


EDGE_ROWS = 8
EDGE_COLS = 16
SPAN = 384
PAIR_TAPS = [tap for s in (1, 2, 4) for tap in ((0, s), (s, -s), (s, 0), (s, s))]


def shifted_by(cells, off_x):
    return cells if off_x == 0 else pltpu.roll(cells, (-off_x) % cells.shape[-1], cells.ndim - 1)


def vmem_of(mib):
    return pltpu.CompilerParams(vmem_limit_bytes=mib * 2**20)


def lane_of(shape):
    return lax.broadcasted_iota(jnp.int32, shape, len(shape) - 1)


def edges_kernel(up_ref, mid_ref, down_ref, left_ref, right_ref):
    channels = mid_ref.shape[1]
    group = lane_of((channels, 128)) // EDGE_COLS
    sources = [up_ref] + [mid_ref.at[pl.ds(8 * g, 8)] for g in range(mid_ref.shape[0] // 8)] + [down_ref]
    for g, source in enumerate(sources):
        left = jnp.zeros((channels, 128), jnp.float32)
        right = jnp.zeros((channels, 128), jnp.float32)
        for i in range(8):
            first = source[i, :, :128].astype(jnp.float32)
            last = source[i, :, -128:].astype(jnp.float32)
            left = jnp.where(group == i, pltpu.roll(first, EDGE_COLS * i, 1), left)
            right = jnp.where(group == i, pltpu.roll(last, (EDGE_COLS * (i + 1)) % 128, 1), right)
        left_ref[g] = left.astype(left_ref.dtype)
        right_ref[g] = right.astype(right_ref.dtype)


def sweep_row(weights, center_row, read_row):
    total = weights(0) * read_row(center_row)
    for index, (off_y, off_x) in enumerate(PAIR_TAPS):
        total += weights(1 + index) * shifted_by(read_row(center_row + off_y), off_x)
        total += weights(13 + index) * shifted_by(read_row(center_row - off_y), -off_x)
    return total


def affinity_kernel(
    place_ref, up_ref, mid_ref, down_ref, left_ref, right_ref, current_ref, weights_ref,
    feats, probs, next_probs, pairs, *, full_rows, full_cols, feat_channels, classes,
):
    rows = mid_ref.shape[0]
    cols = mid_ref.shape[2]
    tall = rows + 2 * EDGE_ROWS
    channels = mid_ref.shape[1]
    lanes = lane_of((channels, 128))

    def gather(i, carry):
        for g in range(tall // 8):
            if g == 0:
                body = up_ref[i]
            elif g == tall // 8 - 1:
                body = down_ref[i]
            else:
                body = mid_ref[8 * (g - 1) + i]
            from_right = pltpu.roll(right_ref[g].astype(jnp.float32), (128 - EDGE_COLS * i) % 128, 1)
            from_left = pltpu.roll(left_ref[g].astype(jnp.float32), (240 - EDGE_COLS * i) % 128, 1)
            side = jnp.where(lanes < EDGE_COLS, from_right, jnp.where(lanes >= 128 - EDGE_COLS, from_left, 0.0))
            body = body.astype(jnp.float32)
            row = 8 * g + i
            high, low = feat_channels, feat_channels + classes
            feats[row, :, :cols] = body[:high]
            feats[row, :, cols:] = side[:high]
            probs[row, :, :cols] = body[high:low] + body[low:]
            probs[row, :, cols:] = side[high:low] + side[low:]
        return carry

    lax.fori_loop(0, 8, gather, 0)
    pairs[:, tall - 8 :, :] = jnp.zeros((len(PAIR_TAPS), 8, SPAN), jnp.float32)

    def distances(row, carry):
        sums = [jnp.zeros((8, SPAN), jnp.float32) for _ in PAIR_TAPS]
        for c in range(feat_channels // 8):
            here = feats[row, 8 * c : 8 * c + 8, :]
            there = {0: here}
            for index, (off_y, off_x) in enumerate(PAIR_TAPS):
                if off_y not in there:
                    there[off_y] = feats[row + off_y, 8 * c : 8 * c + 8, :]
                gap = here - shifted_by(there[off_y], off_x)
                sums[index] += gap * gap
        for index in range(len(PAIR_TAPS)):
            pairs[index, pl.ds(row, 1), :] = jnp.sum(sums[index], axis=0, keepdims=True)
        return carry

    lax.fori_loop(0, tall - 4, distances, 0)

    shape = (tall, SPAN)
    lane = lane_of(shape)
    row_at = place_ref[0] - EDGE_ROWS + lax.broadcasted_iota(jnp.int32, shape, 0)
    col_at = place_ref[1] + jnp.where(lane < cols + EDGE_COLS, lane, lane - SPAN)

    def inside(off_y, off_x):
        y, x = row_at + off_y, col_at + off_x
        return (y >= 0) & (y < full_rows) & (x >= 0) & (x < full_cols)

    here_inside = inside(0, 0)
    for index, (off_y, off_x) in enumerate(PAIR_TAPS):
        present = here_inside & inside(off_y, off_x)
        pairs[index] = jnp.where(present, jnp.exp(pairs[index] * (-1.0 / feat_channels)), 0.0)
    wide = rows + EDGE_ROWS
    total = jnp.ones((wide, SPAN), jnp.float32)
    for index, (off_y, off_x) in enumerate(PAIR_TAPS):
        ahead = pairs[index, 4 : 4 + wide, :]
        behind = shifted_by(pairs[index, 4 - off_y : 4 - off_y + wide, :], -off_x)
        weights_ref[1 + index] = ahead
        weights_ref[13 + index] = behind
        total = total + (ahead + behind)
    scale = 1.0 / total
    weights_ref[0] = scale
    for index in range(1, 25):
        weights_ref[index] = weights_ref[index] * scale
    two_sweeps(weights_ref, lambda row: probs[row], next_probs, current_ref, rows)


def two_sweeps(weights_ref, read_row, middle, out_ref, rows):
    def first(row, carry):
        middle[row] = sweep_row(lambda o: weights_ref[o, pl.ds(row, 1), :], row + 4, read_row)
        return carry

    lax.fori_loop(0, rows + 8, first, 0)

    def second(row, carry):
        value = sweep_row(lambda o: weights_ref[o, pl.ds(row + 4, 1), :], row + 4, lambda r: middle[r])
        out_ref[row] = value[:, : out_ref.shape[2]]
        return carry

    lax.fori_loop(0, rows, second, 0)


def finish_kernel(weights_ref, up_ref, mid_ref, down_ref, out_ref, probs, next_probs):
    rows = mid_ref.shape[0]
    probs[:EDGE_ROWS] = up_ref[...]
    probs[EDGE_ROWS : EDGE_ROWS + rows] = mid_ref[...]
    probs[EDGE_ROWS + rows :] = down_ref[...]
    two_sweeps(weights_ref, lambda row: probs[row], next_probs, out_ref, rows)


def pass_on(cells, axis, step):
    ends = lax.axis_size(axis) - 1
    if step > 0:
        return lax.ppermute(cells, axis, [(i, i + 1) for i in range(ends)])
    return lax.ppermute(cells, axis, [(i + 1, i) for i in range(ends)])


def refine(teacher_feats, teacher_probs):
    feat_channels, rows, cols = teacher_feats.shape
    classes = teacher_probs.shape[0]
    high = lax.reduce_precision(teacher_probs, 8, 7)
    low = teacher_probs - high
    mid = jnp.concatenate(
        [teacher_feats, high.astype(jnp.bfloat16), low.astype(jnp.bfloat16)], axis=0
    ).transpose(1, 0, 2)
    up = pass_on(mid[rows - EDGE_ROWS :], "row", 1)
    down = pass_on(mid[:EDGE_ROWS], "row", -1)
    channels = mid.shape[1]
    groups = (rows + 2 * EDGE_ROWS) // 8
    edge = jax.ShapeDtypeStruct((groups, channels, 128), jnp.bfloat16)
    to_left, to_right = pl.pallas_call(edges_kernel, out_shape=(edge, edge), name="edges", compiler_params=vmem_of(12))(up, mid, down)
    left = pass_on(to_right, "col", 1)
    right = pass_on(to_left, "col", -1)
    place = jnp.stack([lax.axis_index("row") * rows, lax.axis_index("col") * cols]).astype(jnp.int32)
    tall = rows + 2 * EDGE_ROWS
    vmem = pl.BlockSpec(memory_space=pltpu.VMEM)
    current, weights = pl.pallas_call(
        functools.partial(
            affinity_kernel,
            full_rows=rows * lax.axis_size("row"),
            full_cols=cols * lax.axis_size("col"),
            feat_channels=feat_channels,
            classes=classes,
        ),
        out_shape=(
            jax.ShapeDtypeStruct((rows, classes, SPAN), jnp.float32),
            jax.ShapeDtypeStruct((25, rows + EDGE_ROWS, SPAN), jnp.float32),
        ),
        in_specs=[pl.BlockSpec(memory_space=pltpu.SMEM)] + [vmem] * 5,
        out_specs=(vmem, vmem),
        scratch_shapes=[
            pltpu.VMEM((tall, feat_channels, SPAN), jnp.float32),
            pltpu.VMEM((tall, classes, SPAN), jnp.float32),
            pltpu.VMEM((rows + 8, classes, SPAN), jnp.float32),
            pltpu.VMEM((len(PAIR_TAPS), tall, SPAN), jnp.float32),
        ],
        name="affinity",
        compiler_params=vmem_of(20),
    )(place, up, mid, down, left, right)
    up = pass_on(current[rows - EDGE_ROWS :], "row", 1)
    down = pass_on(current[:EDGE_ROWS], "row", -1)
    refined = pl.pallas_call(
        finish_kernel,
        out_shape=jax.ShapeDtypeStruct((rows, classes, cols), jnp.float32),
        scratch_shapes=[
            pltpu.VMEM((tall, classes, SPAN), jnp.float32),
            pltpu.VMEM((rows + 8, classes, SPAN), jnp.float32),
        ],
        name="finish",
        compiler_params=vmem_of(12),
    )(weights, up, current, down)
    return refined


def split_chunks(conv_part, class_part, devices):
    height, width = conv_part.shape
    tiles = conv_part.reshape(height // 8, 8, width // 128, 128).transpose(0, 2, 1, 3)
    tiles = tiles.reshape(-1, 8, 128)
    whole = (tiles.shape[0] // devices) * devices
    head = tiles[:whole].reshape(devices, -1, 128)
    rest = tiles[whole:].reshape(devices, -1, 128)
    small = class_part.reshape(devices, -1)
    small = jnp.pad(small, ((0, 0), (0, 128 - small.shape[1])))[:, None, :]
    return head, rest, small


def join_chunks(chunks, shapes, devices):
    conv_shape, class_shape = shapes
    channels, hidden = conv_shape[0] // 3, conv_shape[1] // 3
    n_tiles = 9 * channels * hidden // 1024
    head_rows = (n_tiles // devices) * 8
    conv_rows = n_tiles * 8 // devices
    head = chunks[:, :head_rows].reshape(-1, 8, 128)
    rest = chunks[:, head_rows:conv_rows].reshape(-1, 8, 128)
    tiles = jnp.concatenate([head, rest], axis=0)
    tiles = tiles.reshape(3, channels // 8, 3, hidden // 128, 8, 128).transpose(0, 2, 1, 4, 3, 5)
    small = chunks[:, conv_rows, : class_shape[0] * class_shape[1] // devices]
    return tiles.reshape(9, channels, hidden), small.reshape(class_shape)


def shift_of(largest):
    return jnp.clip(jnp.ceil(jnp.log2(jnp.maximum(largest, 1e-30))), -100.0, 120.0)


def pack_half(values, exponent):
    scaled = (values * jnp.exp2(14.0 - exponent)).astype(jnp.float16)
    marks = jnp.broadcast_to(exponent, values.shape[:-2] + (1, 128)).astype(jnp.float16)
    rows = values.shape[-2]
    fill = -(-(rows + 1) // 8) * 8 - rows - 1
    zeros = jnp.zeros(values.shape[:-2] + (fill, 128), jnp.float16)
    return jnp.concatenate([scaled, marks, zeros], axis=-2)


def unpack_half(packed, rows):
    exponent = packed[..., rows : rows + 1, :1].astype(jnp.float32)
    return packed[..., :rows, :].astype(jnp.float32) * jnp.exp2(exponent - 14.0)


def sum_everywhere(conv_part, class_part, axes):
    devices = 1
    for axis in axes:
        devices = devices * lax.axis_size(axis)
    head, rest, small = split_chunks(conv_part, class_part, devices)
    values = jnp.concatenate([head, rest, small], axis=1)
    rows = values.shape[1]
    largest = jnp.maximum(jnp.max(jnp.abs(conv_part)), jnp.max(jnp.abs(class_part)))
    sent = pack_half(values, shift_of(largest))
    got = lax.all_to_all(sent, axes, split_axis=0, concat_axis=0, tiled=True)
    total = jnp.sum(unpack_half(got, rows), axis=0)
    mine = pack_half(total, shift_of(jnp.max(jnp.abs(total))))
    spread = jnp.broadcast_to(mine[None], (devices,) + mine.shape)
    everyone = lax.all_to_all(spread, axes, split_axis=0, concat_axis=0, tiled=True)
    return join_chunks(unpack_half(everyone, rows), (conv_part.shape, class_part.shape), devices)


def unit_edges_kernel(up_ref, mid_ref, down_ref, left_ref, right_ref):
    rows, channels, cols = mid_ref.shape
    lanes = lane_of((channels, 128))
    left = jnp.zeros((channels, 128), jnp.float32)
    right = jnp.zeros((channels, 128), jnp.float32)
    for i in range(rows + 2):
        source = up_ref.at[0] if i == 0 else down_ref.at[0] if i == rows + 1 else mid_ref.at[i - 1]
        first = source[:, :128].astype(jnp.float32)
        last = source[:, cols - 128 :].astype(jnp.float32)
        left = jnp.where(lanes == i, pltpu.roll(first, i, 1), left)
        right = jnp.where(lanes == i, pltpu.roll(last, i + 1, 1), right)
    left_ref[...] = left.astype(left_ref.dtype)
    right_ref[...] = right.astype(right_ref.dtype)


def side_sums(side_ref, weights):
    side = side_ref[...].astype(jnp.float32)
    moved = [pltpu.roll(side, (128 - a) % 128, 1).astype(jnp.bfloat16) for a in range(3)]
    return jnp.dot(weights, jnp.concatenate(moved, axis=0), preferred_element_type=jnp.float32)


def conv_start(up_ref, mid_ref, down_ref, left_ref, right_ref, weights_ref, padded, left_sum, right_sum):
    rows, channels, _ = mid_ref.shape
    out = weights_ref.shape[0] // 3

    @pl.when(pl.program_id(0) == 0)
    def _():
        padded[0] = up_ref[0]
        padded[pl.ds(1, rows)] = mid_ref[...]
        padded[rows + 1] = down_ref[0]
        left_sum[...] = side_sums(left_ref, weights_ref[:out])
        right_sum[...] = side_sums(right_ref, weights_ref[2 * out :])


def conv_row(row, weights_ref, padded, left_sum, right_sum):
    out = weights_ref.shape[0] // 3
    cols = padded.shape[2]
    stack = jnp.concatenate([padded[row], padded[row + 1], padded[row + 2]], axis=0)
    parts = jnp.dot(weights_ref[...], stack, preferred_element_type=jnp.float32)
    lanes = lane_of((out, cols))
    left = jnp.concatenate([pltpu.roll(left_sum[...], (128 - row) % 128, 1), jnp.zeros((out, cols - 128), jnp.float32)], axis=1)
    right = jnp.concatenate([jnp.zeros((out, cols - 128), jnp.float32), pltpu.roll(right_sum[...], 127 - row, 1)], axis=1)
    before = jnp.where(lanes == 0, left, pltpu.roll(parts[:out], 1, 1))
    after = jnp.where(lanes == cols - 1, right, pltpu.roll(parts[2 * out :], cols - 1, 1))
    return parts[out : 2 * out] + (before + after)


STEP_ROWS = 2


def forward_kernel(
    up_ref, mid_ref, down_ref, left_ref, right_ref, weights_ref, class_ref,
    slope_ref, hidden_ref, guess_ref, padded, left_sum, right_sum,
):
    conv_start(up_ref, mid_ref, down_ref, left_ref, right_ref, weights_ref, padded, left_sum, right_sum)
    for k in range(STEP_ROWS):
        pre_act = conv_row(pl.program_id(0) * STEP_ROWS + k, weights_ref, padded, left_sum, right_sum)
        logistic = jax.nn.sigmoid(pre_act)
        slope_ref[k] = logistic * (1.0 + pre_act * (1.0 - logistic))
        hidden = (pre_act * logistic).astype(jnp.bfloat16)
        hidden_ref[k] = hidden
        logit = jnp.dot(class_ref[...], hidden, preferred_element_type=jnp.float32)
        guess_ref[k] = jax.nn.sigmoid(logit)


def back_kernel(guess_ref, refined_ref, slope_ref, class_ref, back_ref, error_ref):
    for k in range(STEP_ROWS):
        error = (guess_ref[k] - refined_ref[k]).astype(jnp.bfloat16)
        error_ref[k] = error
        summed = jnp.dot(class_ref[...], error, preferred_element_type=jnp.float32)
        back_ref[k] = (summed * slope_ref[k]).astype(jnp.bfloat16)


CONTRACT_LAST = (((1,), (1,)), ((), ()))


def grads_kernel(
    up_ref, mid_ref, down_ref, left_ref, right_ref, back_ref, hidden_ref, error_ref,
    conv_ref, class_ref, padded, first_cols, last_cols,
):
    rows, channels, cols = mid_ref.shape
    step = pl.program_id(0)

    @pl.when(step == 0)
    def _():
        padded[0] = up_ref[0]
        padded[pl.ds(1, rows)] = mid_ref[...]
        padded[rows + 1] = down_ref[0]
        conv_ref[...] = jnp.zeros(conv_ref.shape, jnp.float32)
        class_ref[...] = jnp.zeros(class_ref.shape, jnp.float32)
        first_cols[...] = jnp.zeros(first_cols.shape, jnp.float32)
        last_cols[...] = jnp.zeros(last_cols.shape, jnp.float32)

    lanes = lane_of((back_ref.shape[1], cols))
    narrow = lane_of((back_ref.shape[1], 128))
    images, backs = [], []
    for k in range(STEP_ROWS):
        row = step * STEP_ROWS + k
        images.append(jnp.concatenate([padded[row], padded[row + 1], padded[row + 2]], axis=0))
        back = back_ref[k].astype(jnp.float32)
        first_cols[...] = jnp.where(narrow == row + 1, pltpu.roll(back[:, :128], row + 1, 1), first_cols[...])
        last_cols[...] = jnp.where(narrow == row + 1, pltpu.roll(back[:, cols - 128 :], row + 2, 1), last_cols[...])
        below = jnp.where(lanes == cols - 1, 0.0, pltpu.roll(back, cols - 1, 1))
        above = jnp.where(lanes == 0, 0.0, pltpu.roll(back, 1, 1))
        backs.append(
            jnp.concatenate([below.astype(jnp.bfloat16), back_ref[k], above.astype(jnp.bfloat16)], axis=0)
        )
        class_ref[...] += lax.dot_general(
            hidden_ref[k], error_ref[k], CONTRACT_LAST, preferred_element_type=jnp.float32
        )
    conv_ref[...] += lax.dot_general(
        jnp.concatenate(images, axis=1), jnp.concatenate(backs, axis=1), CONTRACT_LAST,
        preferred_element_type=jnp.float32,
    )

    @pl.when(step == pl.num_programs(0) - 1)
    def _():
        hidden = back_ref.shape[1]
        for side_ref, cells, place in ((left_ref, first_cols, 0), (right_ref, last_cols, 2 * hidden)):
            side = side_ref[...].astype(jnp.float32)
            moved = [pltpu.roll(side, (1 - a) % 128, 1).astype(jnp.bfloat16) for a in range(3)]
            conv_ref[:, pl.ds(place, hidden)] += lax.dot_general(
                jnp.concatenate(moved, axis=0), cells[...].astype(jnp.bfloat16), CONTRACT_LAST,
                preferred_element_type=jnp.float32,
            )


def feature_kernel(
    up_ref, mid_ref, down_ref, left_ref, right_ref, weights_ref, out_ref, padded, left_sum, right_sum
):
    conv_start(up_ref, mid_ref, down_ref, left_ref, right_ref, weights_ref, padded, left_sum, right_sum)
    for k in range(STEP_ROWS):
        row = pl.program_id(0) * STEP_ROWS + k
        out_ref[k] = conv_row(row, weights_ref, padded, left_sum, right_sum).astype(out_ref.dtype)


def whole(array):
    return pl.BlockSpec(array.shape, lambda i: (0,) * array.ndim)


def by_rows(shape):
    return pl.BlockSpec((STEP_ROWS,) + shape[1:], lambda i: (i, 0, 0))


def unit_rows(cells):
    return pass_on(cells[-1:], "row", 1), pass_on(cells[:1], "row", -1)


def unit_cols(cells, up, down):
    edge = jax.ShapeDtypeStruct((cells.shape[1], 128), cells.dtype)
    to_left, to_right = pl.pallas_call(
        unit_edges_kernel, out_shape=(edge, edge), name="unit_edges",
        compiler_params=vmem_of(16),
    )(up, cells, down)
    return pass_on(to_right, "col", 1), pass_on(to_left, "col", -1)


def conv_scratch(rows, channels, cols, out):
    return [
        pltpu.VMEM((rows + 2, channels, cols), jnp.bfloat16),
        pltpu.VMEM((out, 128), jnp.float32),
        pltpu.VMEM((out, 128), jnp.float32),
    ]


def row_call(kernel, name, rows, args, arg_rows, outs, out_rows, scratch, vmem):
    return pl.pallas_call(
        kernel,
        grid=(rows // STEP_ROWS,),
        in_specs=[by_rows(a.shape) if split else whole(a) for a, split in zip(args, arg_rows)],
        out_specs=tuple(by_rows(o.shape) if split else whole(o) for o, split in zip(outs, out_rows)),
        out_shape=tuple(outs),
        scratch_shapes=scratch,
        name=name,
        compiler_params=vmem_of(vmem),
    )(*args)


def shards(teacher_feats, teacher_probs, student_feats, conv_weight, class_weight):
    channels, rows, cols = student_feats.shape
    hidden_size, classes = class_weight.shape
    pixel_count = float(rows * cols)
    taps = conv_weight.reshape(3, 3, channels, hidden_size)
    forward_weight = taps.transpose(1, 3, 0, 2).reshape(3 * hidden_size, 3 * channels)
    back_weight = taps[::-1, ::-1].transpose(1, 2, 0, 3).reshape(3 * channels, 3 * hidden_size)
    student = student_feats.transpose(1, 0, 2)
    student_up, student_down = unit_rows(student)
    student_left, student_right = unit_cols(student, student_up, student_down)
    halo = (student_up, student, student_down, student_left, student_right)
    f32, bf16 = jnp.float32, jnp.bfloat16
    slope, hidden, guess = row_call(
        forward_kernel, "forward", rows,
        halo + (forward_weight, class_weight.T), [False] * 7,
        [
            jax.ShapeDtypeStruct((rows, hidden_size, cols), f32),
            jax.ShapeDtypeStruct((rows, hidden_size, cols), bf16),
            jax.ShapeDtypeStruct((rows, classes, cols), f32),
        ],
        [True] * 3, conv_scratch(rows, channels, cols, hidden_size), 32,
    )
    refined = refine(teacher_feats, teacher_probs)
    back, error = row_call(
        back_kernel, "back", rows, (guess, refined, slope, class_weight), [True, True, True, False],
        [
            jax.ShapeDtypeStruct((rows, hidden_size, cols), bf16),
            jax.ShapeDtypeStruct((rows, classes, cols), bf16),
        ],
        [True] * 2, [], 16,
    )
    back_up, back_down = unit_rows(back)
    conv_part, class_part = row_call(
        grads_kernel, "grads", rows, halo + (back, hidden, error), [False] * 5 + [True] * 3,
        [
            jax.ShapeDtypeStruct((3 * channels, 3 * hidden_size), f32),
            jax.ShapeDtypeStruct((hidden_size, classes), f32),
        ],
        [False] * 2,
        [pltpu.VMEM((rows + 2, channels, cols), bf16)] + [pltpu.VMEM((hidden_size, 128), f32)] * 2, 40,
    )
    back_left, back_right = unit_cols(back, back_up, back_down)
    (feature_grad,) = row_call(
        feature_kernel, "feature", rows,
        (back_up, back, back_down, back_left, back_right, back_weight), [False] * 6,
        [jax.ShapeDtypeStruct((rows, channels, cols), bf16)],
        [True], conv_scratch(rows, hidden_size, cols, channels), 32,
    )
    summed_conv, summed_class = sum_everywhere(conv_part, class_part, ("row", "col"))
    grad_conv = summed_conv / pixel_count
    grad_class = summed_class / pixel_count
    return (refined.transpose(1, 0, 2), feature_grad.transpose(1, 0, 2), grad_conv, grad_class)


def solution(mesh):
    in_specs = (P(None, "row", "col"), P(None, "row", "col"), P(None, "row", "col"), P(), P())
    out_specs = (P(None, "row", "col"), P(None, "row", "col"), P(), P())
    return jax.shard_map(shards, mesh=mesh, in_specs=in_specs, out_specs=out_specs, check_vma=False)
```

```python
import functools

import jax
import jax.numpy as jnp
from jax import lax
from jax.experimental import pallas as pl
from jax.experimental.pallas import tpu as pltpu
from jax.sharding import PartitionSpec as P


EDGE_ROWS = 8
EDGE_COLS = 16
SPAN = 384
PAIR_TAPS = [tap for s in (1, 2, 4) for tap in ((0, s), (s, -s), (s, 0), (s, s))]


def shifted_by(cells, off_x):
    return cells if off_x == 0 else pltpu.roll(cells, (-off_x) % cells.shape[-1], cells.ndim - 1)


def vmem_of(mib):
    return pltpu.CompilerParams(vmem_limit_bytes=mib * 2**20)


def cost_of(micros):
    return pl.CostEstimate(flops=int(micros * 1e9), transcendentals=0, bytes_accessed=int(micros * 3e6))


def lane_of(shape):
    return lax.broadcasted_iota(jnp.int32, shape, len(shape) - 1)


def edges_kernel(up_ref, mid_ref, down_ref, left_ref, right_ref):
    channels = mid_ref.shape[1]
    group = lane_of((channels, 128)) // EDGE_COLS
    sources = [up_ref] + [mid_ref.at[pl.ds(8 * g, 8)] for g in range(mid_ref.shape[0] // 8)] + [down_ref]
    for g, source in enumerate(sources):
        left = jnp.zeros((channels, 128), jnp.float32)
        right = jnp.zeros((channels, 128), jnp.float32)
        for i in range(8):
            first = source[i, :, :128].astype(jnp.float32)
            last = source[i, :, -128:].astype(jnp.float32)
            left = jnp.where(group == i, pltpu.roll(first, EDGE_COLS * i, 1), left)
            right = jnp.where(group == i, pltpu.roll(last, (EDGE_COLS * (i + 1)) % 128, 1), right)
        left_ref[g] = left.astype(left_ref.dtype)
        right_ref[g] = right.astype(right_ref.dtype)


def sweep_row(weights, center_row, read_row):
    total = weights(0) * read_row(center_row)
    for index, (off_y, off_x) in enumerate(PAIR_TAPS):
        total += weights(1 + index) * shifted_by(read_row(center_row + off_y), off_x)
        total += weights(13 + index) * shifted_by(read_row(center_row - off_y), -off_x)
    return total


def affinity_kernel(
    place_ref, up_ref, mid_ref, down_ref, left_ref, right_ref, current_ref, weights_ref,
    feats, probs, next_probs, pairs, squares, *, full_rows, full_cols, feat_channels, classes,
):
    rows = mid_ref.shape[0]
    cols = mid_ref.shape[2]
    tall = rows + 2 * EDGE_ROWS
    channels = mid_ref.shape[1]
    lanes = lane_of((channels, 128))

    def gather(i, carry):
        for g in range(tall // 8):
            if g == 0:
                body = up_ref[i]
            elif g == tall // 8 - 1:
                body = down_ref[i]
            else:
                body = mid_ref[8 * (g - 1) + i]
            from_right = pltpu.roll(right_ref[g].astype(jnp.float32), (128 - EDGE_COLS * i) % 128, 1)
            from_left = pltpu.roll(left_ref[g].astype(jnp.float32), (240 - EDGE_COLS * i) % 128, 1)
            side = jnp.where(lanes < EDGE_COLS, from_right, jnp.where(lanes >= 128 - EDGE_COLS, from_left, 0.0))
            body = body.astype(jnp.float32)
            row = 8 * g + i
            high, low = feat_channels, feat_channels + classes
            feats[row, :, :cols] = body[:high]
            feats[row, :, cols:] = side[:high]
            probs[row, :, :cols] = body[high:low] + body[low:]
            probs[row, :, cols:] = side[high:low] + side[low:]
        return carry

    lax.fori_loop(0, 8, gather, 0)
    pairs[:, tall - 8 :, :] = jnp.zeros((len(PAIR_TAPS), 8, SPAN), jnp.float32)

    def distances(row, carry):
        sums = [None for _ in PAIR_TAPS]
        for c in range(feat_channels // 8):
            here = feats[row, 8 * c : 8 * c + 8, :]
            there = {0: here}
            for index, (off_y, off_x) in enumerate(PAIR_TAPS):
                if off_y not in there:
                    there[off_y] = feats[row + off_y, 8 * c : 8 * c + 8, :]
                product = here * shifted_by(there[off_y], off_x)
                sums[index] = product if c == 0 else sums[index] + product
        for index in range(len(PAIR_TAPS)):
            pairs[index, pl.ds(row, 1), :] = jnp.sum(sums[index], axis=0, keepdims=True)
        return carry

    lax.fori_loop(0, tall - 4, distances, 0)

    def sizes(row, carry):
        cells = feats[row]
        squares[pl.ds(row, 1), :] = jnp.sum(cells * cells, axis=0, keepdims=True)
        return carry

    lax.fori_loop(0, tall, sizes, 0, unroll=4)
    squares[tall:, :] = jnp.zeros((8, SPAN), jnp.float32)

    shape = (tall, SPAN)
    lane = lane_of(shape)
    row_at = place_ref[0] - EDGE_ROWS + lax.broadcasted_iota(jnp.int32, shape, 0)
    col_at = place_ref[1] + jnp.where(lane < cols + EDGE_COLS, lane, lane - SPAN)

    def inside(off_y, off_x):
        y, x = row_at + off_y, col_at + off_x
        return (y >= 0) & (y < full_rows) & (x >= 0) & (x < full_cols)

    here_inside = inside(0, 0)
    for index, (off_y, off_x) in enumerate(PAIR_TAPS):
        present = here_inside & inside(off_y, off_x)
        both = squares[:tall, :] + shifted_by(squares[off_y : off_y + tall, :], off_x)
        distance = jnp.maximum(both - 2.0 * pairs[index], 0.0)
        pairs[index] = jnp.where(present, jnp.exp(distance * (-1.0 / feat_channels)), 0.0)
    wide = rows + EDGE_ROWS
    total = jnp.ones((wide, SPAN), jnp.float32)
    for index, (off_y, off_x) in enumerate(PAIR_TAPS):
        ahead = pairs[index, 4 : 4 + wide, :]
        behind = shifted_by(pairs[index, 4 - off_y : 4 - off_y + wide, :], -off_x)
        weights_ref[1 + index] = ahead
        weights_ref[13 + index] = behind
        total = total + (ahead + behind)
    scale = 1.0 / total
    weights_ref[0] = scale
    for index in range(1, 25):
        weights_ref[index] = weights_ref[index] * scale
    two_sweeps(weights_ref, lambda row: probs[row], next_probs, current_ref, rows)


def two_sweeps(weights_ref, read_row, middle, out_ref, rows):
    def first(row, carry):
        middle[row] = sweep_row(lambda o: weights_ref[o, pl.ds(row, 1), :], row + 4, read_row)
        return carry

    lax.fori_loop(0, rows + 8, first, 0, unroll=4)

    def second(row, carry):
        value = sweep_row(lambda o: weights_ref[o, pl.ds(row + 4, 1), :], row + 4, lambda r: middle[r])
        out_ref[row] = value[:, : out_ref.shape[2]]
        return carry

    lax.fori_loop(0, rows, second, 0, unroll=4)


def finish_kernel(weights_ref, up_ref, mid_ref, down_ref, out_ref, probs, next_probs):
    rows = mid_ref.shape[0]
    probs[:EDGE_ROWS] = up_ref[...]
    probs[EDGE_ROWS : EDGE_ROWS + rows] = mid_ref[...]
    probs[EDGE_ROWS + rows :] = down_ref[...]
    two_sweeps(weights_ref, lambda row: probs[row], next_probs, out_ref, rows)


def pass_on(cells, axis, step):
    ends = lax.axis_size(axis) - 1
    if step > 0:
        return lax.ppermute(cells, axis, [(i, i + 1) for i in range(ends)])
    return lax.ppermute(cells, axis, [(i + 1, i) for i in range(ends)])


def refine(teacher_feats, teacher_probs, student):
    feat_channels, rows, cols = teacher_feats.shape
    classes = teacher_probs.shape[0]
    high = lax.reduce_precision(teacher_probs, 8, 7)
    low = teacher_probs - high
    mid = jnp.concatenate(
        [teacher_feats, high.astype(jnp.bfloat16), low.astype(jnp.bfloat16)], axis=0
    ).transpose(1, 0, 2)
    up = pass_on(mid[rows - EDGE_ROWS :], "row", 1)
    down = pass_on(mid[:EDGE_ROWS], "row", -1)
    student_rows = unit_rows(student)
    channels = mid.shape[1]
    groups = (rows + 2 * EDGE_ROWS) // 8
    edge = jax.ShapeDtypeStruct((groups, channels, 128), jnp.bfloat16)
    to_left, to_right = pl.pallas_call(edges_kernel, out_shape=(edge, edge), name="edges", compiler_params=vmem_of(12), cost_estimate=cost_of(1))(up, mid, down)
    left = pass_on(to_right, "col", 1)
    right = pass_on(to_left, "col", -1)
    left, right, student_left, student_right = lax.optimization_barrier(
        (left, right) + unit_cols(student, *student_rows)
    )
    place = jnp.stack([lax.axis_index("row") * rows, lax.axis_index("col") * cols]).astype(jnp.int32)
    tall = rows + 2 * EDGE_ROWS
    vmem = pl.BlockSpec(memory_space=pltpu.VMEM)
    current, weights = pl.pallas_call(
        functools.partial(
            affinity_kernel,
            full_rows=rows * lax.axis_size("row"),
            full_cols=cols * lax.axis_size("col"),
            feat_channels=feat_channels,
            classes=classes,
        ),
        out_shape=(
            jax.ShapeDtypeStruct((rows, classes, SPAN), jnp.float32),
            jax.ShapeDtypeStruct((25, rows + EDGE_ROWS, SPAN), jnp.float32),
        ),
        in_specs=[pl.BlockSpec(memory_space=pltpu.SMEM)] + [vmem] * 5,
        out_specs=(vmem, vmem),
        scratch_shapes=[
            pltpu.VMEM((tall, feat_channels, SPAN), jnp.float32),
            pltpu.VMEM((tall, classes, SPAN), jnp.float32),
            pltpu.VMEM((rows + 8, classes, SPAN), jnp.float32),
            pltpu.VMEM((len(PAIR_TAPS), tall, SPAN), jnp.float32),
            pltpu.VMEM((tall + 8, SPAN), jnp.float32),
        ],
        name="affinity",
        compiler_params=vmem_of(20),
        cost_estimate=cost_of(12),
    )(place, up, mid, down, left, right)
    return current, weights, student_rows + (student_left, student_right)


def finish(current, weights, cols):
    rows, classes, _ = current.shape
    tall = rows + 2 * EDGE_ROWS
    up = pass_on(current[rows - EDGE_ROWS :], "row", 1)
    down = pass_on(current[:EDGE_ROWS], "row", -1)
    refined = pl.pallas_call(
        finish_kernel,
        out_shape=jax.ShapeDtypeStruct((rows, classes, cols), jnp.float32),
        scratch_shapes=[
            pltpu.VMEM((tall, classes, SPAN), jnp.float32),
            pltpu.VMEM((rows + 8, classes, SPAN), jnp.float32),
        ],
        name="finish",
        compiler_params=vmem_of(12),
        cost_estimate=cost_of(4),
    )(weights, up, current, down)
    return refined


def split_chunks(conv_part, class_part, devices):
    height, width = conv_part.shape
    tiles = conv_part.reshape(height // 8, 8, width // 128, 128).transpose(0, 2, 1, 3)
    tiles = tiles.reshape(-1, 8, 128)
    whole = (tiles.shape[0] // devices) * devices
    head = tiles[:whole].reshape(devices, -1, 128)
    rest = tiles[whole:].reshape(devices, -1, 128)
    small = class_part.reshape(devices, -1)
    small = jnp.pad(small, ((0, 0), (0, 128 - small.shape[1])))[:, None, :]
    return head, rest, small


def join_chunks(chunks, shapes, devices):
    conv_shape, class_shape = shapes
    channels, hidden = conv_shape[0] // 3, conv_shape[1] // 3
    n_tiles = 9 * channels * hidden // 1024
    head_rows = (n_tiles // devices) * 8
    conv_rows = n_tiles * 8 // devices
    head = chunks[:, :head_rows].reshape(-1, 8, 128)
    rest = chunks[:, head_rows:conv_rows].reshape(-1, 8, 128)
    tiles = jnp.concatenate([head, rest], axis=0)
    tiles = tiles.reshape(3, channels // 8, 3, hidden // 128, 8, 128).transpose(0, 2, 1, 4, 3, 5)
    small = chunks[:, conv_rows, : class_shape[0] * class_shape[1] // devices]
    return tiles.reshape(9, channels, hidden), small.reshape(class_shape)


def shift_of(largest):
    return jnp.clip(jnp.ceil(jnp.log2(jnp.maximum(largest, 1e-30))), -100.0, 120.0)


def pack_half(values, exponent):
    scaled = (values * jnp.exp2(14.0 - exponent)).astype(jnp.float16)
    marks = jnp.broadcast_to(exponent, values.shape[:-2] + (1, 128)).astype(jnp.float16)
    rows = values.shape[-2]
    fill = -(-(rows + 1) // 8) * 8 - rows - 1
    zeros = jnp.zeros(values.shape[:-2] + (fill, 128), jnp.float16)
    return jnp.concatenate([scaled, marks, zeros], axis=-2)


def unpack_half(packed, rows):
    exponent = packed[..., rows : rows + 1, :1].astype(jnp.float32)
    return packed[..., :rows, :].astype(jnp.float32) * jnp.exp2(exponent - 14.0)


def sum_everywhere(conv_part, class_part, axes):
    devices = 1
    for axis in axes:
        devices = devices * lax.axis_size(axis)
    head, rest, small = split_chunks(conv_part, class_part, devices)
    values = jnp.concatenate([head, rest, small], axis=1)
    rows = values.shape[1]
    largest = jnp.maximum(jnp.max(jnp.abs(conv_part)), jnp.max(jnp.abs(class_part)))
    sent = pack_half(values, shift_of(largest))
    got = lax.all_to_all(sent, axes, split_axis=0, concat_axis=0, tiled=True)
    total = jnp.sum(unpack_half(got, rows), axis=0)
    mine = pack_half(total, shift_of(jnp.max(jnp.abs(total))))
    spread = jnp.broadcast_to(mine[None], (devices,) + mine.shape)
    everyone = lax.all_to_all(spread, axes, split_axis=0, concat_axis=0, tiled=True)
    return join_chunks(unpack_half(everyone, rows), (conv_part.shape, class_part.shape), devices)


def unit_edges_kernel(up_ref, mid_ref, down_ref, left_ref, right_ref):
    rows, channels, cols = mid_ref.shape
    lanes = lane_of((channels, 128))
    left = jnp.zeros((channels, 128), jnp.float32)
    right = jnp.zeros((channels, 128), jnp.float32)
    for i in range(rows + 2):
        source = up_ref.at[0] if i == 0 else down_ref.at[0] if i == rows + 1 else mid_ref.at[i - 1]
        first = source[:, :128].astype(jnp.float32)
        last = source[:, cols - 128 :].astype(jnp.float32)
        left = jnp.where(lanes == i, pltpu.roll(first, i, 1), left)
        right = jnp.where(lanes == i, pltpu.roll(last, i + 1, 1), right)
    left_ref[...] = left.astype(left_ref.dtype)
    right_ref[...] = right.astype(right_ref.dtype)


def side_sums(side_ref, weights):
    side = side_ref[...].astype(jnp.float32)
    moved = [pltpu.roll(side, (128 - a) % 128, 1).astype(jnp.bfloat16) for a in range(3)]
    return jnp.dot(weights, jnp.concatenate(moved, axis=0), preferred_element_type=jnp.float32)


def conv_start(
    up_ref, mid_ref, down_ref, left_ref, right_ref, taps_ref, padded, left_sum, right_sum, weights_ref, forward
):
    rows, channels, _ = mid_ref.shape
    out = weights_ref.shape[0] // 3

    @pl.when(pl.program_id(0) == 0)
    def _():
        for b in range(3):
            for a in range(3):
                tap = taps_ref[3 * a + b].T if forward else taps_ref[3 * (2 - a) + (2 - b)]
                weights_ref[out * b : out * (b + 1), channels * a : channels * (a + 1)] = tap
        padded[0] = up_ref[0]
        padded[pl.ds(1, rows)] = mid_ref[...]
        padded[rows + 1] = down_ref[0]
        left_sum[...] = side_sums(left_ref, weights_ref[:out])
        right_sum[...] = side_sums(right_ref, weights_ref[2 * out :])


def conv_row(row, weights_ref, padded, left_sum, right_sum):
    out = weights_ref.shape[0] // 3
    cols = padded.shape[2]
    stack = jnp.concatenate([padded[row], padded[row + 1], padded[row + 2]], axis=0)
    parts = jnp.dot(weights_ref[...], stack, preferred_element_type=jnp.float32)
    lanes = lane_of((out, 128))
    before = pltpu.roll(parts[:out], 1, 1)
    after = pltpu.roll(parts[2 * out :], cols - 1, 1)
    left = pltpu.roll(left_sum[...], (128 - row) % 128, 1)
    right = pltpu.roll(right_sum[...], 127 - row, 1)
    before = jnp.concatenate([jnp.where(lanes == 0, left, before[:, :128]), before[:, 128:]], axis=1)
    after = jnp.concatenate([after[:, :-128], jnp.where(lanes == 127, right, after[:, -128:])], axis=1)
    return parts[out : 2 * out] + (before + after)


STEP_ROWS = 2


def forward_kernel(
    up_ref, mid_ref, down_ref, left_ref, right_ref, taps_ref, class_ref,
    slope_ref, hidden_ref, guess_ref, padded, left_sum, right_sum, weights_ref,
):
    conv_start(
        up_ref, mid_ref, down_ref, left_ref, right_ref, taps_ref, padded, left_sum, right_sum, weights_ref, True
    )
    for k in range(STEP_ROWS):
        pre_act = conv_row(pl.program_id(0) * STEP_ROWS + k, weights_ref, padded, left_sum, right_sum)
        logistic = 0.5 * jnp.tanh(0.5 * pre_act) + 0.5
        silu = pre_act * logistic
        slope_ref[k] = logistic + silu * (1.0 - logistic)
        hidden = silu.astype(jnp.bfloat16)
        hidden_ref[k] = hidden
        logit = jnp.dot(class_ref[...], hidden, preferred_element_type=jnp.float32)
        guess_ref[k] = jax.nn.sigmoid(logit)


def back_kernel(guess_ref, refined_ref, slope_ref, class_ref, back_ref, error_ref):
    for k in range(STEP_ROWS):
        error = (guess_ref[k] - refined_ref[k]).astype(jnp.bfloat16)
        error_ref[k] = error
        summed = jnp.dot(class_ref[...], error, preferred_element_type=jnp.float32)
        back_ref[k] = (summed * slope_ref[k]).astype(jnp.bfloat16)


CONTRACT_LAST = (((1,), (1,)), ((), ()))


def grads_kernel(
    up_ref, mid_ref, down_ref, left_ref, right_ref, back_ref, hidden_ref, error_ref,
    conv_ref, class_ref, padded, first_cols, last_cols,
):
    rows, channels, cols = mid_ref.shape
    step = pl.program_id(0)

    @pl.when(step == 0)
    def _():
        padded[0] = up_ref[0]
        padded[pl.ds(1, rows)] = mid_ref[...]
        padded[rows + 1] = down_ref[0]
        conv_ref[...] = jnp.zeros(conv_ref.shape, jnp.float32)
        class_ref[...] = jnp.zeros(class_ref.shape, jnp.float32)
        first_cols[...] = jnp.zeros(first_cols.shape, jnp.float32)
        last_cols[...] = jnp.zeros(last_cols.shape, jnp.float32)

    lanes = lane_of((back_ref.shape[1], cols))
    narrow = lane_of((back_ref.shape[1], 128))
    images, backs = [], []
    for k in range(STEP_ROWS):
        row = step * STEP_ROWS + k
        images.append(jnp.concatenate([padded[row], padded[row + 1], padded[row + 2]], axis=0))
        back = back_ref[k].astype(jnp.float32)
        first_cols[...] = jnp.where(narrow == row + 1, pltpu.roll(back[:, :128], row + 1, 1), first_cols[...])
        last_cols[...] = jnp.where(narrow == row + 1, pltpu.roll(back[:, cols - 128 :], row + 2, 1), last_cols[...])
        below = jnp.where(lanes == cols - 1, 0.0, pltpu.roll(back, cols - 1, 1))
        above = jnp.where(lanes == 0, 0.0, pltpu.roll(back, 1, 1))
        backs.append(
            jnp.concatenate([below.astype(jnp.bfloat16), back_ref[k], above.astype(jnp.bfloat16)], axis=0)
        )
        class_ref[...] += lax.dot_general(
            hidden_ref[k], error_ref[k], CONTRACT_LAST, preferred_element_type=jnp.float32
        )
    conv_ref[...] += lax.dot_general(
        jnp.concatenate(images, axis=1), jnp.concatenate(backs, axis=1), CONTRACT_LAST,
        preferred_element_type=jnp.float32,
    )

    @pl.when(step == pl.num_programs(0) - 1)
    def _():
        hidden = back_ref.shape[1]
        for side_ref, cells, place in ((left_ref, first_cols, 0), (right_ref, last_cols, 2 * hidden)):
            side = side_ref[...].astype(jnp.float32)
            moved = [pltpu.roll(side, (1 - a) % 128, 1).astype(jnp.bfloat16) for a in range(3)]
            conv_ref[:, pl.ds(place, hidden)] += lax.dot_general(
                jnp.concatenate(moved, axis=0), cells[...].astype(jnp.bfloat16), CONTRACT_LAST,
                preferred_element_type=jnp.float32,
            )


def feature_kernel(
    up_ref, mid_ref, down_ref, left_ref, right_ref, taps_ref, out_ref, padded, left_sum, right_sum, weights_ref
):
    conv_start(
        up_ref, mid_ref, down_ref, left_ref, right_ref, taps_ref, padded, left_sum, right_sum, weights_ref, False
    )
    for k in range(STEP_ROWS):
        row = pl.program_id(0) * STEP_ROWS + k
        out_ref[k] = conv_row(row, weights_ref, padded, left_sum, right_sum).astype(out_ref.dtype)


def whole(array):
    return pl.BlockSpec(array.shape, lambda i: (0,) * array.ndim)


def by_rows(shape):
    return pl.BlockSpec((STEP_ROWS,) + shape[1:], lambda i: (i, 0, 0))


def unit_rows(cells):
    return pass_on(cells[-1:], "row", 1), pass_on(cells[:1], "row", -1)


def unit_cols(cells, up, down):
    edge = jax.ShapeDtypeStruct((cells.shape[1], 128), cells.dtype)
    to_left, to_right = pl.pallas_call(
        unit_edges_kernel, out_shape=(edge, edge), name="unit_edges",
        compiler_params=vmem_of(16),
        cost_estimate=cost_of(1),
    )(up, cells, down)
    return pass_on(to_right, "col", 1), pass_on(to_left, "col", -1)


def conv_scratch(rows, channels, cols, out):
    return [
        pltpu.VMEM((rows + 2, channels, cols), jnp.bfloat16),
        pltpu.VMEM((out, 128), jnp.float32),
        pltpu.VMEM((out, 128), jnp.float32),
        pltpu.VMEM((3 * out, 3 * channels), jnp.bfloat16),
    ]


def row_call(kernel, name, rows, args, arg_rows, outs, out_rows, scratch, vmem, micros):
    return pl.pallas_call(
        kernel,
        grid=(rows // STEP_ROWS,),
        in_specs=[by_rows(a.shape) if split else whole(a) for a, split in zip(args, arg_rows)],
        out_specs=tuple(by_rows(o.shape) if split else whole(o) for o, split in zip(outs, out_rows)),
        out_shape=tuple(outs),
        scratch_shapes=scratch,
        name=name,
        compiler_params=vmem_of(vmem),
        cost_estimate=cost_of(micros),
    )(*args)


def shards(teacher_feats, teacher_probs, student_feats, conv_weight, class_weight):
    channels, rows, cols = student_feats.shape
    hidden_size, classes = class_weight.shape
    pixel_count = float(rows * cols)
    student = student_feats.transpose(1, 0, 2)
    current, weights, student_halo = refine(teacher_feats, teacher_probs, student)
    halo = (student_halo[0], student, student_halo[1]) + student_halo[2:]
    f32, bf16 = jnp.float32, jnp.bfloat16
    slope, hidden, guess = row_call(
        forward_kernel, "forward", rows,
        halo + (conv_weight, class_weight.T), [False] * 7,
        [
            jax.ShapeDtypeStruct((rows, hidden_size, cols), f32),
            jax.ShapeDtypeStruct((rows, hidden_size, cols), bf16),
            jax.ShapeDtypeStruct((rows, classes, cols), f32),
        ],
        [True] * 3, conv_scratch(rows, channels, cols, hidden_size), 32, 12,
    )
    refined = finish(current, weights, cols)
    back, error = row_call(
        back_kernel, "back", rows, (guess, refined, slope, class_weight), [True, True, True, False],
        [
            jax.ShapeDtypeStruct((rows, hidden_size, cols), bf16),
            jax.ShapeDtypeStruct((rows, classes, cols), bf16),
        ],
        [True] * 2, [], 16, 2,
    )
    back_up, back_down = unit_rows(back)
    conv_part, class_part = row_call(
        grads_kernel, "grads", rows, halo + (back, hidden, error), [False] * 5 + [True] * 3,
        [
            jax.ShapeDtypeStruct((3 * channels, 3 * hidden_size), f32),
            jax.ShapeDtypeStruct((hidden_size, classes), f32),
        ],
        [False] * 2,
        [pltpu.VMEM((rows + 2, channels, cols), bf16)] + [pltpu.VMEM((hidden_size, 128), f32)] * 2, 40, 9,
    )
    back_left, back_right, conv_part, class_part = lax.optimization_barrier(
        unit_cols(back, back_up, back_down) + (conv_part, class_part)
    )
    (feature_grad,) = row_call(
        feature_kernel, "feature", rows,
        (back_up, back, back_down, back_left, back_right, conv_weight), [False] * 6,
        [jax.ShapeDtypeStruct((rows, channels, cols), bf16)],
        [True], conv_scratch(rows, hidden_size, cols, channels), 32, 8,
    )
    summed_conv, summed_class = sum_everywhere(conv_part, class_part, ("row", "col"))
    grad_conv = summed_conv / pixel_count
    grad_class = summed_class / pixel_count
    return (refined.transpose(1, 0, 2), feature_grad.transpose(1, 0, 2), grad_conv, grad_class)


def solution(mesh):
    in_specs = (P(None, "row", "col"), P(None, "row", "col"), P(None, "row", "col"), P(), P())
    out_specs = (P(None, "row", "col"), P(None, "row", "col"), P(), P())
    return jax.shard_map(shards, mesh=mesh, in_specs=in_specs, out_specs=out_specs, check_vma=False)
```

```python
import functools
import math

import jax
import jax.numpy as jnp
from jax import lax
from jax.experimental import pallas as pl
from jax.experimental.pallas import tpu as pltpu
from jax.sharding import Mesh
from jax.sharding import PartitionSpec as P


EDGE_ROWS = 8
EDGE_COLS = 16
SPAN = 384
PAIR_TAPS = [tap for s in (1, 2, 4) for tap in ((0, s), (s, -s), (s, 0), (s, s))]


def shifted_by(cells, off_x):
    return cells if off_x == 0 else pltpu.roll(cells, (-off_x) % cells.shape[-1], cells.ndim - 1)


def vmem_of(mib):
    return pltpu.CompilerParams(vmem_limit_bytes=mib * 2**20)


def cost_of(micros):
    return pl.CostEstimate(flops=int(micros * 1e9), transcendentals=0, bytes_accessed=int(micros * 3e6))


def lane_of(shape):
    return lax.broadcasted_iota(jnp.int32, shape, len(shape) - 1)


def edges_kernel(up_ref, mid_ref, down_ref, left_ref, right_ref):
    channels = mid_ref.shape[1]
    group = lane_of((channels, 128)) // EDGE_COLS
    sources = [up_ref] + [mid_ref.at[pl.ds(8 * g, 8)] for g in range(mid_ref.shape[0] // 8)] + [down_ref]
    for g, source in enumerate(sources):
        left = jnp.zeros((channels, 128), jnp.float32)
        right = jnp.zeros((channels, 128), jnp.float32)
        for i in range(8):
            first = source[i, :, :128].astype(jnp.float32)
            last = source[i, :, -128:].astype(jnp.float32)
            left = jnp.where(group == i, pltpu.roll(first, EDGE_COLS * i, 1), left)
            right = jnp.where(group == i, pltpu.roll(last, (EDGE_COLS * (i + 1)) % 128, 1), right)
        left_ref[g] = left.astype(left_ref.dtype)
        right_ref[g] = right.astype(right_ref.dtype)


def sweep_row(weights, center_row, read_row):
    total = weights(0) * read_row(center_row)
    for index, (off_y, off_x) in enumerate(PAIR_TAPS):
        total += weights(1 + index) * shifted_by(read_row(center_row + off_y), off_x)
        total += weights(13 + index) * shifted_by(read_row(center_row - off_y), -off_x)
    return total


def affinity_kernel(
    place_ref, up_ref, mid_ref, down_ref, left_ref, right_ref, current_ref, weights_ref,
    feats, probs, next_probs, pairs, squares, *, full_rows, full_cols, feat_channels, classes,
):
    rows = mid_ref.shape[0]
    cols = mid_ref.shape[2]
    tall = rows + 2 * EDGE_ROWS
    channels = mid_ref.shape[1]
    lanes = lane_of((channels, 128))

    def gather(i, carry):
        for g in range(tall // 8):
            if g == 0:
                body = up_ref[i]
            elif g == tall // 8 - 1:
                body = down_ref[i]
            else:
                body = mid_ref[8 * (g - 1) + i]
            from_right = pltpu.roll(right_ref[g].astype(jnp.float32), (128 - EDGE_COLS * i) % 128, 1)
            from_left = pltpu.roll(left_ref[g].astype(jnp.float32), (240 - EDGE_COLS * i) % 128, 1)
            side = jnp.where(lanes < EDGE_COLS, from_right, jnp.where(lanes >= 128 - EDGE_COLS, from_left, 0.0))
            body = body.astype(jnp.float32)
            row = 8 * g + i
            high, low = feat_channels, feat_channels + classes
            feats[row, :, :cols] = body[:high]
            feats[row, :, cols:] = side[:high]
            probs[row, :, :cols] = body[high:low] + body[low:]
            probs[row, :, cols:] = side[high:low] + side[low:]
        return carry

    lax.fori_loop(0, 8, gather, 0)
    pairs[:, tall - 8 :, :] = jnp.zeros((len(PAIR_TAPS), 8, SPAN), jnp.float32)

    def distances(row, carry):
        sums = [None for _ in PAIR_TAPS]
        for c in range(feat_channels // 8):
            here = feats[row, 8 * c : 8 * c + 8, :]
            there = {0: here}
            for index, (off_y, off_x) in enumerate(PAIR_TAPS):
                if off_y not in there:
                    there[off_y] = feats[row + off_y, 8 * c : 8 * c + 8, :]
                product = here * shifted_by(there[off_y], off_x)
                sums[index] = product if c == 0 else sums[index] + product
        for index in range(len(PAIR_TAPS)):
            pairs[index, pl.ds(row, 1), :] = jnp.sum(sums[index], axis=0, keepdims=True)
        return carry

    lax.fori_loop(0, tall - 4, distances, 0)

    def sizes(row, carry):
        cells = feats[row]
        squares[pl.ds(row, 1), :] = jnp.sum(cells * cells, axis=0, keepdims=True)
        return carry

    lax.fori_loop(0, tall, sizes, 0, unroll=4)
    squares[tall:, :] = jnp.zeros((8, SPAN), jnp.float32)

    shape = (tall, SPAN)
    lane = lane_of(shape)
    row_at = place_ref[0] - EDGE_ROWS + lax.broadcasted_iota(jnp.int32, shape, 0)
    col_at = place_ref[1] + jnp.where(lane < cols + EDGE_COLS, lane, lane - SPAN)

    def inside(off_y, off_x):
        y, x = row_at + off_y, col_at + off_x
        return (y >= 0) & (y < full_rows) & (x >= 0) & (x < full_cols)

    here_inside = inside(0, 0)
    for index, (off_y, off_x) in enumerate(PAIR_TAPS):
        present = here_inside & inside(off_y, off_x)
        both = squares[:tall, :] + shifted_by(squares[off_y : off_y + tall, :], off_x)
        distance = jnp.maximum(both - 2.0 * pairs[index], 0.0)
        pairs[index] = jnp.where(present, jnp.exp(distance * (-1.0 / feat_channels)), 0.0)
    wide = rows + EDGE_ROWS
    total = jnp.ones((wide, SPAN), jnp.float32)
    for index, (off_y, off_x) in enumerate(PAIR_TAPS):
        ahead = pairs[index, 4 : 4 + wide, :]
        behind = shifted_by(pairs[index, 4 - off_y : 4 - off_y + wide, :], -off_x)
        weights_ref[1 + index] = ahead
        weights_ref[13 + index] = behind
        total = total + (ahead + behind)
    scale = 1.0 / total
    weights_ref[0] = scale
    for index in range(1, 25):
        weights_ref[index] = weights_ref[index] * scale
    two_sweeps(weights_ref, lambda row: probs[row], next_probs, current_ref, rows)


def two_sweeps(weights_ref, read_row, middle, out_ref, rows):
    def first(row, carry):
        middle[row] = sweep_row(lambda o: weights_ref[o, pl.ds(row, 1), :], row + 4, read_row)
        return carry

    lax.fori_loop(0, rows + 8, first, 0, unroll=4)

    def second(row, carry):
        value = sweep_row(lambda o: weights_ref[o, pl.ds(row + 4, 1), :], row + 4, lambda r: middle[r])
        out_ref[row] = value[:, : out_ref.shape[2]]
        return carry

    lax.fori_loop(0, rows, second, 0, unroll=4)


def finish_kernel(weights_ref, up_ref, mid_ref, down_ref, out_ref, probs, next_probs):
    rows = mid_ref.shape[0]
    probs[:EDGE_ROWS] = up_ref[...]
    probs[EDGE_ROWS : EDGE_ROWS + rows] = mid_ref[...]
    probs[EDGE_ROWS + rows :] = down_ref[...]
    two_sweeps(weights_ref, lambda row: probs[row], next_probs, out_ref, rows)


COL = ("pair", "core")


def size_of(axes):
    return math.prod(lax.axis_size(a) for a in axes) if isinstance(axes, tuple) else lax.axis_size(axes)


def pass_on(cells, axis, step):
    ends = size_of(axis) - 1
    if step > 0:
        return lax.ppermute(cells, axis, [(i, i + 1) for i in range(ends)])
    return lax.ppermute(cells, axis, [(i + 1, i) for i in range(ends)])


def teacher_rows(teacher_feats, teacher_probs):
    rows = teacher_feats.shape[1]
    high = lax.reduce_precision(teacher_probs, 8, 7)
    low = teacher_probs - high
    mid = jnp.concatenate(
        [teacher_feats, high.astype(jnp.bfloat16), low.astype(jnp.bfloat16)], axis=0
    ).transpose(1, 0, 2)
    return mid, pass_on(mid[rows - EDGE_ROWS :], "row", 1), pass_on(mid[:EDGE_ROWS], "row", -1)


def refine(mid, up, down, feat_channels, classes):
    rows, _, cols = mid.shape
    channels = mid.shape[1]
    groups = (rows + 2 * EDGE_ROWS) // 8
    edge = jax.ShapeDtypeStruct((groups, channels, 128), jnp.bfloat16)
    to_left, to_right = pl.pallas_call(edges_kernel, out_shape=(edge, edge), name="edges", compiler_params=vmem_of(12), cost_estimate=cost_of(1))(up, mid, down)
    left = pass_on(to_right, COL, 1)
    right = pass_on(to_left, COL, -1)
    place = jnp.stack([lax.axis_index("row") * rows, lax.axis_index(COL) * cols]).astype(jnp.int32)
    tall = rows + 2 * EDGE_ROWS
    vmem = pl.BlockSpec(memory_space=pltpu.VMEM)
    current, weights = pl.pallas_call(
        functools.partial(
            affinity_kernel,
            full_rows=rows * lax.axis_size("row"),
            full_cols=cols * size_of(COL),
            feat_channels=feat_channels,
            classes=classes,
        ),
        out_shape=(
            jax.ShapeDtypeStruct((rows, classes, SPAN), jnp.float32),
            jax.ShapeDtypeStruct((25, rows + EDGE_ROWS, SPAN), jnp.float32),
        ),
        in_specs=[pl.BlockSpec(memory_space=pltpu.SMEM)] + [vmem] * 5,
        out_specs=(vmem, vmem),
        scratch_shapes=[
            pltpu.VMEM((tall, feat_channels, SPAN), jnp.float32),
            pltpu.VMEM((tall, classes, SPAN), jnp.float32),
            pltpu.VMEM((rows + 8, classes, SPAN), jnp.float32),
            pltpu.VMEM((len(PAIR_TAPS), tall, SPAN), jnp.float32),
            pltpu.VMEM((tall + 8, SPAN), jnp.float32),
        ],
        name="affinity",
        compiler_params=vmem_of(20),
        cost_estimate=cost_of(12),
    )(place, up, mid, down, left, right)
    return current, weights


def finish(current, weights, cols):
    rows, classes, _ = current.shape
    tall = rows + 2 * EDGE_ROWS
    up = pass_on(current[rows - EDGE_ROWS :], "row", 1)
    down = pass_on(current[:EDGE_ROWS], "row", -1)
    refined = pl.pallas_call(
        finish_kernel,
        out_shape=jax.ShapeDtypeStruct((rows, classes, cols), jnp.float32),
        scratch_shapes=[
            pltpu.VMEM((tall, classes, SPAN), jnp.float32),
            pltpu.VMEM((rows + 8, classes, SPAN), jnp.float32),
        ],
        name="finish",
        compiler_params=vmem_of(12),
        cost_estimate=cost_of(4),
    )(weights, up, current, down)
    return refined


CHIPS = ("row", "pair")
PARTNER = [(0, 1), (1, 0)]
CLASS_ROW = 36
MARK_ROW = 37
CHUNK_ROWS = 40


def tile_places(n_tiles, chips):
    full = n_tiles // chips
    for tile in range(n_tiles):
        if tile < full * chips:
            yield tile, 0, 8, tile // full, 8 * (tile % full)
        else:
            share = 8 * (n_tiles - full * chips) // chips
            for part in range(8 // share):
                chip = (tile - full * chips) * (8 // share) + part
                yield tile, part * share, share, chip, 8 * full


def write_chunks(chunk_ref, conv_ref, class_ref, half):
    height, width = conv_ref.shape[0] // 2, conv_ref.shape[1]
    chips = chunk_ref.shape[0]
    first = pl.multiple_of(half * height, height)
    chunk_ref[:, CLASS_ROW:, :] = jnp.zeros((chips, CHUNK_ROWS - CLASS_ROW, 128), jnp.float32)
    for tile, skip, count, chip, row in tile_places(height * width // 1024, chips):
        block, lane = tile // (width // 128), tile % (width // 128)
        rows = conv_ref[pl.ds(pl.multiple_of(first + 8 * block, 8), 8), 128 * lane : 128 * (lane + 1)]
        chunk_ref[chip, row : row + count, :] = rows[skip : skip + count]
    sums = jnp.where(half == 0, class_ref[:, :128], class_ref[:, 128:])
    for k in range(class_ref.shape[0]):
        chunk_ref[k, CLASS_ROW : CLASS_ROW + 1, :] = sums[k : k + 1]


def read_chunks(core_ref, own_ref, other_ref, conv_ref, class_ref, *, scale):
    _, channels, hidden = conv_ref.shape
    width = 3 * hidden
    chips = own_ref.shape[0]
    for half in range(2):
        mine = core_ref[0] == half
        for tile, skip, count, chip, row in tile_places(3 * channels * width // 2048, chips):
            block, lane = tile // (width // 128), tile % (width // 128)
            top = half * 3 * channels // 2 + 8 * block
            a, b = top // channels, 128 * lane // hidden
            value = jnp.where(mine, own_ref[chip, row : row + count, :], other_ref[chip, row : row + count, :])
            conv_ref[
                3 * a + b, top % channels + skip : top % channels + skip + count,
                128 * lane % hidden : 128 * lane % hidden + 128,
            ] = value * scale
        for k in range(class_ref.shape[0]):
            value = jnp.where(
                mine, own_ref[k, CLASS_ROW : CLASS_ROW + 1, :], other_ref[k, CLASS_ROW : CLASS_ROW + 1, :]
            )
            class_ref[k : k + 1, 128 * half : 128 * (half + 1)] = value * scale


def pack_half(values):
    marks = lax.broadcasted_iota(jnp.int32, values.shape, values.ndim - 2) == MARK_ROW
    largest = jnp.max(jnp.where(marks, 0.0, jnp.abs(values)))
    exponent = jnp.clip(jnp.ceil(jnp.log2(jnp.maximum(largest, 1e-30))), -100.0, 120.0)
    return jnp.where(marks, exponent, values * jnp.exp2(14.0 - exponent)).astype(jnp.float16)


def unpack_half(packed):
    exponent = packed[..., MARK_ROW : MARK_ROW + 1, :].astype(jnp.float32)
    return packed.astype(jnp.float32) * jnp.exp2(exponent - 14.0)


def gather_all(total, core, conv_shape, class_shape, scale):
    mine = pack_half(total)
    spread = jnp.broadcast_to(mine[None], (size_of(CHIPS),) + mine.shape)
    own = lax.all_to_all(spread, CHIPS, split_axis=0, concat_axis=0, tiled=True)
    other = lax.ppermute(own, "core", PARTNER)
    vmem = pl.BlockSpec(memory_space=pltpu.VMEM)
    conv, small = pl.pallas_call(
        functools.partial(read_chunks, scale=scale),
        out_shape=(
            jax.ShapeDtypeStruct(conv_shape, jnp.float32),
            jax.ShapeDtypeStruct(class_shape[::-1], jnp.float32),
        ),
        in_specs=[pl.BlockSpec(memory_space=pltpu.SMEM), vmem, vmem],
        out_specs=(vmem, vmem),
        name="place",
        compiler_params=vmem_of(12),
        cost_estimate=cost_of(2),
    )(core, unpack_half(own), unpack_half(other))
    return conv, small.T


def unit_edges_kernel(up_ref, mid_ref, down_ref, left_ref, right_ref):
    rows, channels, cols = mid_ref.shape
    lanes = lane_of((channels, 128))
    left = jnp.zeros((channels, 128), jnp.float32)
    right = jnp.zeros((channels, 128), jnp.float32)
    for i in range(rows + 2):
        source = up_ref.at[0] if i == 0 else down_ref.at[0] if i == rows + 1 else mid_ref.at[i - 1]
        first = source[:, :128].astype(jnp.float32)
        last = source[:, cols - 128 :].astype(jnp.float32)
        left = jnp.where(lanes == i, pltpu.roll(first, i, 1), left)
        right = jnp.where(lanes == i, pltpu.roll(last, i + 1, 1), right)
    left_ref[...] = left.astype(left_ref.dtype)
    right_ref[...] = right.astype(right_ref.dtype)


def side_sums(side_ref, weights):
    side = side_ref[...].astype(jnp.float32)
    moved = [pltpu.roll(side, (128 - a) % 128, 1).astype(jnp.bfloat16) for a in range(3)]
    return jnp.dot(weights, jnp.concatenate(moved, axis=0), preferred_element_type=jnp.float32)


def conv_start(
    up_ref, mid_ref, down_ref, left_ref, right_ref, taps_ref, padded, left_sum, right_sum, weights_ref, forward
):
    rows, channels, _ = mid_ref.shape
    out = weights_ref.shape[0] // 3

    @pl.when(pl.program_id(0) == 0)
    def _():
        for b in range(3):
            for a in range(3):
                tap = taps_ref[3 * a + b].T if forward else taps_ref[3 * (2 - a) + (2 - b)]
                weights_ref[out * b : out * (b + 1), channels * a : channels * (a + 1)] = tap
        padded[0] = up_ref[0]
        padded[pl.ds(1, rows)] = mid_ref[...]
        padded[rows + 1] = down_ref[0]
        left_sum[...] = side_sums(left_ref, weights_ref[:out])
        right_sum[...] = side_sums(right_ref, weights_ref[2 * out :])


def conv_row(row, weights_ref, padded, left_sum, right_sum):
    out = weights_ref.shape[0] // 3
    cols = padded.shape[2]
    stack = jnp.concatenate([padded[row], padded[row + 1], padded[row + 2]], axis=0)
    parts = jnp.dot(weights_ref[...], stack, preferred_element_type=jnp.float32)
    lanes = lane_of((out, 128))
    before = pltpu.roll(parts[:out], 1, 1)
    after = pltpu.roll(parts[2 * out :], cols - 1, 1)
    left = pltpu.roll(left_sum[...], (128 - row) % 128, 1)
    right = pltpu.roll(right_sum[...], 127 - row, 1)
    before = jnp.concatenate([jnp.where(lanes == 0, left, before[:, :128]), before[:, 128:]], axis=1)
    after = jnp.concatenate([after[:, :-128], jnp.where(lanes == 127, right, after[:, -128:])], axis=1)
    return parts[out : 2 * out] + (before + after)


STEP_ROWS = 2


def forward_kernel(
    up_ref, mid_ref, down_ref, left_ref, right_ref, taps_ref, class_ref,
    slope_ref, hidden_ref, guess_ref, padded, left_sum, right_sum, weights_ref,
):
    conv_start(
        up_ref, mid_ref, down_ref, left_ref, right_ref, taps_ref, padded, left_sum, right_sum, weights_ref, True
    )
    for k in range(STEP_ROWS):
        pre_act = conv_row(pl.program_id(0) * STEP_ROWS + k, weights_ref, padded, left_sum, right_sum)
        logistic = 0.5 * jnp.tanh(0.5 * pre_act) + 0.5
        silu = pre_act * logistic
        slope_ref[k] = logistic + silu * (1.0 - logistic)
        hidden = silu.astype(jnp.bfloat16)
        hidden_ref[k] = hidden
        logit = jnp.dot(class_ref[...], hidden, preferred_element_type=jnp.float32)
        guess_ref[k] = jax.nn.sigmoid(logit)


def back_kernel(guess_ref, refined_ref, slope_ref, class_ref, back_ref, error_ref):
    for k in range(STEP_ROWS):
        error = (guess_ref[k] - refined_ref[k]).astype(jnp.bfloat16)
        error_ref[k] = error
        summed = jnp.dot(class_ref[...], error, preferred_element_type=jnp.float32)
        back_ref[k] = (summed * slope_ref[k]).astype(jnp.bfloat16)


CONTRACT_LAST = (((1,), (1,)), ((), ()))


def grads_kernel(
    core_ref, up_ref, mid_ref, down_ref, left_ref, right_ref, back_ref, hidden_ref, error_ref,
    keep_ref, send_ref, padded, first_cols, last_cols, conv_ref, class_ref,
):
    rows, _, cols = mid_ref.shape
    step = pl.program_id(0)

    @pl.when(step == 0)
    def _():
        padded[0] = up_ref[0]
        padded[pl.ds(1, rows)] = mid_ref[...]
        padded[rows + 1] = down_ref[0]
        conv_ref[...] = jnp.zeros(conv_ref.shape, jnp.float32)
        class_ref[...] = jnp.zeros(class_ref.shape, jnp.float32)
        first_cols[...] = jnp.zeros(first_cols.shape, jnp.float32)
        last_cols[...] = jnp.zeros(last_cols.shape, jnp.float32)

    lanes = lane_of((back_ref.shape[1], cols))
    narrow = lane_of((back_ref.shape[1], 128))
    images, backs = [], []
    for k in range(STEP_ROWS):
        row = step * STEP_ROWS + k
        images.append(jnp.concatenate([padded[row], padded[row + 1], padded[row + 2]], axis=0))
        back = back_ref[k].astype(jnp.float32)
        first_cols[...] = jnp.where(narrow == row + 1, pltpu.roll(back[:, :128], row + 1, 1), first_cols[...])
        last_cols[...] = jnp.where(narrow == row + 1, pltpu.roll(back[:, cols - 128 :], row + 2, 1), last_cols[...])
        below = jnp.where(lanes == cols - 1, 0.0, pltpu.roll(back, cols - 1, 1))
        above = jnp.where(lanes == 0, 0.0, pltpu.roll(back, 1, 1))
        backs.append(
            jnp.concatenate([below.astype(jnp.bfloat16), back_ref[k], above.astype(jnp.bfloat16)], axis=0)
        )
        class_ref[...] += lax.dot_general(
            error_ref[k], hidden_ref[k], CONTRACT_LAST, preferred_element_type=jnp.float32
        )
    conv_ref[...] += lax.dot_general(
        jnp.concatenate(images, axis=1), jnp.concatenate(backs, axis=1), CONTRACT_LAST,
        preferred_element_type=jnp.float32,
    )

    @pl.when(step == pl.num_programs(0) - 1)
    def _():
        hidden = back_ref.shape[1]
        for side_ref, cells, place in ((left_ref, first_cols, 0), (right_ref, last_cols, 2 * hidden)):
            side = side_ref[...].astype(jnp.float32)
            moved = [pltpu.roll(side, (1 - a) % 128, 1).astype(jnp.bfloat16) for a in range(3)]
            conv_ref[:, pl.ds(place, hidden)] += lax.dot_general(
                jnp.concatenate(moved, axis=0), cells[...].astype(jnp.bfloat16), CONTRACT_LAST,
                preferred_element_type=jnp.float32,
            )
        write_chunks(keep_ref, conv_ref, class_ref, core_ref[0])
        write_chunks(send_ref, conv_ref, class_ref, 1 - core_ref[0])


def feature_kernel(
    up_ref, mid_ref, down_ref, left_ref, right_ref, taps_ref, out_ref, padded, left_sum, right_sum, weights_ref
):
    conv_start(
        up_ref, mid_ref, down_ref, left_ref, right_ref, taps_ref, padded, left_sum, right_sum, weights_ref, False
    )
    for k in range(STEP_ROWS):
        row = pl.program_id(0) * STEP_ROWS + k
        out_ref[k] = conv_row(row, weights_ref, padded, left_sum, right_sum).astype(out_ref.dtype)


def whole(array):
    return pl.BlockSpec(array.shape, lambda i: (0,) * array.ndim, pipeline_mode=pl.Buffered(1))


def by_rows(shape):
    return pl.BlockSpec((STEP_ROWS,) + shape[1:], lambda i: (i, 0, 0))


def unit_rows(cells):
    return pass_on(cells[-1:], "row", 1), pass_on(cells[:1], "row", -1)


def unit_cols(cells, up, down):
    edge = jax.ShapeDtypeStruct((cells.shape[1], 128), cells.dtype)
    to_left, to_right = pl.pallas_call(
        unit_edges_kernel, out_shape=(edge, edge), name="unit_edges",
        compiler_params=vmem_of(16),
        cost_estimate=cost_of(1),
    )(up, cells, down)
    return pass_on(to_right, COL, 1), pass_on(to_left, COL, -1)


def conv_scratch(rows, channels, cols, out):
    return [
        pltpu.VMEM((rows + 2, channels, cols), jnp.bfloat16),
        pltpu.VMEM((out, 128), jnp.float32),
        pltpu.VMEM((out, 128), jnp.float32),
        pltpu.VMEM((3 * out, 3 * channels), jnp.bfloat16),
    ]


def row_call(kernel, rows, args, arg_rows, outs, out_rows, scratch, vmem, micros):
    return pl.pallas_call(
        kernel,
        grid=(rows // STEP_ROWS,),
        in_specs=[
            pl.BlockSpec(memory_space=pltpu.SMEM) if a.ndim == 1 else by_rows(a.shape) if split else whole(a)
            for a, split in zip(args, arg_rows)
        ],
        out_specs=tuple(by_rows(o.shape) if split else whole(o) for o, split in zip(outs, out_rows)),
        out_shape=tuple(outs),
        scratch_shapes=scratch,
        compiler_params=vmem_of(vmem),
        cost_estimate=cost_of(micros),
    )(*args)


def local_step(teacher_feats, teacher_probs, student_feats, conv_weight, class_weight):
    channels, rows, cols = student_feats.shape
    hidden_size, classes = class_weight.shape
    pixel_count = float(rows * cols)
    student = student_feats.transpose(1, 0, 2)
    student_up, student_down = unit_rows(student)
    mid, up, down = teacher_rows(teacher_feats, teacher_probs)
    halo = (student_up, student, student_down) + unit_cols(student, student_up, student_down)
    f32, bf16 = jnp.float32, jnp.bfloat16
    slope, hidden, guess = row_call(
        forward_kernel, rows,
        halo + (conv_weight, class_weight.T), [False] * 7,
        [
            jax.ShapeDtypeStruct((rows, hidden_size, cols), f32),
            jax.ShapeDtypeStruct((rows, hidden_size, cols), bf16),
            jax.ShapeDtypeStruct((rows, classes, cols), f32),
        ],
        [True] * 3, conv_scratch(rows, channels, cols, hidden_size), 16, 12,
    )
    up, down, guess = lax.optimization_barrier((up, down, guess))
    current, weights = refine(mid, up, down, teacher_feats.shape[0], classes)
    refined = finish(current, weights, cols)
    back, error = row_call(
        back_kernel, rows, (guess, refined, slope, class_weight), [True, True, True, False],
        [
            jax.ShapeDtypeStruct((rows, hidden_size, cols), bf16),
            jax.ShapeDtypeStruct((rows, classes, cols), bf16),
        ],
        [True] * 2, [], 16, 2,
    )
    back_up, back_down = unit_rows(back)
    core = lax.axis_index("core").astype(jnp.int32).reshape(1)
    chunks = jax.ShapeDtypeStruct((size_of(CHIPS), CHUNK_ROWS, 128), f32)
    keep, sent = row_call(
        grads_kernel, rows, (core,) + halo + (back, hidden, error), [False] * 6 + [True] * 3,
        [chunks, chunks], [False] * 2,
        [pltpu.VMEM((rows + 2, channels, cols), bf16)]
        + [pltpu.VMEM((hidden_size, 128), f32)] * 2
        + [pltpu.VMEM((3 * channels, 3 * hidden_size), f32), pltpu.VMEM((classes, hidden_size), f32)], 28, 9,
    )
    back_up, back_down, sent = lax.optimization_barrier((back_up, back_down, sent))
    other = lax.ppermute(sent, "core", PARTNER)
    back_cols = unit_cols(back, back_up, back_down)
    packed = pack_half(keep + other)
    back_left, back_right, packed = lax.optimization_barrier(back_cols + (packed,))
    (feature_grad,) = row_call(
        feature_kernel, rows,
        (back_up, back, back_down, back_left, back_right, conv_weight), [False] * 6,
        [jax.ShapeDtypeStruct((rows, channels, cols), bf16)],
        [True], conv_scratch(rows, hidden_size, cols, channels), 16, 8,
    )
    received = lax.all_to_all(packed, CHIPS, split_axis=0, concat_axis=0, tiled=True)
    total = jnp.sum(unpack_half(received), axis=0)
    total, feature_grad = lax.optimization_barrier((total, feature_grad))
    grad_conv, grad_class = gather_all(total, core, conv_weight.shape, class_weight.shape, 1.0 / pixel_count)
    return (refined.transpose(1, 0, 2), feature_grad.transpose(1, 0, 2), grad_conv, grad_class)


def solution(mesh):
    devices = mesh.devices
    mesh = Mesh(devices.reshape(devices.shape[0], -1, 2), ("row",) + COL)
    split = P(None, "row", COL)
    in_specs = (split, split, split, P(), P())
    out_specs = (split, split, P(), P())
    return jax.shard_map(local_step, mesh=mesh, in_specs=in_specs, out_specs=out_specs, check_vma=False)
```

```python
import functools
import math

import jax
import jax.numpy as jnp
from jax import lax
from jax.experimental import pallas as pl
from jax.experimental.pallas import tpu as pltpu
from jax.sharding import Mesh
from jax.sharding import PartitionSpec as P


EDGE_ROWS = 8
EDGE_COLS = 16
SPAN = 384
PAIR_TAPS = [tap for s in (1, 2, 4) for tap in ((0, s), (s, -s), (s, 0), (s, s))]


def shifted_by(cells, off_x):
    return cells if off_x == 0 else pltpu.roll(cells, (-off_x) % cells.shape[-1], cells.ndim - 1)


def vmem_of(mib):
    return pltpu.CompilerParams(vmem_limit_bytes=mib * 2**20)


def cost_of(micros):
    return pl.CostEstimate(flops=int(micros * 1e9), transcendentals=0, bytes_accessed=int(micros * 3e6))


def lane_of(shape):
    return lax.broadcasted_iota(jnp.int32, shape, len(shape) - 1)


def packed_row(ref, skip):
    return jnp.concatenate([ref[i, skip:, :] for i in range(EDGE_ROWS)], axis=0)


def edges_kernel(up_ref, mid_ref, down_ref, student_ref, left_ref, right_ref):
    rows, channels, _ = mid_ref.shape
    group = lane_of((channels, 128)) // EDGE_COLS
    groups = rows // 8 + 2
    for g in range(groups):
        source = up_ref if g == 0 else down_ref if g == groups - 1 else mid_ref.at[pl.ds(8 * (g - 1), 8)]
        left = jnp.zeros((channels, 128), jnp.float32)
        right = jnp.zeros((channels, 128), jnp.float32)
        for i in range(8):
            first = source[i, :channels, :128].astype(jnp.float32)
            last = source[i, :channels, -128:].astype(jnp.float32)
            left = jnp.where(group == i, pltpu.roll(first, EDGE_COLS * i, 1), left)
            right = jnp.where(group == i, pltpu.roll(last, (EDGE_COLS * (i + 1)) % 128, 1), right)
        left_ref[channels * g : channels * (g + 1)] = left.astype(left_ref.dtype)
        right_ref[channels * g : channels * (g + 1)] = right.astype(right_ref.dtype)
    up, down = packed_row(up_ref, channels), packed_row(down_ref, channels)
    left, right = border_cells([up] + [student_ref.at[i] for i in range(rows)] + [down], student_ref.shape[1:])
    left_ref[channels * groups :] = left.astype(left_ref.dtype)
    right_ref[channels * groups :] = right.astype(right_ref.dtype)


def border_cells(sources, shape):
    channels, cols = shape
    lanes = lane_of((channels, 128))
    left = jnp.zeros((channels, 128), jnp.float32)
    right = jnp.zeros((channels, 128), jnp.float32)
    for i, source in enumerate(sources):
        first = source[:, :128].astype(jnp.float32)
        last = source[:, cols - 128 :].astype(jnp.float32)
        left = jnp.where(lanes == i, pltpu.roll(first, i, 1), left)
        right = jnp.where(lanes == i, pltpu.roll(last, i + 1, 1), right)
    return left, right


def sweep_row(weights, center_row, read_row):
    total = weights(0) * read_row(center_row)
    for index, (off_y, off_x) in enumerate(PAIR_TAPS):
        total += weights(1 + index) * shifted_by(read_row(center_row + off_y), off_x)
        total += weights(13 + index) * shifted_by(read_row(center_row - off_y), -off_x)
    return total


def affinity_kernel(
    place_ref, up_ref, mid_ref, down_ref, left_ref, right_ref, current_ref, weights_ref,
    feats, probs, next_probs, pairs, squares, *, full_rows, full_cols, feat_channels, classes,
):
    rows = mid_ref.shape[0]
    cols = mid_ref.shape[2]
    tall = rows + 2 * EDGE_ROWS
    channels = mid_ref.shape[1]
    lanes = lane_of((channels, 128))

    def gather(i, carry):
        for g in range(tall // 8):
            if g == 0:
                body = up_ref[i, :channels]
            elif g == tall // 8 - 1:
                body = down_ref[i, :channels]
            else:
                body = mid_ref[8 * (g - 1) + i]
            from_right = pltpu.roll(right_ref[channels * g : channels * (g + 1)].astype(jnp.float32), (128 - EDGE_COLS * i) % 128, 1)
            from_left = pltpu.roll(left_ref[channels * g : channels * (g + 1)].astype(jnp.float32), (240 - EDGE_COLS * i) % 128, 1)
            side = jnp.where(lanes < EDGE_COLS, from_right, jnp.where(lanes >= 128 - EDGE_COLS, from_left, 0.0))
            body = body.astype(jnp.float32)
            row = 8 * g + i
            high, low = feat_channels, feat_channels + classes
            feats[row, :, :cols] = body[:high]
            feats[row, :, cols:] = side[:high]
            probs[row, :, :cols] = body[high:low] + body[low:]
            probs[row, :, cols:] = side[high:low] + side[low:]
        return carry

    lax.fori_loop(0, 8, gather, 0)
    pairs[:, tall - 8 :, :] = jnp.zeros((len(PAIR_TAPS), 8, SPAN), jnp.float32)

    def distances(row, carry):
        sums = [None for _ in PAIR_TAPS]
        for c in range(feat_channels // 8):
            here = feats[row, 8 * c : 8 * c + 8, :]
            there = {0: here}
            for index, (off_y, off_x) in enumerate(PAIR_TAPS):
                if off_y not in there:
                    there[off_y] = feats[row + off_y, 8 * c : 8 * c + 8, :]
                product = here * shifted_by(there[off_y], off_x)
                sums[index] = product if c == 0 else sums[index] + product
        for index in range(len(PAIR_TAPS)):
            pairs[index, pl.ds(row, 1), :] = jnp.sum(sums[index], axis=0, keepdims=True)
        return carry

    lax.fori_loop(0, tall - 4, distances, 0)

    def sizes(row, carry):
        cells = feats[row]
        squares[pl.ds(row, 1), :] = jnp.sum(cells * cells, axis=0, keepdims=True)
        return carry

    lax.fori_loop(0, tall, sizes, 0, unroll=4)
    squares[tall:, :] = jnp.zeros((8, SPAN), jnp.float32)

    shape = (tall, SPAN)
    lane = lane_of(shape)
    row_at = place_ref[0] - EDGE_ROWS + lax.broadcasted_iota(jnp.int32, shape, 0)
    col_at = place_ref[1] + jnp.where(lane < cols + EDGE_COLS, lane, lane - SPAN)

    def inside(off_y, off_x):
        y, x = row_at + off_y, col_at + off_x
        return (y >= 0) & (y < full_rows) & (x >= 0) & (x < full_cols)

    here_inside = inside(0, 0)
    for index, (off_y, off_x) in enumerate(PAIR_TAPS):
        present = here_inside & inside(off_y, off_x)
        both = squares[:tall, :] + shifted_by(squares[off_y : off_y + tall, :], off_x)
        distance = jnp.maximum(both - 2.0 * pairs[index], 0.0)
        pairs[index] = jnp.where(present, jnp.exp(distance * (-1.0 / feat_channels)), 0.0)
    wide = rows + EDGE_ROWS
    total = jnp.ones((wide, SPAN), jnp.float32)
    for index, (off_y, off_x) in enumerate(PAIR_TAPS):
        ahead = pairs[index, 4 : 4 + wide, :]
        behind = shifted_by(pairs[index, 4 - off_y : 4 - off_y + wide, :], -off_x)
        weights_ref[1 + index] = ahead
        weights_ref[13 + index] = behind
        total = total + (ahead + behind)
    scale = 1.0 / total
    weights_ref[0] = scale
    for index in range(1, 25):
        weights_ref[index] = weights_ref[index] * scale
    two_sweeps(weights_ref, lambda row: probs[row], next_probs, current_ref, rows)


def two_sweeps(weights_ref, read_row, middle, out_ref, rows):
    def first(row, carry):
        middle[row] = sweep_row(lambda o: weights_ref[o, pl.ds(row, 1), :], row + 4, read_row)
        return carry

    lax.fori_loop(0, rows + 8, first, 0, unroll=4)

    def second(row, carry):
        value = sweep_row(lambda o: weights_ref[o, pl.ds(row + 4, 1), :], row + 4, lambda r: middle[r])
        out_ref[row] = value[:, : out_ref.shape[2]]
        return carry

    lax.fori_loop(0, rows, second, 0, unroll=4)


def finish_kernel(weights_ref, up_ref, mid_ref, down_ref, out_ref, probs, next_probs):
    rows = mid_ref.shape[0]
    probs[:EDGE_ROWS] = up_ref[...]
    probs[EDGE_ROWS : EDGE_ROWS + rows] = mid_ref[...]
    probs[EDGE_ROWS + rows :] = down_ref[...]
    two_sweeps(weights_ref, lambda row: probs[row], next_probs, out_ref, rows)


COL = ("pair", "core")


def size_of(axes):
    return math.prod(lax.axis_size(a) for a in axes) if isinstance(axes, tuple) else lax.axis_size(axes)


def pass_on(cells, axis, step):
    ends = size_of(axis) - 1
    if step > 0:
        return lax.ppermute(cells, axis, [(i, i + 1) for i in range(ends)])
    return lax.ppermute(cells, axis, [(i + 1, i) for i in range(ends)])


def share_rows(teacher_feats, teacher_probs, student):
    rows = teacher_feats.shape[1]
    high = lax.reduce_precision(teacher_probs, 8, 7)
    low = teacher_probs - high
    mid = jnp.concatenate(
        [teacher_feats, high.astype(jnp.bfloat16), low.astype(jnp.bfloat16)], axis=0
    ).transpose(1, 0, 2)

    def message(first, row):
        return jnp.concatenate(
            [mid[first : first + EDGE_ROWS], student[row].reshape(EDGE_ROWS, -1, student.shape[2])], axis=1
        )

    up = pass_on(message(rows - EDGE_ROWS, rows - 1), "row", 1)
    down = pass_on(message(0, 0), "row", -1)
    return mid, up, down


def share_cols(mid, up, down, student):
    rows, channels, _ = mid.shape
    groups = rows // 8 + 2
    edge = jax.ShapeDtypeStruct((groups * channels + student.shape[1], 128), jnp.bfloat16)
    to_left, to_right = pl.pallas_call(
        edges_kernel, out_shape=(edge, edge), name="edges", compiler_params=vmem_of(16), cost_estimate=cost_of(2)
    )(up, mid, down, student)
    return pass_on(to_right, COL, 1), pass_on(to_left, COL, -1)


def refine(mid, up, down, left, right, feat_channels, classes):
    rows, _, cols = mid.shape
    place = jnp.stack([lax.axis_index("row") * rows, lax.axis_index(COL) * cols]).astype(jnp.int32)
    tall = rows + 2 * EDGE_ROWS
    vmem = pl.BlockSpec(memory_space=pltpu.VMEM)
    current, weights = pl.pallas_call(
        functools.partial(
            affinity_kernel,
            full_rows=rows * lax.axis_size("row"),
            full_cols=cols * size_of(COL),
            feat_channels=feat_channels,
            classes=classes,
        ),
        out_shape=(
            jax.ShapeDtypeStruct((rows, classes, SPAN), jnp.float32),
            jax.ShapeDtypeStruct((25, rows + EDGE_ROWS, SPAN), jnp.float32),
        ),
        in_specs=[pl.BlockSpec(memory_space=pltpu.SMEM)] + [vmem] * 5,
        out_specs=(vmem, vmem),
        scratch_shapes=[
            pltpu.VMEM((tall, feat_channels, SPAN), jnp.float32),
            pltpu.VMEM((tall, classes, SPAN), jnp.float32),
            pltpu.VMEM((rows + 8, classes, SPAN), jnp.float32),
            pltpu.VMEM((len(PAIR_TAPS), tall, SPAN), jnp.float32),
            pltpu.VMEM((tall + 8, SPAN), jnp.float32),
        ],
        name="affinity",
        compiler_params=vmem_of(20),
        cost_estimate=cost_of(12),
    )(place, up, mid, down, left, right)
    return current, weights


def finish(current, weights, cols, up, down):
    rows, classes, _ = current.shape
    tall = rows + 2 * EDGE_ROWS
    refined = pl.pallas_call(
        finish_kernel,
        out_shape=jax.ShapeDtypeStruct((rows, classes, cols), jnp.float32),
        scratch_shapes=[
            pltpu.VMEM((tall, classes, SPAN), jnp.float32),
            pltpu.VMEM((rows + 8, classes, SPAN), jnp.float32),
        ],
        name="finish",
        compiler_params=vmem_of(12),
        cost_estimate=cost_of(4),
    )(weights, up, current, down)
    return refined


CHIPS = ("row", "pair")
PARTNER = [(0, 1), (1, 0)]
CLASS_ROW = 36
MARK_ROW = 37
CHUNK_ROWS = 40


def tile_places(n_tiles, chips):
    full = n_tiles // chips
    for tile in range(n_tiles):
        if tile < full * chips:
            yield tile, 0, 8, tile // full, 8 * (tile % full)
        else:
            share = 8 * (n_tiles - full * chips) // chips
            for part in range(8 // share):
                chip = (tile - full * chips) * (8 // share) + part
                yield tile, part * share, share, chip, 8 * full


def write_chunks(chunk_ref, conv_ref, class_ref, half):
    height, width = conv_ref.shape[0] // 2, conv_ref.shape[1]
    chips = chunk_ref.shape[0]
    first = pl.multiple_of(half * height, height)
    chunk_ref[:, CLASS_ROW:, :] = jnp.zeros((chips, CHUNK_ROWS - CLASS_ROW, 128), jnp.float32)
    for tile, skip, count, chip, row in tile_places(height * width // 1024, chips):
        block, lane = tile // (width // 128), tile % (width // 128)
        rows = conv_ref[pl.ds(pl.multiple_of(first + 8 * block, 8), 8), 128 * lane : 128 * (lane + 1)]
        chunk_ref[chip, row : row + count, :] = rows[skip : skip + count]
    sums = jnp.where(half == 0, class_ref[:, :128], class_ref[:, 128:])
    for k in range(class_ref.shape[0]):
        chunk_ref[k, CLASS_ROW : CLASS_ROW + 1, :] = sums[k : k + 1]


def read_chunks(core_ref, own_ref, other_ref, conv_ref, class_ref, *, scale):
    _, channels, hidden = conv_ref.shape
    width = 3 * hidden
    chips = own_ref.shape[0]
    for half in range(2):
        mine = core_ref[0] == half
        for tile, skip, count, chip, row in tile_places(3 * channels * width // 2048, chips):
            block, lane = tile // (width // 128), tile % (width // 128)
            top = half * 3 * channels // 2 + 8 * block
            a, b = top // channels, 128 * lane // hidden
            value = jnp.where(mine, own_ref[chip, row : row + count, :], other_ref[chip, row : row + count, :])
            conv_ref[
                3 * a + b, top % channels + skip : top % channels + skip + count,
                128 * lane % hidden : 128 * lane % hidden + 128,
            ] = value * scale
        for k in range(class_ref.shape[0]):
            value = jnp.where(
                mine, own_ref[k, CLASS_ROW : CLASS_ROW + 1, :], other_ref[k, CLASS_ROW : CLASS_ROW + 1, :]
            )
            class_ref[k : k + 1, 128 * half : 128 * (half + 1)] = value * scale


def pack_half(values):
    marks = lax.broadcasted_iota(jnp.int32, values.shape, values.ndim - 2) == MARK_ROW
    largest = jnp.max(jnp.where(marks, 0.0, jnp.abs(values)))
    exponent = jnp.clip(jnp.ceil(jnp.log2(jnp.maximum(largest, 1e-30))), -100.0, 120.0)
    return jnp.where(marks, exponent, values * jnp.exp2(14.0 - exponent)).astype(jnp.float16)


def unpack_half(packed):
    exponent = packed[..., MARK_ROW : MARK_ROW + 1, :].astype(jnp.float32)
    return packed.astype(jnp.float32) * jnp.exp2(exponent - 14.0)


def gather_all(total, core, conv_shape, class_shape, scale):
    mine = pack_half(total)
    spread = jnp.broadcast_to(mine[None], (size_of(CHIPS),) + mine.shape)
    own = lax.all_to_all(spread, CHIPS, split_axis=0, concat_axis=0, tiled=True)
    other = lax.ppermute(own, "core", PARTNER)
    vmem = pl.BlockSpec(memory_space=pltpu.VMEM)
    conv, small = pl.pallas_call(
        functools.partial(read_chunks, scale=scale),
        out_shape=(
            jax.ShapeDtypeStruct(conv_shape, jnp.float32),
            jax.ShapeDtypeStruct(class_shape[::-1], jnp.float32),
        ),
        in_specs=[pl.BlockSpec(memory_space=pltpu.SMEM), vmem, vmem],
        out_specs=(vmem, vmem),
        name="place",
        compiler_params=vmem_of(12),
        cost_estimate=cost_of(2),
    )(core, unpack_half(own), unpack_half(other))
    return conv, small.T


def unit_edges_kernel(up_ref, mid_ref, down_ref, left_ref, right_ref):
    sources = [up_ref.at[0]] + [mid_ref.at[i] for i in range(mid_ref.shape[0])] + [down_ref.at[0]]
    left, right = border_cells(sources, mid_ref.shape[1:])
    left_ref[...] = left.astype(left_ref.dtype)
    right_ref[...] = right.astype(right_ref.dtype)


def side_sums(side, weights):
    side = side.astype(jnp.float32)
    moved = [pltpu.roll(side, (128 - a) % 128, 1).astype(jnp.bfloat16) for a in range(3)]
    return jnp.dot(weights, jnp.concatenate(moved, axis=0), preferred_element_type=jnp.float32)


def conv_start(
    up_ref, mid_ref, down_ref, left_ref, right_ref, taps_ref, padded, left_sum, right_sum, weights_ref
):
    rows, channels, _ = mid_ref.shape
    out = weights_ref.shape[0] // 3

    @pl.when(pl.program_id(0) == 0)
    def _():
        for b in range(3):
            for a in range(3):
                tap = taps_ref[3 * (2 - a) + (2 - b)]
                weights_ref[out * b : out * (b + 1), channels * a : channels * (a + 1)] = tap
        padded[0] = up_ref[0]
        padded[pl.ds(1, rows)] = mid_ref[...]
        padded[rows + 1] = down_ref[0]
        left_sum[...] = side_sums(left_ref[...], weights_ref[:out])
        right_sum[...] = side_sums(right_ref[...], weights_ref[2 * out :])


def conv_row(row, weights_ref, padded, left_sum, right_sum):
    out = weights_ref.shape[0] // 3
    cols = padded.shape[2]
    stack = jnp.concatenate([padded[row], padded[row + 1], padded[row + 2]], axis=0)
    parts = jnp.dot(weights_ref[...], stack, preferred_element_type=jnp.float32)
    lanes = lane_of((out, 128))
    before = pltpu.roll(parts[:out], 1, 1)
    after = pltpu.roll(parts[2 * out :], cols - 1, 1)
    left = pltpu.roll(left_sum[...], (128 - row) % 128, 1)
    right = pltpu.roll(right_sum[...], 127 - row, 1)
    before = jnp.concatenate([jnp.where(lanes == 0, left, before[:, :128]), before[:, 128:]], axis=1)
    after = jnp.concatenate([after[:, :-128], jnp.where(lanes == 127, right, after[:, -128:])], axis=1)
    return parts[out : 2 * out] + (before + after)


STEP_ROWS = 2


def joined(parts, out):
    cols = parts.shape[1]
    lanes = lane_of((out, cols))
    before = jnp.where(lanes == 0, 0.0, pltpu.roll(parts[:out], 1, 1))
    after = jnp.where(lanes == cols - 1, 0.0, pltpu.roll(parts[2 * out :], cols - 1, 1))
    return parts[out : 2 * out] + (before + after)


def convolve_kernel(mid_ref, taps_ref, pre_ref, weights_ref, padded):
    rows, channels, cols = mid_ref.shape
    out = weights_ref.shape[0] // 3

    @pl.when(pl.program_id(0) == 0)
    def _():
        for b in range(3):
            for a in range(3):
                weights_ref[out * b : out * (b + 1), channels * a : channels * (a + 1)] = taps_ref[3 * a + b].T
        padded[0] = jnp.zeros((channels, cols), padded.dtype)
        padded[pl.ds(1, rows)] = mid_ref[...]
        padded[rows + 1] = jnp.zeros((channels, cols), padded.dtype)

    for k in range(STEP_ROWS):
        row = pl.program_id(0) * STEP_ROWS + k
        stack = jnp.concatenate([padded[row], padded[row + 1], padded[row + 2]], axis=0)
        pre_ref[k] = joined(jnp.dot(weights_ref[...], stack, preferred_element_type=jnp.float32), out)


def activate_kernel(
    up_ref, down_ref, left_ref, right_ref, weights_ref, class_ref, pre_ref,
    slope_ref, hidden_ref, guess_ref, left_sum, right_sum, borders, *, skip,
):
    out, channels = weights_ref.shape[0] // 3, weights_ref.shape[1] // 3
    step = pl.program_id(0)

    @pl.when(step == 0)
    def _():
        left_sum[...] = side_sums(left_ref[-channels:], weights_ref[:out])
        right_sum[...] = side_sums(right_ref[-channels:], weights_ref[2 * out :])
        for index, ref in enumerate((up_ref, down_ref)):
            taps = weights_ref[:, 2 * channels * index : 2 * channels * index + channels]
            parts = jnp.dot(taps, packed_row(ref, skip), preferred_element_type=jnp.float32)
            borders[index] = joined(parts, out)

    lanes = lane_of((out, 128))
    for k in range(STEP_ROWS):
        row = step * STEP_ROWS + k
        left = jnp.where(lanes == 0, pltpu.roll(left_sum[...], (128 - row) % 128, 1), 0.0)
        right = jnp.where(lanes == 127, pltpu.roll(right_sum[...], 127 - row, 1), 0.0)
        pre_act = pre_ref[k]
        pre_act = jnp.concatenate([pre_act[:, :128] + left, pre_act[:, 128:] + right], axis=1)
        if k == 0:
            pre_act = pre_act + jnp.where(step == 0, borders[0], 0.0)
        if k == STEP_ROWS - 1:
            pre_act = pre_act + jnp.where(step == pl.num_programs(0) - 1, borders[1], 0.0)
        logistic = 0.5 * jnp.tanh(0.5 * pre_act) + 0.5
        silu = pre_act * logistic
        slope_ref[k] = logistic + silu * (1.0 - logistic)
        hidden = silu.astype(jnp.bfloat16)
        hidden_ref[k] = hidden
        logit = jnp.dot(class_ref[...], hidden, preferred_element_type=jnp.float32)
        guess_ref[k] = 0.5 * jnp.tanh(0.5 * logit) + 0.5


def back_kernel(guess_ref, refined_ref, slope_ref, class_ref, back_ref, error_ref):
    for k in range(STEP_ROWS):
        error = (guess_ref[k] - refined_ref[k]).astype(jnp.bfloat16)
        error_ref[k] = error
        summed = jnp.dot(class_ref[...], error, preferred_element_type=jnp.float32)
        back_ref[k] = (summed * slope_ref[k]).astype(jnp.bfloat16)


CONTRACT_LAST = (((1,), (1,)), ((), ()))


def grads_kernel(
    core_ref, up_ref, mid_ref, down_ref, left_ref, right_ref, back_ref, hidden_ref, error_ref,
    keep_ref, send_ref, padded, first_cols, last_cols, conv_ref, class_ref,
):
    rows, channels, cols = mid_ref.shape
    step = pl.program_id(0)

    @pl.when(step == 0)
    def _():
        padded[0] = packed_row(up_ref, up_ref.shape[1] - channels // EDGE_ROWS)
        padded[pl.ds(1, rows)] = mid_ref[...]
        padded[rows + 1] = packed_row(down_ref, down_ref.shape[1] - channels // EDGE_ROWS)
        conv_ref[...] = jnp.zeros(conv_ref.shape, jnp.float32)
        class_ref[...] = jnp.zeros(class_ref.shape, jnp.float32)
        first_cols[...] = jnp.zeros(first_cols.shape, jnp.float32)
        last_cols[...] = jnp.zeros(last_cols.shape, jnp.float32)

    lanes = lane_of((back_ref.shape[1], cols))
    narrow = lane_of((back_ref.shape[1], 128))
    images, backs = [], []
    for k in range(STEP_ROWS):
        row = step * STEP_ROWS + k
        images.append(jnp.concatenate([padded[row], padded[row + 1], padded[row + 2]], axis=0))
        back = back_ref[k].astype(jnp.float32)
        first_cols[...] = jnp.where(narrow == row + 1, pltpu.roll(back[:, :128], row + 1, 1), first_cols[...])
        last_cols[...] = jnp.where(narrow == row + 1, pltpu.roll(back[:, cols - 128 :], row + 2, 1), last_cols[...])
        below = jnp.where(lanes == cols - 1, 0.0, pltpu.roll(back, cols - 1, 1))
        above = jnp.where(lanes == 0, 0.0, pltpu.roll(back, 1, 1))
        backs.append(
            jnp.concatenate([below.astype(jnp.bfloat16), back_ref[k], above.astype(jnp.bfloat16)], axis=0)
        )
        class_ref[...] += lax.dot_general(
            error_ref[k], hidden_ref[k], CONTRACT_LAST, preferred_element_type=jnp.float32
        )
    conv_ref[...] += lax.dot_general(
        jnp.concatenate(images, axis=1), jnp.concatenate(backs, axis=1), CONTRACT_LAST,
        preferred_element_type=jnp.float32,
    )

    @pl.when(step == pl.num_programs(0) - 1)
    def _():
        hidden = back_ref.shape[1]
        for side_ref, cells, place in ((left_ref, first_cols, 0), (right_ref, last_cols, 2 * hidden)):
            side = side_ref[-channels:].astype(jnp.float32)
            moved = [pltpu.roll(side, (1 - a) % 128, 1).astype(jnp.bfloat16) for a in range(3)]
            conv_ref[:, pl.ds(place, hidden)] += lax.dot_general(
                jnp.concatenate(moved, axis=0), cells[...].astype(jnp.bfloat16), CONTRACT_LAST,
                preferred_element_type=jnp.float32,
            )
        write_chunks(keep_ref, conv_ref, class_ref, core_ref[0])
        write_chunks(send_ref, conv_ref, class_ref, 1 - core_ref[0])


def feature_kernel(
    up_ref, mid_ref, down_ref, left_ref, right_ref, taps_ref, out_ref, padded, left_sum, right_sum, weights_ref
):
    conv_start(
        up_ref, mid_ref, down_ref, left_ref, right_ref, taps_ref, padded, left_sum, right_sum, weights_ref
    )
    for k in range(STEP_ROWS):
        row = pl.program_id(0) * STEP_ROWS + k
        out_ref[k] = conv_row(row, weights_ref, padded, left_sum, right_sum).astype(out_ref.dtype)


def in_hbm(*arrays):
    return tuple(pltpu.with_memory_space_constraint(a, pltpu.HBM) for a in arrays)


def whole(array):
    return pl.BlockSpec(array.shape, lambda i: (0,) * array.ndim, pipeline_mode=pl.Buffered(1))


def by_rows(shape):
    return pl.BlockSpec((STEP_ROWS,) + shape[1:], lambda i: (i, 0, 0))


def unit_rows(cells):
    return pass_on(cells[-1:], "row", 1), pass_on(cells[:1], "row", -1)


def unit_cols(cells, up, down):
    edge = jax.ShapeDtypeStruct((cells.shape[1], 128), cells.dtype)
    to_left, to_right = pl.pallas_call(
        unit_edges_kernel, out_shape=(edge, edge), name="unit_edges",
        compiler_params=vmem_of(16),
        cost_estimate=cost_of(1),
    )(up, cells, down)
    return pass_on(to_right, COL, 1), pass_on(to_left, COL, -1)


def conv_scratch(rows, channels, cols, out):
    return [
        pltpu.VMEM((rows + 2, channels, cols), jnp.bfloat16),
        pltpu.VMEM((out, 128), jnp.float32),
        pltpu.VMEM((out, 128), jnp.float32),
        pltpu.VMEM((3 * out, 3 * channels), jnp.bfloat16),
    ]


def row_call(kernel, rows, args, arg_rows, outs, out_rows, scratch, vmem, micros):
    return pl.pallas_call(
        kernel,
        grid=(rows // STEP_ROWS,),
        in_specs=[
            pl.BlockSpec(memory_space=pltpu.SMEM) if a.ndim == 1 else by_rows(a.shape) if split else whole(a)
            for a, split in zip(args, arg_rows)
        ],
        out_specs=tuple(by_rows(o.shape) if split else whole(o) for o, split in zip(outs, out_rows)),
        out_shape=tuple(outs),
        scratch_shapes=scratch,
        compiler_params=vmem_of(vmem),
        cost_estimate=cost_of(micros),
    )(*args)


def local_step(teacher_feats, teacher_probs, student_feats, conv_weight, class_weight):
    channels, rows, cols = student_feats.shape
    hidden_size, classes = class_weight.shape
    pixel_count = float(rows * cols)
    student = student_feats.transpose(1, 0, 2)
    f32, bf16 = jnp.float32, jnp.bfloat16
    mid, up, down = share_rows(teacher_feats, teacher_probs, student)
    pre_act, stacked = row_call(
        convolve_kernel, rows, (student, conv_weight), [False] * 2,
        [
            jax.ShapeDtypeStruct((rows, hidden_size, cols), f32),
            jax.ShapeDtypeStruct((3 * hidden_size, 3 * channels), bf16),
        ],
        [True, False], [pltpu.VMEM((rows + 2, channels, cols), bf16)], 16, 9,
    )
    left, right = share_cols(mid, up, down, student)
    halo = (up, student, down, left, right)
    current, weights = refine(mid, up, down, left, right, teacher_feats.shape[0], classes)
    current_rows = pass_on(current[rows - EDGE_ROWS :], "row", 1), pass_on(current[:EDGE_ROWS], "row", -1)
    slope, hidden, guess = row_call(
        functools.partial(activate_kernel, skip=mid.shape[1]), rows,
        (up, down, left, right, stacked, class_weight.T, pre_act), [False] * 6 + [True],
        [
            jax.ShapeDtypeStruct((rows, hidden_size, cols), f32),
            jax.ShapeDtypeStruct((rows, hidden_size, cols), bf16),
            jax.ShapeDtypeStruct((rows, classes, cols), f32),
        ],
        [True] * 3,
        [pltpu.VMEM((hidden_size, 128), f32)] * 2 + [pltpu.VMEM((2, hidden_size, cols), f32)], 16, 7,
    )
    refined = finish(current, weights, cols, *current_rows)
    back, error = row_call(
        back_kernel, rows, (guess, refined, slope, class_weight), [True, True, True, False],
        [
            jax.ShapeDtypeStruct((rows, hidden_size, cols), bf16),
            jax.ShapeDtypeStruct((rows, classes, cols), bf16),
        ],
        [True] * 2, [], 16, 2,
    )
    back_up, back_down = unit_rows(back)
    core = lax.axis_index("core").astype(jnp.int32).reshape(1)
    chunks = jax.ShapeDtypeStruct((size_of(CHIPS), CHUNK_ROWS, 128), f32)
    keep, sent = row_call(
        grads_kernel, rows, (core,) + halo + (back, hidden, error), [False] * 6 + [True] * 3,
        [chunks, chunks], [False] * 2,
        [pltpu.VMEM((rows + 2, channels, cols), bf16)]
        + [pltpu.VMEM((hidden_size, 128), f32)] * 2
        + [pltpu.VMEM((3 * channels, 3 * hidden_size), f32), pltpu.VMEM((classes, hidden_size), f32)], 28, 9,
    )
    back_up, back_down, sent = lax.optimization_barrier((back_up, back_down, sent))
    other = lax.ppermute(sent, "core", PARTNER)
    back_cols = unit_cols(back, back_up, back_down)
    packed = pack_half(keep + other)
    back_left, back_right, packed = lax.optimization_barrier(back_cols + (packed,))
    (feature_grad,) = row_call(
        feature_kernel, rows,
        in_hbm(back_up, back, back_down, back_left, back_right, conv_weight), [False] * 6,
        [jax.ShapeDtypeStruct((rows, channels, cols), bf16)],
        [True], conv_scratch(rows, hidden_size, cols, channels), 16, 8,
    )
    received = lax.all_to_all(packed, CHIPS, split_axis=0, concat_axis=0, tiled=True)
    total = jnp.sum(unpack_half(received), axis=0)
    total, feature_grad = lax.optimization_barrier((total, feature_grad))
    grad_conv, grad_class = gather_all(total, core, conv_weight.shape, class_weight.shape, 1.0 / pixel_count)
    return (refined.transpose(1, 0, 2), feature_grad.transpose(1, 0, 2), grad_conv, grad_class)


def solution(mesh):
    devices = mesh.devices
    mesh = Mesh(devices.reshape(devices.shape[0], -1, 2), ("row",) + COL)
    split = P(None, "row", COL)
    in_specs = (split, split, split, P(), P())
    out_specs = (split, split, P(), P())
    return jax.shard_map(local_step, mesh=mesh, in_specs=in_specs, out_specs=out_specs, check_vma=False)
```

```python
import functools
import math

import jax
import jax.numpy as jnp
from jax import lax
from jax.experimental import pallas as pl
from jax.experimental.pallas import tpu as pltpu
from jax.sharding import Mesh
from jax.sharding import PartitionSpec as P


EDGE_ROWS = 8
EDGE_COLS = 16
SPAN = 384
GROUP = 4
PAIR_TAPS = [tap for s in (1, 2, 4) for tap in ((0, s), (s, -s), (s, 0), (s, s))]


def shifted_by(cells, off_x):
    return cells if off_x == 0 else pltpu.roll(cells, (-off_x) % cells.shape[-1], cells.ndim - 1)


def vmem_of(mib):
    return pltpu.CompilerParams(vmem_limit_bytes=mib * 2**20)


def cost_of(micros):
    return pl.CostEstimate(flops=int(micros * 1e9), transcendentals=0, bytes_accessed=int(micros * 3e6))


def lane_of(shape):
    return lax.broadcasted_iota(jnp.int32, shape, len(shape) - 1)


def packed_row(ref, skip):
    return jnp.concatenate([ref[i, skip:, :] for i in range(EDGE_ROWS)], axis=0)


def edges_kernel(up_ref, mid_ref, down_ref, student_ref, left_ref, right_ref):
    rows, channels, _ = mid_ref.shape
    group = lane_of((channels, 128)) // EDGE_COLS
    groups = rows // 8 + 2
    for g in range(groups):
        source = up_ref if g == 0 else down_ref if g == groups - 1 else mid_ref.at[pl.ds(8 * (g - 1), 8)]
        left = jnp.zeros((channels, 128), jnp.float32)
        right = jnp.zeros((channels, 128), jnp.float32)
        for i in range(8):
            first = source[i, :channels, :128].astype(jnp.float32)
            last = source[i, :channels, -128:].astype(jnp.float32)
            left = jnp.where(group == i, pltpu.roll(first, EDGE_COLS * i, 1), left)
            right = jnp.where(group == i, pltpu.roll(last, (EDGE_COLS * (i + 1)) % 128, 1), right)
        left_ref[channels * g : channels * (g + 1)] = left.astype(left_ref.dtype)
        right_ref[channels * g : channels * (g + 1)] = right.astype(right_ref.dtype)
    up, down = packed_row(up_ref, channels), packed_row(down_ref, channels)
    left, right = border_cells([up] + [student_ref.at[i] for i in range(rows)] + [down], student_ref.shape[1:])
    left_ref[channels * groups :] = left.astype(left_ref.dtype)
    right_ref[channels * groups :] = right.astype(right_ref.dtype)


def border_cells(sources, shape):
    channels, cols = shape
    lanes = lane_of((channels, 128))
    left = jnp.zeros((channels, 128), jnp.float32)
    right = jnp.zeros((channels, 128), jnp.float32)
    for i, source in enumerate(sources):
        first = source[:, :128].astype(jnp.float32)
        last = source[:, cols - 128 :].astype(jnp.float32)
        left = jnp.where(lanes == i, pltpu.roll(first, i, 1), left)
        right = jnp.where(lanes == i, pltpu.roll(last, i + 1, 1), right)
    return left, right


def sweep_row(weights, center_row, read_row):
    total = weights(0) * read_row(center_row)
    for index, (off_y, off_x) in enumerate(PAIR_TAPS):
        total += weights(1 + index) * shifted_by(read_row(center_row + off_y), off_x)
        total += weights(13 + index) * shifted_by(read_row(center_row - off_y), -off_x)
    return total


def affinity_kernel(
    place_ref, up_ref, mid_ref, down_ref, left_ref, right_ref, current_ref, weights_ref,
    feats, probs, next_probs, pairs, squares, *, full_rows, full_cols, feat_channels, classes,
):
    rows = mid_ref.shape[0]
    cols = mid_ref.shape[2]
    tall = rows + 2 * EDGE_ROWS
    channels = mid_ref.shape[1]
    lanes = lane_of((channels, 128))

    def gather(i, carry):
        for g in range(tall // 8):
            if g == 0:
                body = up_ref[i, :channels]
            elif g == tall // 8 - 1:
                body = down_ref[i, :channels]
            else:
                body = mid_ref[8 * (g - 1) + i]
            from_right = pltpu.roll(right_ref[channels * g : channels * (g + 1)].astype(jnp.float32), (128 - EDGE_COLS * i) % 128, 1)
            from_left = pltpu.roll(left_ref[channels * g : channels * (g + 1)].astype(jnp.float32), (240 - EDGE_COLS * i) % 128, 1)
            side = jnp.where(lanes < EDGE_COLS, from_right, jnp.where(lanes >= 128 - EDGE_COLS, from_left, 0.0))
            body = body.astype(jnp.float32)
            row = 8 * g + i
            high, low = feat_channels, feat_channels + classes
            feats[row, :, :cols] = body[:high]
            feats[row, :, cols:] = side[:high]
            probs[row, :, :cols] = body[high:low] + body[low:]
            probs[row, :, cols:] = side[high:low] + side[low:]
        return carry

    lax.fori_loop(0, 8, gather, 0)
    pairs[:, tall - 8 :, :] = jnp.zeros((len(PAIR_TAPS), 8, SPAN), jnp.float32)

    for ring, radius in enumerate((1, 2, 4)):

        def products(step, carry, ring=ring, radius=radius):
            rows_at = [step * GROUP + g for g in range(GROUP)]
            sums = [[None] * 4 for _ in rows_at]
            for c in range(feat_channels // 8):
                for g, row in enumerate(rows_at):
                    here = feats[row, 8 * c : 8 * c + 8, :]
                    there = feats[row + radius, 8 * c : 8 * c + 8, :]
                    for k, (off_y, off_x) in enumerate(PAIR_TAPS[4 * ring : 4 * ring + 4]):
                        product = here * shifted_by(there if off_y else here, off_x)
                        sums[g][k] = product if c == 0 else sums[g][k] + product
            totals = [[jnp.sum(cells, axis=0, keepdims=True) for cells in row_sums] for row_sums in sums]
            for g, row in enumerate(rows_at):
                for k in range(4):
                    pairs[4 * ring + k, pl.ds(row, 1), :] = totals[g][k]
            return carry

        lax.fori_loop(0, (tall - 4) // GROUP, products, 0)

    def sizes(row, carry):
        cells = feats[row]
        squares[pl.ds(row, 1), :] = jnp.sum(cells * cells, axis=0, keepdims=True)
        return carry

    lax.fori_loop(0, tall, sizes, 0, unroll=4)
    squares[tall:, :] = jnp.zeros((8, SPAN), jnp.float32)

    shape = (tall, SPAN)
    lane = lane_of(shape)
    row_at = place_ref[0] - EDGE_ROWS + lax.broadcasted_iota(jnp.int32, shape, 0)
    col_at = place_ref[1] + jnp.where(lane < cols + EDGE_COLS, lane, lane - SPAN)

    def inside(off_y, off_x):
        y, x = row_at + off_y, col_at + off_x
        return (y >= 0) & (y < full_rows) & (x >= 0) & (x < full_cols)

    here_inside = inside(0, 0)
    for index, (off_y, off_x) in enumerate(PAIR_TAPS):
        present = here_inside & inside(off_y, off_x)
        both = squares[:tall, :] + shifted_by(squares[off_y : off_y + tall, :], off_x)
        distance = jnp.maximum(both - 2.0 * pairs[index], 0.0)
        pairs[index] = jnp.where(present, jnp.exp(distance * (-1.0 / feat_channels)), 0.0)
    wide = rows + EDGE_ROWS
    total = jnp.ones((wide, SPAN), jnp.float32)
    for index, (off_y, off_x) in enumerate(PAIR_TAPS):
        ahead = pairs[index, 4 : 4 + wide, :]
        behind = shifted_by(pairs[index, 4 - off_y : 4 - off_y + wide, :], -off_x)
        weights_ref[1 + index] = ahead
        weights_ref[13 + index] = behind
        total = total + (ahead + behind)
    scale = 1.0 / total
    weights_ref[0] = scale
    for index in range(1, 25):
        weights_ref[index] = weights_ref[index] * scale
    two_sweeps(weights_ref, lambda row: probs[row], next_probs, current_ref, rows)


def two_sweeps(weights_ref, read_row, middle, out_ref, rows):
    def first(row, carry):
        middle[row] = sweep_row(lambda o: weights_ref[o, pl.ds(row, 1), :], row + 4, read_row)
        return carry

    lax.fori_loop(0, rows + 8, first, 0, unroll=4)

    def second(row, carry):
        value = sweep_row(lambda o: weights_ref[o, pl.ds(row + 4, 1), :], row + 4, lambda r: middle[r])
        out_ref[row] = value[:, : out_ref.shape[2]]
        return carry

    lax.fori_loop(0, rows, second, 0, unroll=4)


def finish_kernel(weights_ref, up_ref, mid_ref, down_ref, out_ref, probs, next_probs):
    rows = mid_ref.shape[0]
    probs[:EDGE_ROWS] = up_ref[...]
    probs[EDGE_ROWS : EDGE_ROWS + rows] = mid_ref[...]
    probs[EDGE_ROWS + rows :] = down_ref[...]
    two_sweeps(weights_ref, lambda row: probs[row], next_probs, out_ref, rows)


COL = ("pair", "core")


def size_of(axes):
    return math.prod(lax.axis_size(a) for a in axes) if isinstance(axes, tuple) else lax.axis_size(axes)


def pass_on(cells, axis, step):
    ends = size_of(axis) - 1
    if step > 0:
        return lax.ppermute(cells, axis, [(i, i + 1) for i in range(ends)])
    return lax.ppermute(cells, axis, [(i + 1, i) for i in range(ends)])


def share_rows(teacher_feats, teacher_probs, student):
    rows = teacher_feats.shape[1]
    high = lax.reduce_precision(teacher_probs, 8, 7)
    low = teacher_probs - high
    mid = jnp.concatenate(
        [teacher_feats, high.astype(jnp.bfloat16), low.astype(jnp.bfloat16)], axis=0
    ).transpose(1, 0, 2)

    def message(first, row):
        return jnp.concatenate(
            [mid[first : first + EDGE_ROWS], student[row].reshape(EDGE_ROWS, -1, student.shape[2])], axis=1
        )

    up = pass_on(message(rows - EDGE_ROWS, rows - 1), "row", 1)
    down = pass_on(message(0, 0), "row", -1)
    return mid, up, down


def share_cols(mid, up, down, student):
    rows, channels, _ = mid.shape
    groups = rows // 8 + 2
    edge = jax.ShapeDtypeStruct((groups * channels + student.shape[1], 128), jnp.bfloat16)
    to_left, to_right = pl.pallas_call(
        edges_kernel, out_shape=(edge, edge), name="edges", compiler_params=vmem_of(16), cost_estimate=cost_of(2)
    )(up, mid, down, student)
    return pass_on(to_right, COL, 1), pass_on(to_left, COL, -1)


def refine(mid, up, down, left, right, feat_channels, classes):
    rows, _, cols = mid.shape
    place = jnp.stack([lax.axis_index("row") * rows, lax.axis_index(COL) * cols]).astype(jnp.int32)
    tall = rows + 2 * EDGE_ROWS
    vmem = pl.BlockSpec(memory_space=pltpu.VMEM)
    current, weights = pl.pallas_call(
        functools.partial(
            affinity_kernel,
            full_rows=rows * lax.axis_size("row"),
            full_cols=cols * size_of(COL),
            feat_channels=feat_channels,
            classes=classes,
        ),
        out_shape=(
            jax.ShapeDtypeStruct((rows, classes, SPAN), jnp.float32),
            jax.ShapeDtypeStruct((25, rows + EDGE_ROWS, SPAN), jnp.float32),
        ),
        in_specs=[pl.BlockSpec(memory_space=pltpu.SMEM)] + [vmem] * 5,
        out_specs=(vmem, vmem),
        scratch_shapes=[
            pltpu.VMEM((tall, feat_channels, SPAN), jnp.float32),
            pltpu.VMEM((tall, classes, SPAN), jnp.float32),
            pltpu.VMEM((rows + 8, classes, SPAN), jnp.float32),
            pltpu.VMEM((len(PAIR_TAPS), tall, SPAN), jnp.float32),
            pltpu.VMEM((tall + 8, SPAN), jnp.float32),
        ],
        name="affinity",
        compiler_params=vmem_of(20),
        cost_estimate=cost_of(12),
    )(place, up, mid, down, left, right)
    return current, weights


def finish(current, weights, cols, up, down):
    rows, classes, _ = current.shape
    tall = rows + 2 * EDGE_ROWS
    refined = pl.pallas_call(
        finish_kernel,
        out_shape=jax.ShapeDtypeStruct((rows, classes, cols), jnp.float32),
        scratch_shapes=[
            pltpu.VMEM((tall, classes, SPAN), jnp.float32),
            pltpu.VMEM((rows + 8, classes, SPAN), jnp.float32),
        ],
        name="finish",
        compiler_params=vmem_of(12),
        cost_estimate=cost_of(4),
    )(weights, up, current, down)
    return refined


CHIPS = ("row", "pair")
PARTNER = [(0, 1), (1, 0)]
CLASS_ROW = 36
MARK_ROW = 37
CHUNK_ROWS = 40


def tile_places(n_tiles, chips):
    full = n_tiles // chips
    for tile in range(n_tiles):
        if tile < full * chips:
            yield tile, 0, 8, tile // full, 8 * (tile % full)
        else:
            share = 8 * (n_tiles - full * chips) // chips
            for part in range(8 // share):
                chip = (tile - full * chips) * (8 // share) + part
                yield tile, part * share, share, chip, 8 * full


def write_chunks(chunk_ref, conv_ref, class_ref, half):
    height, width = conv_ref.shape[0] // 2, conv_ref.shape[1]
    chips = chunk_ref.shape[0]
    first = pl.multiple_of(half * height, height)
    chunk_ref[:, CLASS_ROW:, :] = jnp.zeros((chips, CHUNK_ROWS - CLASS_ROW, 128), jnp.float32)
    for tile, skip, count, chip, row in tile_places(height * width // 1024, chips):
        block, lane = tile // (width // 128), tile % (width // 128)
        rows = conv_ref[pl.ds(pl.multiple_of(first + 8 * block, 8), 8), 128 * lane : 128 * (lane + 1)]
        chunk_ref[chip, row : row + count, :] = rows[skip : skip + count]
    sums = jnp.where(half == 0, class_ref[:, :128], class_ref[:, 128:])
    for k in range(class_ref.shape[0]):
        chunk_ref[k, CLASS_ROW : CLASS_ROW + 1, :] = sums[k : k + 1]


def read_chunks(core_ref, own_ref, other_ref, conv_ref, class_ref, *, scale):
    _, channels, hidden = conv_ref.shape
    width = 3 * hidden
    chips = own_ref.shape[0]
    for half in range(2):
        mine = core_ref[0] == half
        for tile, skip, count, chip, row in tile_places(3 * channels * width // 2048, chips):
            block, lane = tile // (width // 128), tile % (width // 128)
            top = half * 3 * channels // 2 + 8 * block
            a, b = top // channels, 128 * lane // hidden
            value = jnp.where(mine, own_ref[chip, row : row + count, :], other_ref[chip, row : row + count, :])
            conv_ref[
                3 * a + b, top % channels + skip : top % channels + skip + count,
                128 * lane % hidden : 128 * lane % hidden + 128,
            ] = value * scale
        for k in range(class_ref.shape[0]):
            value = jnp.where(
                mine, own_ref[k, CLASS_ROW : CLASS_ROW + 1, :], other_ref[k, CLASS_ROW : CLASS_ROW + 1, :]
            )
            class_ref[k : k + 1, 128 * half : 128 * (half + 1)] = value * scale


def pack_half(values):
    marks = lax.broadcasted_iota(jnp.int32, values.shape, values.ndim - 2) == MARK_ROW
    largest = jnp.max(jnp.where(marks, 0.0, jnp.abs(values)), axis=-2, keepdims=True)
    exponent = jnp.clip(jnp.ceil(jnp.log2(jnp.maximum(largest, 1e-30))), -100.0, 120.0)
    return jnp.where(marks, exponent, values * jnp.exp2(14.0 - exponent)).astype(jnp.float16)


def unpack_half(packed):
    exponent = packed[..., MARK_ROW : MARK_ROW + 1, :].astype(jnp.float32)
    return packed.astype(jnp.float32) * jnp.exp2(exponent - 14.0)


def gather_all(total, core, conv_shape, class_shape, scale):
    mine = pack_half(total)
    spread = jnp.broadcast_to(mine[None], (size_of(CHIPS),) + mine.shape)
    own = lax.all_to_all(spread, CHIPS, split_axis=0, concat_axis=0, tiled=True)
    other = lax.ppermute(own, "core", PARTNER)
    vmem = pl.BlockSpec(memory_space=pltpu.VMEM)
    conv, small = pl.pallas_call(
        functools.partial(read_chunks, scale=scale),
        out_shape=(
            jax.ShapeDtypeStruct(conv_shape, jnp.float32),
            jax.ShapeDtypeStruct(class_shape[::-1], jnp.float32),
        ),
        in_specs=[pl.BlockSpec(memory_space=pltpu.SMEM), vmem, vmem],
        out_specs=(vmem, vmem),
        name="place",
        compiler_params=vmem_of(12),
        cost_estimate=cost_of(2),
    )(core, unpack_half(own), unpack_half(other))
    return conv, small.T


def unit_edges_kernel(up_ref, mid_ref, down_ref, left_ref, right_ref):
    sources = [up_ref.at[0]] + [mid_ref.at[i] for i in range(mid_ref.shape[0])] + [down_ref.at[0]]
    left, right = border_cells(sources, mid_ref.shape[1:])
    left_ref[...] = left.astype(left_ref.dtype)
    right_ref[...] = right.astype(right_ref.dtype)


def side_sums(side, weights):
    side = side.astype(jnp.float32)
    moved = [pltpu.roll(side, (128 - a) % 128, 1).astype(jnp.bfloat16) for a in range(3)]
    return jnp.dot(weights, jnp.concatenate(moved, axis=0), preferred_element_type=jnp.float32)


STEP_ROWS = 2


def joined(parts, out):
    cols = parts.shape[1]
    lanes = lane_of((out, cols))
    before = jnp.where(lanes == 0, 0.0, pltpu.roll(parts[:out], 1, 1))
    after = jnp.where(lanes == cols - 1, 0.0, pltpu.roll(parts[2 * out :], cols - 1, 1))
    return parts[out : 2 * out] + (before + after)


def convolve_kernel(mid_ref, taps_ref, pre_ref, weights_ref, padded):
    rows, channels, cols = mid_ref.shape
    out = weights_ref.shape[0] // 3

    @pl.when(pl.program_id(0) == 0)
    def _():
        for b in range(3):
            for a in range(3):
                weights_ref[out * b : out * (b + 1), channels * a : channels * (a + 1)] = taps_ref[3 * a + b].T
        padded[0] = jnp.zeros((channels, cols), padded.dtype)
        padded[pl.ds(1, rows)] = mid_ref[...]
        padded[rows + 1] = jnp.zeros((channels, cols), padded.dtype)

    for k in range(STEP_ROWS):
        row = pl.program_id(0) * STEP_ROWS + k
        stack = jnp.concatenate([padded[row], padded[row + 1], padded[row + 2]], axis=0)
        pre_ref[k] = joined(jnp.dot(weights_ref[...], stack, preferred_element_type=jnp.float32), out)


def activate_kernel(
    up_ref, down_ref, left_ref, right_ref, weights_ref, class_ref, pre_ref,
    slope_ref, hidden_ref, guess_ref, left_sum, right_sum, borders, *, skip,
):
    out, channels = weights_ref.shape[0] // 3, weights_ref.shape[1] // 3
    step = pl.program_id(0)

    @pl.when(step == 0)
    def _():
        left_sum[...] = side_sums(left_ref[-channels:], weights_ref[:out])
        right_sum[...] = side_sums(right_ref[-channels:], weights_ref[2 * out :])
        for index, ref in enumerate((up_ref, down_ref)):
            taps = weights_ref[:, 2 * channels * index : 2 * channels * index + channels]
            parts = jnp.dot(taps, packed_row(ref, skip), preferred_element_type=jnp.float32)
            borders[index] = joined(parts, out)

    lanes = lane_of((out, 128))
    for k in range(STEP_ROWS):
        row = step * STEP_ROWS + k
        left = jnp.where(lanes == 0, pltpu.roll(left_sum[...], (128 - row) % 128, 1), 0.0)
        right = jnp.where(lanes == 127, pltpu.roll(right_sum[...], 127 - row, 1), 0.0)
        pre_act = pre_ref[k]
        pre_act = jnp.concatenate([pre_act[:, :128] + left, pre_act[:, 128:] + right], axis=1)
        if k == 0:
            pre_act = pre_act + jnp.where(step == 0, borders[0], 0.0)
        if k == STEP_ROWS - 1:
            pre_act = pre_act + jnp.where(step == pl.num_programs(0) - 1, borders[1], 0.0)
        logistic = 0.5 * jnp.tanh(0.5 * pre_act) + 0.5
        silu = pre_act * logistic
        slope_ref[k] = logistic + silu * (1.0 - logistic)
        hidden = silu.astype(jnp.bfloat16)
        hidden_ref[k] = hidden
        logit = jnp.dot(class_ref[...], hidden, preferred_element_type=jnp.float32)
        guess_ref[k] = 0.5 * jnp.tanh(0.5 * logit) + 0.5


def back_kernel(guess_ref, refined_ref, slope_ref, class_ref, back_ref, error_ref):
    for k in range(STEP_ROWS):
        error = (guess_ref[k] - refined_ref[k]).astype(jnp.bfloat16)
        error_ref[k] = error
        summed = jnp.dot(class_ref[...], error, preferred_element_type=jnp.float32)
        back_ref[k] = (summed * slope_ref[k]).astype(jnp.bfloat16)


CONTRACT_LAST = (((1,), (1,)), ((), ()))


def grads_kernel(
    core_ref, up_ref, mid_ref, down_ref, left_ref, right_ref, back_ref, hidden_ref, error_ref,
    keep_ref, send_ref, padded, first_cols, last_cols, conv_ref, class_ref,
):
    rows, channels, cols = mid_ref.shape
    step = pl.program_id(0)

    @pl.when(step == 0)
    def _():
        padded[0] = packed_row(up_ref, up_ref.shape[1] - channels // EDGE_ROWS)
        padded[pl.ds(1, rows)] = mid_ref[...]
        padded[rows + 1] = packed_row(down_ref, down_ref.shape[1] - channels // EDGE_ROWS)
        conv_ref[...] = jnp.zeros(conv_ref.shape, jnp.float32)
        class_ref[...] = jnp.zeros(class_ref.shape, jnp.float32)
        first_cols[...] = jnp.zeros(first_cols.shape, jnp.float32)
        last_cols[...] = jnp.zeros(last_cols.shape, jnp.float32)

    lanes = lane_of((back_ref.shape[1], cols))
    narrow = lane_of((back_ref.shape[1], 128))
    images, backs = [], []
    for k in range(STEP_ROWS):
        row = step * STEP_ROWS + k
        images.append(jnp.concatenate([padded[row], padded[row + 1], padded[row + 2]], axis=0))
        back = back_ref[k].astype(jnp.float32)
        first_cols[...] = jnp.where(narrow == row + 1, pltpu.roll(back[:, :128], row + 1, 1), first_cols[...])
        last_cols[...] = jnp.where(narrow == row + 1, pltpu.roll(back[:, cols - 128 :], row + 2, 1), last_cols[...])
        below = jnp.where(lanes == cols - 1, 0.0, pltpu.roll(back, cols - 1, 1))
        above = jnp.where(lanes == 0, 0.0, pltpu.roll(back, 1, 1))
        backs.append(
            jnp.concatenate([below.astype(jnp.bfloat16), back_ref[k], above.astype(jnp.bfloat16)], axis=0)
        )
        class_ref[...] += lax.dot_general(
            error_ref[k], hidden_ref[k], CONTRACT_LAST, preferred_element_type=jnp.float32
        )
    conv_ref[...] += lax.dot_general(
        jnp.concatenate(images, axis=1), jnp.concatenate(backs, axis=1), CONTRACT_LAST,
        preferred_element_type=jnp.float32,
    )

    @pl.when(step == pl.num_programs(0) - 1)
    def _():
        hidden = back_ref.shape[1]
        for side_ref, cells, place in ((left_ref, first_cols, 0), (right_ref, last_cols, 2 * hidden)):
            side = side_ref[-channels:].astype(jnp.float32)
            moved = [pltpu.roll(side, (1 - a) % 128, 1).astype(jnp.bfloat16) for a in range(3)]
            conv_ref[:, pl.ds(place, hidden)] += lax.dot_general(
                jnp.concatenate(moved, axis=0), cells[...].astype(jnp.bfloat16), CONTRACT_LAST,
                preferred_element_type=jnp.float32,
            )
        write_chunks(keep_ref, conv_ref, class_ref, core_ref[0])
        write_chunks(send_ref, conv_ref, class_ref, 1 - core_ref[0])


def feature_kernel(
    up_ref, above_ref, mid_ref, below_ref, down_ref, left_ref, right_ref, taps_ref, out_ref,
    left_sum, right_sum, weights_ref,
):
    out, channels = weights_ref.shape[0] // 3, weights_ref.shape[1] // 3
    cols = mid_ref.shape[2]
    step = pl.program_id(0)

    @pl.when(step == 0)
    def _():
        for b in range(3):
            for a in range(3):
                tap = taps_ref[3 * (2 - a) + (2 - b)]
                weights_ref[out * b : out * (b + 1), channels * a : channels * (a + 1)] = tap
        left_sum[...] = side_sums(left_ref[...], weights_ref[:out])
        right_sum[...] = side_sums(right_ref[...], weights_ref[2 * out :])

    above = jnp.where(step == 0, up_ref[0], above_ref[STEP_ROWS - 1])
    below = jnp.where(step == pl.num_programs(0) - 1, down_ref[0], below_ref[0])
    cells = [above] + [mid_ref[k] for k in range(STEP_ROWS)] + [below]
    lanes = lane_of((out, 128))
    for k in range(STEP_ROWS):
        row = step * STEP_ROWS + k
        parts = jnp.dot(
            weights_ref[...], jnp.concatenate(cells[k : k + 3], axis=0), preferred_element_type=jnp.float32
        )
        before = pltpu.roll(parts[:out], 1, 1)
        after = pltpu.roll(parts[2 * out :], cols - 1, 1)
        left = pltpu.roll(left_sum[...], (128 - row) % 128, 1)
        right = pltpu.roll(right_sum[...], 127 - row, 1)
        before = jnp.concatenate([jnp.where(lanes == 0, left, before[:, :128]), before[:, 128:]], axis=1)
        after = jnp.concatenate([after[:, :-128], jnp.where(lanes == 127, right, after[:, -128:])], axis=1)
        out_ref[k] = (parts[out : 2 * out] + (before + after)).astype(out_ref.dtype)


def in_hbm(*arrays):
    return tuple(pltpu.with_memory_space_constraint(a, pltpu.HBM) for a in arrays)


def whole(array):
    return pl.BlockSpec(array.shape, lambda i: (0,) * array.ndim, pipeline_mode=pl.Buffered(1))


def by_rows(shape):
    return pl.BlockSpec((STEP_ROWS,) + shape[1:], lambda i: (i, 0, 0))


def unit_rows(cells):
    return pass_on(cells[-1:], "row", 1), pass_on(cells[:1], "row", -1)


def unit_cols(cells, up, down):
    edge = jax.ShapeDtypeStruct((cells.shape[1], 128), cells.dtype)
    to_left, to_right = pl.pallas_call(
        unit_edges_kernel, out_shape=(edge, edge), name="unit_edges",
        compiler_params=vmem_of(16),
        cost_estimate=cost_of(1),
    )(up, cells, down)
    return pass_on(to_right, COL, 1), pass_on(to_left, COL, -1)


def row_call(kernel, rows, args, arg_rows, outs, out_rows, scratch, vmem, micros):
    return pl.pallas_call(
        kernel,
        grid=(rows // STEP_ROWS,),
        in_specs=[
            pl.BlockSpec(memory_space=pltpu.SMEM) if a.ndim == 1 else by_rows(a.shape) if split else whole(a)
            for a, split in zip(args, arg_rows)
        ],
        out_specs=tuple(by_rows(o.shape) if split else whole(o) for o, split in zip(outs, out_rows)),
        out_shape=tuple(outs),
        scratch_shapes=scratch,
        compiler_params=vmem_of(vmem),
        cost_estimate=cost_of(micros),
    )(*args)


def local_step(teacher_feats, teacher_probs, student_feats, conv_weight, class_weight):
    channels, rows, cols = student_feats.shape
    hidden_size, classes = class_weight.shape
    pixel_count = float(rows * cols)
    student = student_feats.transpose(1, 0, 2)
    f32, bf16 = jnp.float32, jnp.bfloat16
    mid, up, down = share_rows(teacher_feats, teacher_probs, student)
    pre_act, stacked = row_call(
        convolve_kernel, rows, (student, conv_weight), [False] * 2,
        [
            jax.ShapeDtypeStruct((rows, hidden_size, cols), f32),
            jax.ShapeDtypeStruct((3 * hidden_size, 3 * channels), bf16),
        ],
        [True, False], [pltpu.VMEM((rows + 2, channels, cols), bf16)], 16, 9,
    )
    left, right = share_cols(mid, up, down, student)
    halo = (up, student, down, left, right)
    current, weights = refine(mid, up, down, left, right, teacher_feats.shape[0], classes)
    current_rows = pass_on(current[rows - EDGE_ROWS :], "row", 1), pass_on(current[:EDGE_ROWS], "row", -1)
    slope, hidden, guess = row_call(
        functools.partial(activate_kernel, skip=mid.shape[1]), rows,
        (up, down, left, right, stacked, class_weight.T, pre_act), [False] * 6 + [True],
        [
            jax.ShapeDtypeStruct((rows, hidden_size, cols), f32),
            jax.ShapeDtypeStruct((rows, hidden_size, cols), bf16),
            jax.ShapeDtypeStruct((rows, classes, cols), f32),
        ],
        [True] * 3,
        [pltpu.VMEM((hidden_size, 128), f32)] * 2 + [pltpu.VMEM((2, hidden_size, cols), f32)], 16, 7,
    )
    refined = finish(current, weights, cols, *current_rows)
    back, error = row_call(
        back_kernel, rows, (guess, refined, slope, class_weight), [True, True, True, False],
        [
            jax.ShapeDtypeStruct((rows, hidden_size, cols), bf16),
            jax.ShapeDtypeStruct((rows, classes, cols), bf16),
        ],
        [True] * 2, [], 16, 2,
    )
    back_up, back_down = unit_rows(back)
    core = lax.axis_index("core").astype(jnp.int32).reshape(1)
    chunks = jax.ShapeDtypeStruct((size_of(CHIPS), CHUNK_ROWS, 128), f32)
    keep, sent = row_call(
        grads_kernel, rows, (core,) + halo + (back, hidden, error), [False] * 6 + [True] * 3,
        [chunks, chunks], [False] * 2,
        [pltpu.VMEM((rows + 2, channels, cols), bf16)]
        + [pltpu.VMEM((hidden_size, 128), f32)] * 2
        + [pltpu.VMEM((3 * channels, 3 * hidden_size), f32), pltpu.VMEM((classes, hidden_size), f32)], 28, 9,
    )
    back_up, back_down, sent = lax.optimization_barrier((back_up, back_down, sent))
    other = lax.ppermute(sent, "core", PARTNER)
    back_cols = unit_cols(back, back_up, back_down)
    packed = pack_half(keep + other)
    back_left, back_right, packed = lax.optimization_barrier(back_cols + (packed,))
    steps = rows // STEP_ROWS
    block = (STEP_ROWS, hidden_size, cols)
    feature_args = in_hbm(back_up, back, back_down, back_left, back_right, conv_weight)
    feature_grad = pl.pallas_call(
        feature_kernel,
        grid=(steps,),
        in_specs=[
            whole(back_up),
            pl.BlockSpec(block, lambda i: (jnp.maximum(i - 1, 0), 0, 0)),
            pl.BlockSpec(block, lambda i: (i, 0, 0)),
            pl.BlockSpec(block, lambda i: (jnp.minimum(i + 1, steps - 1), 0, 0)),
            whole(back_down), whole(back_left), whole(back_right), whole(conv_weight),
        ],
        out_specs=by_rows((rows, channels, cols)),
        out_shape=jax.ShapeDtypeStruct((rows, channels, cols), bf16),
        scratch_shapes=[pltpu.VMEM((channels, 128), f32)] * 2
        + [pltpu.VMEM((3 * channels, 3 * hidden_size), bf16)],
        name="feature",
        compiler_params=vmem_of(16),
        cost_estimate=cost_of(8),
    )(feature_args[0], feature_args[1], feature_args[1], feature_args[1], *feature_args[2:])
    received = lax.all_to_all(packed, CHIPS, split_axis=0, concat_axis=0, tiled=True)
    total = jnp.sum(unpack_half(received), axis=0)
    total, feature_grad = lax.optimization_barrier((total, feature_grad))
    grad_conv, grad_class = gather_all(total, core, conv_weight.shape, class_weight.shape, 1.0 / pixel_count)
    return (refined.transpose(1, 0, 2), feature_grad.transpose(1, 0, 2), grad_conv, grad_class)


def solution(mesh):
    devices = mesh.devices
    mesh = Mesh(devices.reshape(devices.shape[0], -1, 2), ("row",) + COL)
    split = P(None, "row", COL)
    in_specs = (split, split, split, P(), P())
    out_specs = (split, split, P(), P())
    return jax.shard_map(local_step, mesh=mesh, in_specs=in_specs, out_specs=out_specs, check_vma=False)
```

```python
import functools
import math

import jax
import jax.numpy as jnp
from jax import lax
from jax.experimental import pallas as pl
from jax.experimental.pallas import tpu as pltpu
from jax.sharding import Mesh
from jax.sharding import PartitionSpec as P


EDGE_ROWS = 8
EDGE_COLS = 16
SPAN = 384
GROUP = 4
PAIR_TAPS = [tap for s in (1, 2, 4) for tap in ((0, s), (s, -s), (s, 0), (s, s))]


def shifted_by(cells, off_x):
    return cells if off_x == 0 else pltpu.roll(cells, (-off_x) % cells.shape[-1], cells.ndim - 1)


def vmem_of(mib):
    return pltpu.CompilerParams(vmem_limit_bytes=mib * 2**20)


def cost_of(micros):
    return pl.CostEstimate(flops=int(micros * 1e9), transcendentals=0, bytes_accessed=int(micros * 3e6))


def lane_of(shape):
    return lax.broadcasted_iota(jnp.int32, shape, len(shape) - 1)


def packed_row(ref, skip):
    return jnp.concatenate([ref[i, skip:, :] for i in range(EDGE_ROWS)], axis=0)


def edges_kernel(up_ref, mid_ref, down_ref, student_ref, left_ref, right_ref):
    rows, channels, _ = mid_ref.shape
    group = lane_of((channels, 128)) // EDGE_COLS
    groups = rows // 8 + 2
    for g in range(groups):
        source = up_ref if g == 0 else down_ref if g == groups - 1 else mid_ref.at[pl.ds(8 * (g - 1), 8)]
        left = jnp.zeros((channels, 128), jnp.float32)
        right = jnp.zeros((channels, 128), jnp.float32)
        for i in range(8):
            first = source[i, :channels, :128].astype(jnp.float32)
            last = source[i, :channels, -128:].astype(jnp.float32)
            left = jnp.where(group == i, pltpu.roll(first, EDGE_COLS * i, 1), left)
            right = jnp.where(group == i, pltpu.roll(last, (EDGE_COLS * (i + 1)) % 128, 1), right)
        left_ref[channels * g : channels * (g + 1)] = left.astype(left_ref.dtype)
        right_ref[channels * g : channels * (g + 1)] = right.astype(right_ref.dtype)
    up, down = packed_row(up_ref, channels), packed_row(down_ref, channels)
    left, right = border_cells([up] + [student_ref.at[i] for i in range(rows)] + [down], student_ref.shape[1:])
    left_ref[channels * groups :] = left.astype(left_ref.dtype)
    right_ref[channels * groups :] = right.astype(right_ref.dtype)


def border_cells(sources, shape):
    channels, cols = shape
    lanes = lane_of((channels, 128))
    left = jnp.zeros((channels, 128), jnp.float32)
    right = jnp.zeros((channels, 128), jnp.float32)
    for i, source in enumerate(sources):
        first = source[:, :128].astype(jnp.float32)
        last = source[:, cols - 128 :].astype(jnp.float32)
        left = jnp.where(lanes == i, pltpu.roll(first, i, 1), left)
        right = jnp.where(lanes == i, pltpu.roll(last, i + 1, 1), right)
    return left, right


def sweep_row(weights, center_row, read_row):
    total = weights(0) * read_row(center_row)
    for index, (off_y, off_x) in enumerate(PAIR_TAPS):
        total += weights(1 + index) * shifted_by(read_row(center_row + off_y), off_x)
        total += weights(13 + index) * shifted_by(read_row(center_row - off_y), -off_x)
    return total


def affinity_kernel(
    place_ref, up_ref, mid_ref, down_ref, left_ref, right_ref, current_ref, weights_ref,
    feats, probs, next_probs, pairs, squares, *, full_rows, full_cols, feat_channels, classes,
):
    rows = mid_ref.shape[0]
    cols = mid_ref.shape[2]
    tall = rows + 2 * EDGE_ROWS
    channels = mid_ref.shape[1]
    lanes = lane_of((channels, 128))

    def gather(i, carry):
        for g in range(tall // 8):
            if g == 0:
                body = up_ref[i, :channels]
            elif g == tall // 8 - 1:
                body = down_ref[i, :channels]
            else:
                body = mid_ref[8 * (g - 1) + i]
            from_right = pltpu.roll(right_ref[channels * g : channels * (g + 1)].astype(jnp.float32), (128 - EDGE_COLS * i) % 128, 1)
            from_left = pltpu.roll(left_ref[channels * g : channels * (g + 1)].astype(jnp.float32), (240 - EDGE_COLS * i) % 128, 1)
            side = jnp.where(lanes < EDGE_COLS, from_right, jnp.where(lanes >= 128 - EDGE_COLS, from_left, 0.0))
            body = body.astype(jnp.float32)
            row = 8 * g + i
            high, low = feat_channels, feat_channels + classes
            feats[row, :, :cols] = body[:high]
            feats[row, :, cols:] = side[:high]
            probs[row, :, :cols] = body[high:low] + body[low:]
            probs[row, :, cols:] = side[high:low] + side[low:]
        return carry

    lax.fori_loop(0, 8, gather, 0)
    pairs[:, tall - 8 :, :] = jnp.zeros((len(PAIR_TAPS), 8, SPAN), jnp.float32)

    for ring, radius in enumerate((1, 2, 4)):

        def products(step, carry, ring=ring, radius=radius):
            rows_at = [step * GROUP + g for g in range(GROUP)]
            sums = [[None] * 4 for _ in rows_at]
            for c in range(feat_channels // 8):
                for g, row in enumerate(rows_at):
                    here = feats[row, 8 * c : 8 * c + 8, :]
                    there = feats[row + radius, 8 * c : 8 * c + 8, :]
                    for k, (off_y, off_x) in enumerate(PAIR_TAPS[4 * ring : 4 * ring + 4]):
                        product = here * shifted_by(there if off_y else here, off_x)
                        sums[g][k] = product if c == 0 else sums[g][k] + product
            totals = [[jnp.sum(cells, axis=0, keepdims=True) for cells in row_sums] for row_sums in sums]
            for g, row in enumerate(rows_at):
                for k in range(4):
                    pairs[4 * ring + k, pl.ds(row, 1), :] = totals[g][k]
            return carry

        lax.fori_loop(0, (tall - 4) // GROUP, products, 0)

    def sizes(row, carry):
        cells = feats[row]
        squares[pl.ds(row, 1), :] = jnp.sum(cells * cells, axis=0, keepdims=True)
        return carry

    lax.fori_loop(0, tall, sizes, 0, unroll=4)
    squares[tall:, :] = jnp.zeros((8, SPAN), jnp.float32)

    shape = (tall, SPAN)
    lane = lane_of(shape)
    row_at = place_ref[0] - EDGE_ROWS + lax.broadcasted_iota(jnp.int32, shape, 0)
    col_at = place_ref[1] + jnp.where(lane < cols + EDGE_COLS, lane, lane - SPAN)

    def inside(off_y, off_x):
        y, x = row_at + off_y, col_at + off_x
        return (y >= 0) & (y < full_rows) & (x >= 0) & (x < full_cols)

    here_inside = inside(0, 0)
    for index, (off_y, off_x) in enumerate(PAIR_TAPS):
        present = here_inside & inside(off_y, off_x)
        both = squares[:tall, :] + shifted_by(squares[off_y : off_y + tall, :], off_x)
        distance = jnp.maximum(both - 2.0 * pairs[index], 0.0)
        pairs[index] = jnp.where(present, jnp.exp(distance * (-1.0 / feat_channels)), 0.0)
    wide = rows + EDGE_ROWS
    total = jnp.ones((wide, SPAN), jnp.float32)
    for index, (off_y, off_x) in enumerate(PAIR_TAPS):
        ahead = pairs[index, 4 : 4 + wide, :]
        behind = shifted_by(pairs[index, 4 - off_y : 4 - off_y + wide, :], -off_x)
        weights_ref[1 + index] = ahead
        weights_ref[13 + index] = behind
        total = total + (ahead + behind)
    scale = 1.0 / total
    weights_ref[0] = scale
    for index in range(1, 25):
        weights_ref[index] = weights_ref[index] * scale
    two_sweeps(weights_ref, lambda row: probs[row], next_probs, current_ref, rows)


def two_sweeps(weights_ref, read_row, middle, out_ref, rows):
    def first(row, carry):
        middle[row] = sweep_row(lambda o: weights_ref[o, pl.ds(row, 1), :], row + 4, read_row)
        return carry

    lax.fori_loop(0, rows + 8, first, 0, unroll=4)

    def second(row, carry):
        value = sweep_row(lambda o: weights_ref[o, pl.ds(row + 4, 1), :], row + 4, lambda r: middle[r])
        out_ref[row] = value[:, : out_ref.shape[2]]
        return carry

    lax.fori_loop(0, rows, second, 0, unroll=4)


def finish_kernel(weights_ref, up_ref, mid_ref, down_ref, out_ref, probs, next_probs):
    rows = mid_ref.shape[0]
    probs[:EDGE_ROWS] = up_ref[...]
    probs[EDGE_ROWS : EDGE_ROWS + rows] = mid_ref[...]
    probs[EDGE_ROWS + rows :] = down_ref[...]
    two_sweeps(weights_ref, lambda row: probs[row], next_probs, out_ref, rows)


COL = ("pair", "core")


def size_of(axes):
    return math.prod(lax.axis_size(a) for a in axes) if isinstance(axes, tuple) else lax.axis_size(axes)


def pass_on(cells, axis, step):
    ends = size_of(axis) - 1
    if step > 0:
        return lax.ppermute(cells, axis, [(i, i + 1) for i in range(ends)])
    return lax.ppermute(cells, axis, [(i + 1, i) for i in range(ends)])


def share_rows(teacher_feats, teacher_probs, student):
    rows = teacher_feats.shape[1]
    high = lax.reduce_precision(teacher_probs, 8, 7)
    low = teacher_probs - high
    mid = jnp.concatenate(
        [teacher_feats, high.astype(jnp.bfloat16), low.astype(jnp.bfloat16)], axis=0
    ).transpose(1, 0, 2)

    def message(first, row):
        return jnp.concatenate(
            [mid[first : first + EDGE_ROWS], student[row].reshape(EDGE_ROWS, -1, student.shape[2])], axis=1
        )

    up = pass_on(message(rows - EDGE_ROWS, rows - 1), "row", 1)
    down = pass_on(message(0, 0), "row", -1)
    return mid, up, down


def share_cols(mid, up, down, student):
    rows, channels, _ = mid.shape
    groups = rows // 8 + 2
    edge = jax.ShapeDtypeStruct((groups * channels + student.shape[1], 128), jnp.bfloat16)
    to_left, to_right = pl.pallas_call(
        edges_kernel, out_shape=(edge, edge), name="edges", compiler_params=vmem_of(16), cost_estimate=cost_of(2)
    )(up, mid, down, student)
    return pass_on(to_right, COL, 1), pass_on(to_left, COL, -1)


def refine(mid, up, down, left, right, feat_channels, classes):
    rows, _, cols = mid.shape
    place = jnp.stack([lax.axis_index("row") * rows, lax.axis_index(COL) * cols]).astype(jnp.int32)
    tall = rows + 2 * EDGE_ROWS
    vmem = pl.BlockSpec(memory_space=pltpu.VMEM)
    current, weights = pl.pallas_call(
        functools.partial(
            affinity_kernel,
            full_rows=rows * lax.axis_size("row"),
            full_cols=cols * size_of(COL),
            feat_channels=feat_channels,
            classes=classes,
        ),
        out_shape=(
            jax.ShapeDtypeStruct((rows, classes, SPAN), jnp.float32),
            jax.ShapeDtypeStruct((25, rows + EDGE_ROWS, SPAN), jnp.float32),
        ),
        in_specs=[pl.BlockSpec(memory_space=pltpu.SMEM)] + [vmem] * 5,
        out_specs=(vmem, vmem),
        scratch_shapes=[
            pltpu.VMEM((tall, feat_channels, SPAN), jnp.float32),
            pltpu.VMEM((tall, classes, SPAN), jnp.float32),
            pltpu.VMEM((rows + 8, classes, SPAN), jnp.float32),
            pltpu.VMEM((len(PAIR_TAPS), tall, SPAN), jnp.float32),
            pltpu.VMEM((tall + 8, SPAN), jnp.float32),
        ],
        name="affinity",
        compiler_params=vmem_of(20),
        cost_estimate=cost_of(12),
    )(place, up, mid, down, left, right)
    return current, weights


def finish(current, weights, cols, up, down):
    rows, classes, _ = current.shape
    tall = rows + 2 * EDGE_ROWS
    refined = pl.pallas_call(
        finish_kernel,
        out_shape=jax.ShapeDtypeStruct((rows, classes, cols), jnp.float32),
        scratch_shapes=[
            pltpu.VMEM((tall, classes, SPAN), jnp.float32),
            pltpu.VMEM((rows + 8, classes, SPAN), jnp.float32),
        ],
        name="finish",
        compiler_params=vmem_of(12),
        cost_estimate=cost_of(4),
    )(weights, up, current, down)
    return refined


CHIPS = ("row", "pair")
PARTNER = [(0, 1), (1, 0)]
CLASS_ROW = 36
MARK_ROW = 37
CHUNK_ROWS = 40


def tile_places(n_tiles, chips):
    full = n_tiles // chips
    for tile in range(n_tiles):
        if tile < full * chips:
            yield tile, 0, 8, tile // full, 8 * (tile % full)
        else:
            share = 8 * (n_tiles - full * chips) // chips
            for part in range(8 // share):
                chip = (tile - full * chips) * (8 // share) + part
                yield tile, part * share, share, chip, 8 * full


def write_chunks(chunk_ref, conv_ref, class_ref, half):
    height, width = conv_ref.shape[0] // 2, conv_ref.shape[1]
    chips = chunk_ref.shape[0]
    first = pl.multiple_of(half * height, height)
    chunk_ref[:, CLASS_ROW:, :] = jnp.zeros((chips, CHUNK_ROWS - CLASS_ROW, 128), jnp.float32)
    for tile, skip, count, chip, row in tile_places(height * width // 1024, chips):
        block, lane = tile // (width // 128), tile % (width // 128)
        rows = conv_ref[pl.ds(pl.multiple_of(first + 8 * block, 8), 8), 128 * lane : 128 * (lane + 1)]
        chunk_ref[chip, row : row + count, :] = rows[skip : skip + count]
    sums = jnp.where(half == 0, class_ref[:, :128], class_ref[:, 128:])
    for k in range(class_ref.shape[0]):
        chunk_ref[k, CLASS_ROW : CLASS_ROW + 1, :] = sums[k : k + 1]


def read_chunks(core_ref, own_ref, other_ref, conv_ref, class_ref, *, scale):
    _, channels, hidden = conv_ref.shape
    width = 3 * hidden
    chips = own_ref.shape[0]
    for half in range(2):
        mine = core_ref[0] == half
        for tile, skip, count, chip, row in tile_places(3 * channels * width // 2048, chips):
            block, lane = tile // (width // 128), tile % (width // 128)
            top = half * 3 * channels // 2 + 8 * block
            a, b = top // channels, 128 * lane // hidden
            value = jnp.where(mine, own_ref[chip, row : row + count, :], other_ref[chip, row : row + count, :])
            conv_ref[
                3 * a + b, top % channels + skip : top % channels + skip + count,
                128 * lane % hidden : 128 * lane % hidden + 128,
            ] = value * scale
        for k in range(class_ref.shape[0]):
            value = jnp.where(
                mine, own_ref[k, CLASS_ROW : CLASS_ROW + 1, :], other_ref[k, CLASS_ROW : CLASS_ROW + 1, :]
            )
            class_ref[k : k + 1, 128 * half : 128 * (half + 1)] = value * scale


def pack_half(values):
    marks = lax.broadcasted_iota(jnp.int32, values.shape, values.ndim - 2) == MARK_ROW
    largest = jnp.max(jnp.where(marks, 0.0, jnp.abs(values)), axis=-2, keepdims=True)
    exponent = jnp.clip(jnp.ceil(jnp.log2(jnp.maximum(largest, 1e-30))), -100.0, 120.0)
    return jnp.where(marks, exponent, values * jnp.exp2(14.0 - exponent)).astype(jnp.float16)


def unpack_half(packed):
    exponent = packed[..., MARK_ROW : MARK_ROW + 1, :].astype(jnp.float32)
    return packed.astype(jnp.float32) * jnp.exp2(exponent - 14.0)


def gather_all(total, core, conv_shape, class_shape, scale):
    mine = pack_half(total)
    spread = jnp.broadcast_to(mine[None], (size_of(CHIPS),) + mine.shape)
    own = lax.all_to_all(spread, CHIPS, split_axis=0, concat_axis=0, tiled=True)
    other = lax.ppermute(own, "core", PARTNER)
    vmem = pl.BlockSpec(memory_space=pltpu.VMEM)
    conv, small = pl.pallas_call(
        functools.partial(read_chunks, scale=scale),
        out_shape=(
            jax.ShapeDtypeStruct(conv_shape, jnp.float32),
            jax.ShapeDtypeStruct(class_shape[::-1], jnp.float32),
        ),
        in_specs=[pl.BlockSpec(memory_space=pltpu.SMEM), vmem, vmem],
        out_specs=(vmem, vmem),
        name="place",
        compiler_params=vmem_of(12),
        cost_estimate=cost_of(2),
    )(core, unpack_half(own), unpack_half(other))
    return conv, small.T


def unit_edges_kernel(up_ref, mid_ref, down_ref, left_ref, right_ref):
    sources = [up_ref.at[0]] + [mid_ref.at[i] for i in range(mid_ref.shape[0])] + [down_ref.at[0]]
    left, right = border_cells(sources, mid_ref.shape[1:])
    left_ref[...] = left.astype(left_ref.dtype)
    right_ref[...] = right.astype(right_ref.dtype)


def side_sums(side, weights):
    side = side.astype(jnp.float32)
    moved = [pltpu.roll(side, (128 - a) % 128, 1).astype(jnp.bfloat16) for a in range(3)]
    return jnp.dot(weights, jnp.concatenate(moved, axis=0), preferred_element_type=jnp.float32)


STEP_ROWS = 4


def joined(parts, out):
    cols = parts.shape[1]
    lanes = lane_of((out, cols))
    before = jnp.where(lanes == 0, 0.0, pltpu.roll(parts[:out], 1, 1))
    after = jnp.where(lanes == cols - 1, 0.0, pltpu.roll(parts[2 * out :], cols - 1, 1))
    return parts[out : 2 * out] + (before + after)


def convolve_kernel(mid_ref, taps_ref, pre_ref, weights_ref, padded):
    rows, channels, cols = mid_ref.shape
    out = weights_ref.shape[0] // 3

    @pl.when(pl.program_id(0) == 0)
    def _():
        for b in range(3):
            for a in range(3):
                weights_ref[out * b : out * (b + 1), channels * a : channels * (a + 1)] = taps_ref[3 * a + b].T
        padded[0] = jnp.zeros((channels, cols), padded.dtype)
        padded[pl.ds(1, rows)] = mid_ref[...]
        padded[rows + 1] = jnp.zeros((channels, cols), padded.dtype)

    for k in range(STEP_ROWS):
        row = pl.program_id(0) * STEP_ROWS + k
        stack = jnp.concatenate([padded[row], padded[row + 1], padded[row + 2]], axis=0)
        pre_ref[k] = joined(jnp.dot(weights_ref[...], stack, preferred_element_type=jnp.float32), out)


def activate_kernel(
    up_ref, down_ref, left_ref, right_ref, weights_ref, class_ref, pre_ref,
    slope_ref, hidden_ref, guess_ref, left_sum, right_sum, borders, *, skip,
):
    out, channels = weights_ref.shape[0] // 3, weights_ref.shape[1] // 3
    step = pl.program_id(0)

    @pl.when(step == 0)
    def _():
        left_sum[...] = side_sums(left_ref[-channels:], weights_ref[:out])
        right_sum[...] = side_sums(right_ref[-channels:], weights_ref[2 * out :])
        for index, ref in enumerate((up_ref, down_ref)):
            taps = weights_ref[:, 2 * channels * index : 2 * channels * index + channels]
            parts = jnp.dot(taps, packed_row(ref, skip), preferred_element_type=jnp.float32)
            borders[index] = joined(parts, out)

    lanes = lane_of((out, 128))
    for k in range(STEP_ROWS):
        row = step * STEP_ROWS + k
        left = jnp.where(lanes == 0, pltpu.roll(left_sum[...], (128 - row) % 128, 1), 0.0)
        right = jnp.where(lanes == 127, pltpu.roll(right_sum[...], 127 - row, 1), 0.0)
        pre_act = pre_ref[k]
        pre_act = jnp.concatenate([pre_act[:, :128] + left, pre_act[:, 128:] + right], axis=1)
        if k == 0:
            pre_act = pre_act + jnp.where(step == 0, borders[0], 0.0)
        if k == STEP_ROWS - 1:
            pre_act = pre_act + jnp.where(step == pl.num_programs(0) - 1, borders[1], 0.0)
        logistic = 0.5 * jnp.tanh(0.5 * pre_act) + 0.5
        silu = pre_act * logistic
        slope_ref[k] = logistic + silu * (1.0 - logistic)
        hidden = silu.astype(jnp.bfloat16)
        hidden_ref[k] = hidden
        logit = jnp.dot(class_ref[...], hidden, preferred_element_type=jnp.float32)
        guess_ref[k] = 0.5 * jnp.tanh(0.5 * logit) + 0.5


def back_kernel(guess_ref, refined_ref, slope_ref, class_ref, back_ref, error_ref):
    for k in range(STEP_ROWS):
        error = (guess_ref[k] - refined_ref[k]).astype(jnp.bfloat16)
        error_ref[k] = error
        summed = jnp.dot(class_ref[...], error, preferred_element_type=jnp.float32)
        back_ref[k] = (summed * slope_ref[k]).astype(jnp.bfloat16)


CONTRACT_LAST = (((1,), (1,)), ((), ()))


def grads_kernel(
    core_ref, up_ref, mid_ref, down_ref, left_ref, right_ref, back_ref, hidden_ref, error_ref,
    keep_ref, send_ref, padded, first_cols, last_cols, conv_ref, class_ref,
):
    rows, channels, cols = mid_ref.shape
    step = pl.program_id(0)

    @pl.when(step == 0)
    def _():
        padded[0] = packed_row(up_ref, up_ref.shape[1] - channels // EDGE_ROWS)
        padded[pl.ds(1, rows)] = mid_ref[...]
        padded[rows + 1] = packed_row(down_ref, down_ref.shape[1] - channels // EDGE_ROWS)
        conv_ref[...] = jnp.zeros(conv_ref.shape, jnp.float32)
        class_ref[...] = jnp.zeros(class_ref.shape, jnp.float32)
        first_cols[...] = jnp.zeros(first_cols.shape, jnp.float32)
        last_cols[...] = jnp.zeros(last_cols.shape, jnp.float32)

    lanes = lane_of((back_ref.shape[1], cols))
    narrow = lane_of((back_ref.shape[1], 128))
    images, backs = [], []
    for k in range(STEP_ROWS):
        row = step * STEP_ROWS + k
        images.append(jnp.concatenate([padded[row], padded[row + 1], padded[row + 2]], axis=0))
        back = back_ref[k].astype(jnp.float32)
        first_cols[...] = jnp.where(narrow == row + 1, pltpu.roll(back[:, :128], row + 1, 1), first_cols[...])
        last_cols[...] = jnp.where(narrow == row + 1, pltpu.roll(back[:, cols - 128 :], row + 2, 1), last_cols[...])
        below = jnp.where(lanes == cols - 1, 0.0, pltpu.roll(back, cols - 1, 1))
        above = jnp.where(lanes == 0, 0.0, pltpu.roll(back, 1, 1))
        backs.append(
            jnp.concatenate([below.astype(jnp.bfloat16), back_ref[k], above.astype(jnp.bfloat16)], axis=0)
        )
        class_ref[...] += lax.dot_general(
            error_ref[k], hidden_ref[k], CONTRACT_LAST, preferred_element_type=jnp.float32
        )
    conv_ref[...] += lax.dot_general(
        jnp.concatenate(images, axis=1), jnp.concatenate(backs, axis=1), CONTRACT_LAST,
        preferred_element_type=jnp.float32,
    )

    @pl.when(step == pl.num_programs(0) - 1)
    def _():
        hidden = back_ref.shape[1]
        for side_ref, cells, place in ((left_ref, first_cols, 0), (right_ref, last_cols, 2 * hidden)):
            side = side_ref[-channels:].astype(jnp.float32)
            moved = [pltpu.roll(side, (1 - a) % 128, 1).astype(jnp.bfloat16) for a in range(3)]
            conv_ref[:, pl.ds(place, hidden)] += lax.dot_general(
                jnp.concatenate(moved, axis=0), cells[...].astype(jnp.bfloat16), CONTRACT_LAST,
                preferred_element_type=jnp.float32,
            )
        write_chunks(keep_ref, conv_ref, class_ref, core_ref[0])
        write_chunks(send_ref, conv_ref, class_ref, 1 - core_ref[0])


def feature_kernel(
    up_ref, above_ref, mid_ref, below_ref, down_ref, left_ref, right_ref, taps_ref, out_ref,
    left_sum, right_sum, weights_ref,
):
    out, channels = weights_ref.shape[0] // 3, weights_ref.shape[1] // 3
    cols = mid_ref.shape[2]
    step = pl.program_id(0)

    @pl.when(step == 0)
    def _():
        for b in range(3):
            for a in range(3):
                tap = taps_ref[3 * (2 - a) + (2 - b)]
                weights_ref[out * b : out * (b + 1), channels * a : channels * (a + 1)] = tap
        left_sum[...] = side_sums(left_ref[...], weights_ref[:out])
        right_sum[...] = side_sums(right_ref[...], weights_ref[2 * out :])

    above = jnp.where(step == 0, up_ref[0], above_ref[STEP_ROWS - 1])
    below = jnp.where(step == pl.num_programs(0) - 1, down_ref[0], below_ref[0])
    cells = [above] + [mid_ref[k] for k in range(STEP_ROWS)] + [below]
    lanes = lane_of((out, 128))
    for k in range(STEP_ROWS):
        row = step * STEP_ROWS + k
        parts = jnp.dot(
            weights_ref[...], jnp.concatenate(cells[k : k + 3], axis=0), preferred_element_type=jnp.float32
        )
        before = pltpu.roll(parts[:out], 1, 1)
        after = pltpu.roll(parts[2 * out :], cols - 1, 1)
        left = pltpu.roll(left_sum[...], (128 - row) % 128, 1)
        right = pltpu.roll(right_sum[...], 127 - row, 1)
        before = jnp.concatenate([jnp.where(lanes == 0, left, before[:, :128]), before[:, 128:]], axis=1)
        after = jnp.concatenate([after[:, :-128], jnp.where(lanes == 127, right, after[:, -128:])], axis=1)
        out_ref[k] = (parts[out : 2 * out] + (before + after)).astype(out_ref.dtype)


def in_hbm(*arrays):
    return tuple(pltpu.with_memory_space_constraint(a, pltpu.HBM) for a in arrays)


def whole(array):
    return pl.BlockSpec(array.shape, lambda i: (0,) * array.ndim, pipeline_mode=pl.Buffered(1))


def by_rows(shape):
    return pl.BlockSpec((STEP_ROWS,) + shape[1:], lambda i: (i, 0, 0))


def unit_rows(cells):
    return pass_on(cells[-1:], "row", 1), pass_on(cells[:1], "row", -1)


def unit_cols(cells, up, down):
    edge = jax.ShapeDtypeStruct((cells.shape[1], 128), cells.dtype)
    to_left, to_right = pl.pallas_call(
        unit_edges_kernel, out_shape=(edge, edge), name="unit_edges",
        compiler_params=vmem_of(24),
        cost_estimate=cost_of(1),
    )(up, cells, down)
    return pass_on(to_right, COL, 1), pass_on(to_left, COL, -1)


def row_call(kernel, rows, args, arg_rows, outs, out_rows, scratch, vmem, micros):
    return pl.pallas_call(
        kernel,
        grid=(rows // STEP_ROWS,),
        in_specs=[
            pl.BlockSpec(memory_space=pltpu.SMEM) if a.ndim == 1 else by_rows(a.shape) if split else whole(a)
            for a, split in zip(args, arg_rows)
        ],
        out_specs=tuple(by_rows(o.shape) if split else whole(o) for o, split in zip(outs, out_rows)),
        out_shape=tuple(outs),
        scratch_shapes=scratch,
        compiler_params=vmem_of(vmem),
        cost_estimate=cost_of(micros),
    )(*args)


def local_step(teacher_feats, teacher_probs, student_feats, conv_weight, class_weight):
    channels, rows, cols = student_feats.shape
    hidden_size, classes = class_weight.shape
    pixel_count = float(rows * cols)
    student = student_feats.transpose(1, 0, 2)
    f32, bf16 = jnp.float32, jnp.bfloat16
    mid, up, down = share_rows(teacher_feats, teacher_probs, student)
    pre_act, stacked = row_call(
        convolve_kernel, rows, (student, conv_weight), [False] * 2,
        [
            jax.ShapeDtypeStruct((rows, hidden_size, cols), f32),
            jax.ShapeDtypeStruct((3 * hidden_size, 3 * channels), bf16),
        ],
        [True, False], [pltpu.VMEM((rows + 2, channels, cols), bf16)], 24, 9,
    )
    left, right = share_cols(mid, up, down, student)
    halo = (up, student, down, left, right)
    current, weights = refine(mid, up, down, left, right, teacher_feats.shape[0], classes)
    current_rows = pass_on(current[rows - EDGE_ROWS :], "row", 1), pass_on(current[:EDGE_ROWS], "row", -1)
    slope, hidden, guess = row_call(
        functools.partial(activate_kernel, skip=mid.shape[1]), rows,
        (up, down, left, right, stacked, class_weight.T, pre_act), [False] * 6 + [True],
        [
            jax.ShapeDtypeStruct((rows, hidden_size, cols), f32),
            jax.ShapeDtypeStruct((rows, hidden_size, cols), bf16),
            jax.ShapeDtypeStruct((rows, classes, cols), f32),
        ],
        [True] * 3,
        [pltpu.VMEM((hidden_size, 128), f32)] * 2 + [pltpu.VMEM((2, hidden_size, cols), f32)], 24, 7,
    )
    refined = finish(current, weights, cols, *current_rows)
    back, error = row_call(
        back_kernel, rows, (guess, refined, slope, class_weight), [True, True, True, False],
        [
            jax.ShapeDtypeStruct((rows, hidden_size, cols), bf16),
            jax.ShapeDtypeStruct((rows, classes, cols), bf16),
        ],
        [True] * 2, [], 24, 2,
    )
    back_up, back_down = unit_rows(back)
    core = lax.axis_index("core").astype(jnp.int32).reshape(1)
    chunks = jax.ShapeDtypeStruct((size_of(CHIPS), CHUNK_ROWS, 128), f32)
    keep, sent = row_call(
        grads_kernel, rows, (core,) + halo + (back, hidden, error), [False] * 6 + [True] * 3,
        [chunks, chunks], [False] * 2,
        [pltpu.VMEM((rows + 2, channels, cols), bf16)]
        + [pltpu.VMEM((hidden_size, 128), f32)] * 2
        + [pltpu.VMEM((3 * channels, 3 * hidden_size), f32), pltpu.VMEM((classes, hidden_size), f32)], 36, 9,
    )
    back_up, back_down, sent = lax.optimization_barrier((back_up, back_down, sent))
    other = lax.ppermute(sent, "core", PARTNER)
    back_left, back_right = unit_cols(back, back_up, back_down)
    packed = pack_half(keep + other)
    steps = rows // STEP_ROWS
    block = (STEP_ROWS, hidden_size, cols)
    feature_args = in_hbm(back_up, back, back_down) + (back_left, back_right) + in_hbm(conv_weight)
    feature_grad = pl.pallas_call(
        feature_kernel,
        grid=(steps,),
        in_specs=[
            whole(back_up),
            pl.BlockSpec(block, lambda i: (jnp.maximum(i - 1, 0), 0, 0)),
            pl.BlockSpec(block, lambda i: (i, 0, 0)),
            pl.BlockSpec(block, lambda i: (jnp.minimum(i + 1, steps - 1), 0, 0)),
            whole(back_down), whole(back_left), whole(back_right), whole(conv_weight),
        ],
        out_specs=by_rows((rows, channels, cols)),
        out_shape=jax.ShapeDtypeStruct((rows, channels, cols), bf16),
        scratch_shapes=[pltpu.VMEM((channels, 128), f32)] * 2
        + [pltpu.VMEM((3 * channels, 3 * hidden_size), bf16)],
        name="feature",
        compiler_params=vmem_of(24),
        cost_estimate=cost_of(8),
    )(feature_args[0], feature_args[1], feature_args[1], feature_args[1], *feature_args[2:])
    received = lax.all_to_all(packed, CHIPS, split_axis=0, concat_axis=0, tiled=True)
    total = jnp.sum(unpack_half(received), axis=0)
    total, feature_grad = lax.optimization_barrier((total, feature_grad))
    grad_conv, grad_class = gather_all(total, core, conv_weight.shape, class_weight.shape, 1.0 / pixel_count)
    return (refined.transpose(1, 0, 2), feature_grad.transpose(1, 0, 2), grad_conv, grad_class)


def solution(mesh):
    devices = mesh.devices
    mesh = Mesh(devices.reshape(devices.shape[0], -1, 2), ("row",) + COL)
    split = P(None, "row", COL)
    in_specs = (split, split, split, P(), P())
    out_specs = (split, split, P(), P())
    return jax.shard_map(local_step, mesh=mesh, in_specs=in_specs, out_specs=out_specs, check_vma=False)
```

```python
import functools
import math

import jax
import jax.numpy as jnp
from jax import lax
from jax.experimental import pallas as pl
from jax.experimental.pallas import tpu as pltpu
from jax.sharding import Mesh
from jax.sharding import PartitionSpec as P


EDGE_ROWS = 8
EDGE_COLS = 16
SPAN = 384
GROUP = 4
PAIR_TAPS = [tap for s in (1, 2, 4) for tap in ((0, s), (s, -s), (s, 0), (s, s))]


def shifted_by(cells, off_x):
    return cells if off_x == 0 else pltpu.roll(cells, (-off_x) % cells.shape[-1], cells.ndim - 1)


def vmem_of(mib):
    return pltpu.CompilerParams(vmem_limit_bytes=mib * 2**20)


def cost_of(micros):
    return pl.CostEstimate(flops=int(micros * 1e9), transcendentals=0, bytes_accessed=int(micros * 3e6))


def lane_of(shape):
    return lax.broadcasted_iota(jnp.int32, shape, len(shape) - 1)


def packed_row(ref, skip):
    return jnp.concatenate([ref[i, skip:, :] for i in range(EDGE_ROWS)], axis=0)


def edges_kernel(up_ref, mid_ref, down_ref, student_ref, left_ref, right_ref):
    rows, channels, _ = mid_ref.shape
    group = lane_of((channels, 128)) // EDGE_COLS
    groups = rows // 8 + 2
    for g in range(groups):
        source = up_ref if g == 0 else down_ref if g == groups - 1 else mid_ref.at[pl.ds(8 * (g - 1), 8)]
        left = jnp.zeros((channels, 128), jnp.float32)
        right = jnp.zeros((channels, 128), jnp.float32)
        for i in range(8):
            first = source[i, :channels, :128].astype(jnp.float32)
            last = source[i, :channels, -128:].astype(jnp.float32)
            left = jnp.where(group == i, pltpu.roll(first, EDGE_COLS * i, 1), left)
            right = jnp.where(group == i, pltpu.roll(last, (EDGE_COLS * (i + 1)) % 128, 1), right)
        left_ref[channels * g : channels * (g + 1)] = left.astype(left_ref.dtype)
        right_ref[channels * g : channels * (g + 1)] = right.astype(right_ref.dtype)
    up, down = packed_row(up_ref, channels), packed_row(down_ref, channels)
    left, right = border_cells([up] + [student_ref.at[i] for i in range(rows)] + [down], student_ref.shape[1:])
    left_ref[channels * groups :] = left.astype(left_ref.dtype)
    right_ref[channels * groups :] = right.astype(right_ref.dtype)


def border_cells(sources, shape):
    channels, cols = shape
    lanes = lane_of((channels, 128))
    left = jnp.zeros((channels, 128), jnp.float32)
    right = jnp.zeros((channels, 128), jnp.float32)
    for i, source in enumerate(sources):
        first = source[:, :128].astype(jnp.float32)
        last = source[:, cols - 128 :].astype(jnp.float32)
        left = jnp.where(lanes == i, pltpu.roll(first, i, 1), left)
        right = jnp.where(lanes == i, pltpu.roll(last, i + 1, 1), right)
    return left, right


def sweep_row(weights, center_row, read_row):
    total = weights(0) * read_row(center_row)
    for index, (off_y, off_x) in enumerate(PAIR_TAPS):
        total += weights(1 + index) * shifted_by(read_row(center_row + off_y), off_x)
        total += weights(13 + index) * shifted_by(read_row(center_row - off_y), -off_x)
    return total


def affinity_kernel(
    place_ref, up_ref, mid_ref, down_ref, left_ref, right_ref, current_ref, weights_ref,
    feats, probs, next_probs, pairs, squares, *, full_rows, full_cols, feat_channels, classes,
):
    rows = mid_ref.shape[0]
    cols = mid_ref.shape[2]
    tall = rows + 2 * EDGE_ROWS
    channels = mid_ref.shape[1]
    lanes = lane_of((channels, 128))

    def gather(i, carry):
        for g in range(tall // 8):
            if g == 0:
                body = up_ref[i, :channels]
            elif g == tall // 8 - 1:
                body = down_ref[i, :channels]
            else:
                body = mid_ref[8 * (g - 1) + i]
            from_right = pltpu.roll(right_ref[channels * g : channels * (g + 1)].astype(jnp.float32), (128 - EDGE_COLS * i) % 128, 1)
            from_left = pltpu.roll(left_ref[channels * g : channels * (g + 1)].astype(jnp.float32), (240 - EDGE_COLS * i) % 128, 1)
            side = jnp.where(lanes < EDGE_COLS, from_right, jnp.where(lanes >= 128 - EDGE_COLS, from_left, 0.0))
            body = body.astype(jnp.float32)
            row = 8 * g + i
            high, low = feat_channels, feat_channels + classes
            feats[row, :, :cols] = body[:high]
            feats[row, :, cols:] = side[:high]
            probs[row, :, :cols] = body[high:low] + body[low:]
            probs[row, :, cols:] = side[high:low] + side[low:]
        return carry

    lax.fori_loop(0, 8, gather, 0)
    pairs[:, tall - 8 :, :] = jnp.zeros((len(PAIR_TAPS), 8, SPAN), jnp.float32)

    for ring, radius in enumerate((1, 2, 4)):

        def products(step, carry, ring=ring, radius=radius):
            rows_at = [step * GROUP + g for g in range(GROUP)]
            sums = [[None] * 4 for _ in rows_at]
            for c in range(feat_channels // 8):
                for g, row in enumerate(rows_at):
                    here = feats[row, 8 * c : 8 * c + 8, :]
                    there = feats[row + radius, 8 * c : 8 * c + 8, :]
                    for k, (off_y, off_x) in enumerate(PAIR_TAPS[4 * ring : 4 * ring + 4]):
                        product = here * shifted_by(there if off_y else here, off_x)
                        sums[g][k] = product if c == 0 else sums[g][k] + product
            totals = [[jnp.sum(cells, axis=0, keepdims=True) for cells in row_sums] for row_sums in sums]
            for g, row in enumerate(rows_at):
                for k in range(4):
                    pairs[4 * ring + k, pl.ds(row, 1), :] = totals[g][k]
            return carry

        lax.fori_loop(0, (tall - 4) // GROUP, products, 0)

    def sizes(row, carry):
        cells = feats[row]
        squares[pl.ds(row, 1), :] = jnp.sum(cells * cells, axis=0, keepdims=True)
        return carry

    lax.fori_loop(0, tall, sizes, 0, unroll=4)
    squares[tall:, :] = jnp.zeros((8, SPAN), jnp.float32)

    shape = (tall, SPAN)
    lane = lane_of(shape)
    row_at = place_ref[0] - EDGE_ROWS + lax.broadcasted_iota(jnp.int32, shape, 0)
    col_at = place_ref[1] + jnp.where(lane < cols + EDGE_COLS, lane, lane - SPAN)

    def inside(off_y, off_x):
        y, x = row_at + off_y, col_at + off_x
        return (y >= 0) & (y < full_rows) & (x >= 0) & (x < full_cols)

    here_inside = inside(0, 0)
    for index, (off_y, off_x) in enumerate(PAIR_TAPS):
        present = here_inside & inside(off_y, off_x)
        both = squares[:tall, :] + shifted_by(squares[off_y : off_y + tall, :], off_x)
        distance = jnp.maximum(both - 2.0 * pairs[index], 0.0)
        pairs[index] = jnp.where(present, jnp.exp(distance * (-1.0 / feat_channels)), 0.0)
    wide = rows + EDGE_ROWS
    total = jnp.ones((wide, SPAN), jnp.float32)
    for index, (off_y, off_x) in enumerate(PAIR_TAPS):
        ahead = pairs[index, 4 : 4 + wide, :]
        behind = shifted_by(pairs[index, 4 - off_y : 4 - off_y + wide, :], -off_x)
        weights_ref[1 + index] = ahead
        weights_ref[13 + index] = behind
        total = total + (ahead + behind)
    scale = 1.0 / total
    weights_ref[0] = scale
    for index in range(1, 25):
        weights_ref[index] = weights_ref[index] * scale
    two_sweeps(weights_ref, lambda row: probs[row], next_probs, current_ref, rows)


def two_sweeps(weights_ref, read_row, middle, out_ref, rows):
    def first(row, carry):
        middle[row] = sweep_row(lambda o: weights_ref[o, pl.ds(row, 1), :], row + 4, read_row)
        return carry

    lax.fori_loop(0, rows + 8, first, 0, unroll=8)

    def second(row, carry):
        value = sweep_row(lambda o: weights_ref[o, pl.ds(row + 4, 1), :], row + 4, lambda r: middle[r])
        out_ref[row] = value[:, : out_ref.shape[2]]
        return carry

    lax.fori_loop(0, rows, second, 0, unroll=8)


def finish_kernel(weights_ref, up_ref, mid_ref, down_ref, out_ref, probs, next_probs):
    rows = mid_ref.shape[0]
    probs[:EDGE_ROWS] = up_ref[...]
    probs[EDGE_ROWS : EDGE_ROWS + rows] = mid_ref[...]
    probs[EDGE_ROWS + rows :] = down_ref[...]
    two_sweeps(weights_ref, lambda row: probs[row], next_probs, out_ref, rows)


COL = ("pair", "core")


def size_of(axes):
    return math.prod(lax.axis_size(a) for a in axes) if isinstance(axes, tuple) else lax.axis_size(axes)


def pass_on(cells, axis, step):
    ends = size_of(axis) - 1
    if step > 0:
        return lax.ppermute(cells, axis, [(i, i + 1) for i in range(ends)])
    return lax.ppermute(cells, axis, [(i + 1, i) for i in range(ends)])


def share_rows(teacher_feats, teacher_probs, student):
    rows = teacher_feats.shape[1]
    high = lax.reduce_precision(teacher_probs, 8, 7)
    low = teacher_probs - high
    mid = jnp.concatenate(
        [teacher_feats, high.astype(jnp.bfloat16), low.astype(jnp.bfloat16)], axis=0
    ).transpose(1, 0, 2)

    def message(first, row):
        return jnp.concatenate(
            [mid[first : first + EDGE_ROWS], student[row].reshape(EDGE_ROWS, -1, student.shape[2])], axis=1
        )

    up = pass_on(message(rows - EDGE_ROWS, rows - 1), "row", 1)
    down = pass_on(message(0, 0), "row", -1)
    return mid, up, down


def share_cols(mid, up, down, student):
    rows, channels, _ = mid.shape
    groups = rows // 8 + 2
    edge = jax.ShapeDtypeStruct((groups * channels + student.shape[1], 128), jnp.bfloat16)
    to_left, to_right = pl.pallas_call(
        edges_kernel, out_shape=(edge, edge), name="edges", compiler_params=vmem_of(16), cost_estimate=cost_of(2)
    )(up, mid, down, student)
    return pass_on(to_right, COL, 1), pass_on(to_left, COL, -1)


def refine(mid, up, down, left, right, feat_channels, classes):
    rows, _, cols = mid.shape
    place = jnp.stack([lax.axis_index("row") * rows, lax.axis_index(COL) * cols]).astype(jnp.int32)
    tall = rows + 2 * EDGE_ROWS
    vmem = pl.BlockSpec(memory_space=pltpu.VMEM)
    current, weights = pl.pallas_call(
        functools.partial(
            affinity_kernel,
            full_rows=rows * lax.axis_size("row"),
            full_cols=cols * size_of(COL),
            feat_channels=feat_channels,
            classes=classes,
        ),
        out_shape=(
            jax.ShapeDtypeStruct((rows, classes, SPAN), jnp.float32),
            jax.ShapeDtypeStruct((25, rows + EDGE_ROWS, SPAN), jnp.float32),
        ),
        in_specs=[pl.BlockSpec(memory_space=pltpu.SMEM)] + [vmem] * 5,
        out_specs=(vmem, vmem),
        scratch_shapes=[
            pltpu.VMEM((tall, feat_channels, SPAN), jnp.float32),
            pltpu.VMEM((tall, classes, SPAN), jnp.float32),
            pltpu.VMEM((rows + 8, classes, SPAN), jnp.float32),
            pltpu.VMEM((len(PAIR_TAPS), tall, SPAN), jnp.float32),
            pltpu.VMEM((tall + 8, SPAN), jnp.float32),
        ],
        name="affinity",
        compiler_params=vmem_of(20),
        cost_estimate=cost_of(12),
    )(place, *in_hbm(up, mid, down), left, right)
    return current, weights


def finish(current, weights, cols, up, down):
    rows, classes, _ = current.shape
    tall = rows + 2 * EDGE_ROWS
    refined = pl.pallas_call(
        finish_kernel,
        out_shape=jax.ShapeDtypeStruct((rows, classes, cols), jnp.float32),
        scratch_shapes=[
            pltpu.VMEM((tall, classes, SPAN), jnp.float32),
            pltpu.VMEM((rows + 8, classes, SPAN), jnp.float32),
        ],
        name="finish",
        compiler_params=vmem_of(12),
        cost_estimate=cost_of(4),
    )(weights, up, current, down)
    return refined


CHIPS = ("row", "pair")
PARTNER = [(0, 1), (1, 0)]
CLASS_ROW = 36
MARK_ROW = 37
CHUNK_ROWS = 40


def tile_places(n_tiles, chips):
    full = n_tiles // chips
    for tile in range(n_tiles):
        if tile < full * chips:
            yield tile, 0, 8, tile // full, 8 * (tile % full)
        else:
            share = 8 * (n_tiles - full * chips) // chips
            for part in range(8 // share):
                chip = (tile - full * chips) * (8 // share) + part
                yield tile, part * share, share, chip, 8 * full


def write_chunks(chunk_ref, conv_ref, class_ref, half):
    height, width = conv_ref.shape[0] // 2, conv_ref.shape[1]
    chips = chunk_ref.shape[0]
    first = pl.multiple_of(half * height, height)
    chunk_ref[:, CLASS_ROW:, :] = jnp.zeros((chips, CHUNK_ROWS - CLASS_ROW, 128), jnp.float32)
    for tile, skip, count, chip, row in tile_places(height * width // 1024, chips):
        block, lane = tile // (width // 128), tile % (width // 128)
        rows = conv_ref[pl.ds(pl.multiple_of(first + 8 * block, 8), 8), 128 * lane : 128 * (lane + 1)]
        chunk_ref[chip, row : row + count, :] = rows[skip : skip + count]
    sums = jnp.where(half == 0, class_ref[:, :128], class_ref[:, 128:])
    for k in range(class_ref.shape[0]):
        chunk_ref[k, CLASS_ROW : CLASS_ROW + 1, :] = sums[k : k + 1]


def read_chunks(core_ref, own_ref, other_ref, conv_ref, class_ref, *, scale):
    _, channels, hidden = conv_ref.shape
    width = 3 * hidden
    chips = own_ref.shape[0]
    for half in range(2):
        mine = core_ref[0] == half
        for tile, skip, count, chip, row in tile_places(3 * channels * width // 2048, chips):
            block, lane = tile // (width // 128), tile % (width // 128)
            top = half * 3 * channels // 2 + 8 * block
            a, b = top // channels, 128 * lane // hidden
            value = jnp.where(mine, own_ref[chip, row : row + count, :], other_ref[chip, row : row + count, :])
            conv_ref[
                3 * a + b, top % channels + skip : top % channels + skip + count,
                128 * lane % hidden : 128 * lane % hidden + 128,
            ] = value * scale
        for k in range(class_ref.shape[0]):
            value = jnp.where(
                mine, own_ref[k, CLASS_ROW : CLASS_ROW + 1, :], other_ref[k, CLASS_ROW : CLASS_ROW + 1, :]
            )
            class_ref[k : k + 1, 128 * half : 128 * (half + 1)] = value * scale


def pack_half(values):
    marks = lax.broadcasted_iota(jnp.int32, values.shape, values.ndim - 2) == MARK_ROW
    largest = jnp.max(jnp.where(marks, 0.0, jnp.abs(values)), axis=-2, keepdims=True)
    exponent = jnp.clip(jnp.ceil(jnp.log2(jnp.maximum(largest, 1e-30))), -100.0, 120.0)
    return jnp.where(marks, exponent, values * jnp.exp2(14.0 - exponent)).astype(jnp.float16)


def unpack_half(packed):
    exponent = packed[..., MARK_ROW : MARK_ROW + 1, :].astype(jnp.float32)
    return packed.astype(jnp.float32) * jnp.exp2(exponent - 14.0)


def gather_all(total, core, conv_shape, class_shape, scale):
    mine = pack_half(total)
    spread = jnp.broadcast_to(mine[None], (size_of(CHIPS),) + mine.shape)
    own = lax.all_to_all(spread, CHIPS, split_axis=0, concat_axis=0, tiled=True)
    other = lax.ppermute(own, "core", PARTNER)
    vmem = pl.BlockSpec(memory_space=pltpu.VMEM)
    conv, small = pl.pallas_call(
        functools.partial(read_chunks, scale=scale),
        out_shape=(
            jax.ShapeDtypeStruct(conv_shape, jnp.float32),
            jax.ShapeDtypeStruct(class_shape[::-1], jnp.float32),
        ),
        in_specs=[pl.BlockSpec(memory_space=pltpu.SMEM), vmem, vmem],
        out_specs=(vmem, vmem),
        name="place",
        compiler_params=vmem_of(12),
        cost_estimate=cost_of(2),
    )(core, unpack_half(own), unpack_half(other))
    return conv, small.T


def unit_edges_kernel(up_ref, mid_ref, down_ref, left_ref, right_ref):
    sources = [up_ref.at[0]] + [mid_ref.at[i] for i in range(mid_ref.shape[0])] + [down_ref.at[0]]
    left, right = border_cells(sources, mid_ref.shape[1:])
    left_ref[...] = left.astype(left_ref.dtype)
    right_ref[...] = right.astype(right_ref.dtype)


def side_sums(side, weights):
    side = side.astype(jnp.float32)
    moved = [pltpu.roll(side, (128 - a) % 128, 1).astype(jnp.bfloat16) for a in range(3)]
    return jnp.dot(weights, jnp.concatenate(moved, axis=0), preferred_element_type=jnp.float32)


STEP_ROWS = 4


def joined(parts, out):
    cols = parts.shape[1]
    lanes = lane_of((out, cols))
    before = jnp.where(lanes == 0, 0.0, pltpu.roll(parts[:out], 1, 1))
    after = jnp.where(lanes == cols - 1, 0.0, pltpu.roll(parts[2 * out :], cols - 1, 1))
    return parts[out : 2 * out] + (before + after)


def convolve_kernel(mid_ref, taps_ref, pre_ref, weights_ref, padded):
    rows, channels, cols = mid_ref.shape
    out = weights_ref.shape[0] // 3

    @pl.when(pl.program_id(0) == 0)
    def _():
        for b in range(3):
            for a in range(3):
                weights_ref[out * b : out * (b + 1), channels * a : channels * (a + 1)] = taps_ref[3 * a + b].T
        padded[0] = jnp.zeros((channels, cols), padded.dtype)
        padded[pl.ds(1, rows)] = mid_ref[...]
        padded[rows + 1] = jnp.zeros((channels, cols), padded.dtype)

    for k in range(STEP_ROWS):
        row = pl.program_id(0) * STEP_ROWS + k
        stack = jnp.concatenate([padded[row], padded[row + 1], padded[row + 2]], axis=0)
        pre_ref[k] = joined(jnp.dot(weights_ref[...], stack, preferred_element_type=jnp.float32), out)


def activate_kernel(
    up_ref, down_ref, left_ref, right_ref, weights_ref, class_ref, pre_ref,
    slope_ref, hidden_ref, guess_ref, left_sum, right_sum, borders, *, skip,
):
    out, channels = weights_ref.shape[0] // 3, weights_ref.shape[1] // 3
    step = pl.program_id(0)

    @pl.when(step == 0)
    def _():
        left_sum[...] = side_sums(left_ref[-channels:], weights_ref[:out])
        right_sum[...] = side_sums(right_ref[-channels:], weights_ref[2 * out :])
        for index, ref in enumerate((up_ref, down_ref)):
            taps = weights_ref[:, 2 * channels * index : 2 * channels * index + channels]
            parts = jnp.dot(taps, packed_row(ref, skip), preferred_element_type=jnp.float32)
            borders[index] = joined(parts, out)

    lanes = lane_of((out, 128))
    for k in range(STEP_ROWS):
        row = step * STEP_ROWS + k
        left = jnp.where(lanes == 0, pltpu.roll(left_sum[...], (128 - row) % 128, 1), 0.0)
        right = jnp.where(lanes == 127, pltpu.roll(right_sum[...], 127 - row, 1), 0.0)
        pre_act = pre_ref[k]
        pre_act = jnp.concatenate([pre_act[:, :128] + left, pre_act[:, 128:] + right], axis=1)
        if k == 0:
            pre_act = pre_act + jnp.where(step == 0, borders[0], 0.0)
        if k == STEP_ROWS - 1:
            pre_act = pre_act + jnp.where(step == pl.num_programs(0) - 1, borders[1], 0.0)
        logistic = 0.5 * jnp.tanh(0.5 * pre_act) + 0.5
        silu = pre_act * logistic
        slope_ref[k] = logistic + silu * (1.0 - logistic)
        hidden = silu.astype(jnp.bfloat16)
        hidden_ref[k] = hidden
        logit = jnp.dot(class_ref[...], hidden, preferred_element_type=jnp.float32)
        guess_ref[k] = 0.5 * jnp.tanh(0.5 * logit) + 0.5


def back_kernel(guess_ref, refined_ref, slope_ref, class_ref, back_ref, error_ref):
    for k in range(STEP_ROWS):
        error = (guess_ref[k] - refined_ref[k]).astype(jnp.bfloat16)
        error_ref[k] = error
        summed = jnp.dot(class_ref[...], error, preferred_element_type=jnp.float32)
        back_ref[k] = (summed * slope_ref[k]).astype(jnp.bfloat16)


CONTRACT_LAST = (((1,), (1,)), ((), ()))


def grads_kernel(
    core_ref, up_ref, mid_ref, down_ref, left_ref, right_ref, back_ref, hidden_ref, error_ref,
    keep_ref, send_ref, padded, first_cols, last_cols, conv_ref, class_ref,
):
    rows, channels, cols = mid_ref.shape
    step = pl.program_id(0)

    @pl.when(step == 0)
    def _():
        padded[0] = packed_row(up_ref, up_ref.shape[1] - channels // EDGE_ROWS)
        padded[pl.ds(1, rows)] = mid_ref[...]
        padded[rows + 1] = packed_row(down_ref, down_ref.shape[1] - channels // EDGE_ROWS)
        conv_ref[...] = jnp.zeros(conv_ref.shape, jnp.float32)
        class_ref[...] = jnp.zeros(class_ref.shape, jnp.float32)
        first_cols[...] = jnp.zeros(first_cols.shape, jnp.float32)
        last_cols[...] = jnp.zeros(last_cols.shape, jnp.float32)

    lanes = lane_of((back_ref.shape[1], cols))
    narrow = lane_of((back_ref.shape[1], 128))
    images, backs = [], []
    for k in range(STEP_ROWS):
        row = step * STEP_ROWS + k
        images.append(jnp.concatenate([padded[row], padded[row + 1], padded[row + 2]], axis=0))
        back = back_ref[k].astype(jnp.float32)
        first_cols[...] = jnp.where(narrow == row + 1, pltpu.roll(back[:, :128], row + 1, 1), first_cols[...])
        last_cols[...] = jnp.where(narrow == row + 1, pltpu.roll(back[:, cols - 128 :], row + 2, 1), last_cols[...])
        below = jnp.where(lanes == cols - 1, 0.0, pltpu.roll(back, cols - 1, 1))
        above = jnp.where(lanes == 0, 0.0, pltpu.roll(back, 1, 1))
        backs.append(
            jnp.concatenate([below.astype(jnp.bfloat16), back_ref[k], above.astype(jnp.bfloat16)], axis=0)
        )
        class_ref[...] += lax.dot_general(
            error_ref[k], hidden_ref[k], CONTRACT_LAST, preferred_element_type=jnp.float32
        )
    conv_ref[...] += lax.dot_general(
        jnp.concatenate(images, axis=1), jnp.concatenate(backs, axis=1), CONTRACT_LAST,
        preferred_element_type=jnp.float32,
    )

    @pl.when(step == pl.num_programs(0) - 1)
    def _():
        hidden = back_ref.shape[1]
        for side_ref, cells, place in ((left_ref, first_cols, 0), (right_ref, last_cols, 2 * hidden)):
            side = side_ref[-channels:].astype(jnp.float32)
            moved = [pltpu.roll(side, (1 - a) % 128, 1).astype(jnp.bfloat16) for a in range(3)]
            conv_ref[:, pl.ds(place, hidden)] += lax.dot_general(
                jnp.concatenate(moved, axis=0), cells[...].astype(jnp.bfloat16), CONTRACT_LAST,
                preferred_element_type=jnp.float32,
            )
        write_chunks(keep_ref, conv_ref, class_ref, core_ref[0])
        write_chunks(send_ref, conv_ref, class_ref, 1 - core_ref[0])


def feature_kernel(
    up_ref, above_ref, mid_ref, below_ref, down_ref, left_ref, right_ref, taps_ref, out_ref,
    left_sum, right_sum, weights_ref,
):
    out, channels = weights_ref.shape[0] // 3, weights_ref.shape[1] // 3
    cols = mid_ref.shape[2]
    step = pl.program_id(0)

    @pl.when(step == 0)
    def _():
        for b in range(3):
            for a in range(3):
                tap = taps_ref[3 * (2 - a) + (2 - b)]
                weights_ref[out * b : out * (b + 1), channels * a : channels * (a + 1)] = tap
        left_sum[...] = side_sums(left_ref[...], weights_ref[:out])
        right_sum[...] = side_sums(right_ref[...], weights_ref[2 * out :])

    above = jnp.where(step == 0, up_ref[0], above_ref[STEP_ROWS - 1])
    below = jnp.where(step == pl.num_programs(0) - 1, down_ref[0], below_ref[0])
    cells = [above] + [mid_ref[k] for k in range(STEP_ROWS)] + [below]
    lanes = lane_of((out, 128))
    for k in range(STEP_ROWS):
        row = step * STEP_ROWS + k
        parts = jnp.dot(
            weights_ref[...], jnp.concatenate(cells[k : k + 3], axis=0), preferred_element_type=jnp.float32
        )
        before = pltpu.roll(parts[:out], 1, 1)
        after = pltpu.roll(parts[2 * out :], cols - 1, 1)
        left = pltpu.roll(left_sum[...], (128 - row) % 128, 1)
        right = pltpu.roll(right_sum[...], 127 - row, 1)
        before = jnp.concatenate([jnp.where(lanes == 0, left, before[:, :128]), before[:, 128:]], axis=1)
        after = jnp.concatenate([after[:, :-128], jnp.where(lanes == 127, right, after[:, -128:])], axis=1)
        out_ref[k] = (parts[out : 2 * out] + (before + after)).astype(out_ref.dtype)


def in_hbm(*arrays):
    return tuple(pltpu.with_memory_space_constraint(a, pltpu.HBM) for a in arrays)


def whole(array):
    return pl.BlockSpec(array.shape, lambda i: (0,) * array.ndim, pipeline_mode=pl.Buffered(1))


def by_rows(shape):
    return pl.BlockSpec((STEP_ROWS,) + shape[1:], lambda i: (i, 0, 0))


def unit_rows(cells):
    return pass_on(cells[-1:], "row", 1), pass_on(cells[:1], "row", -1)


def unit_cols(cells, up, down):
    edge = jax.ShapeDtypeStruct((cells.shape[1], 128), cells.dtype)
    to_left, to_right = pl.pallas_call(
        unit_edges_kernel, out_shape=(edge, edge), name="unit_edges",
        compiler_params=vmem_of(24),
        cost_estimate=cost_of(1),
    )(up, cells, down)
    return pass_on(to_right, COL, 1), pass_on(to_left, COL, -1)


def row_call(kernel, rows, args, arg_rows, outs, out_rows, scratch, vmem, micros):
    return pl.pallas_call(
        kernel,
        grid=(rows // STEP_ROWS,),
        in_specs=[
            pl.BlockSpec(memory_space=pltpu.SMEM) if a.ndim == 1 else by_rows(a.shape) if split else whole(a)
            for a, split in zip(args, arg_rows)
        ],
        out_specs=tuple(by_rows(o.shape) if split else whole(o) for o, split in zip(outs, out_rows)),
        out_shape=tuple(outs),
        scratch_shapes=scratch,
        compiler_params=vmem_of(vmem),
        cost_estimate=cost_of(micros),
    )(*args)


def local_step(teacher_feats, teacher_probs, student_feats, conv_weight, class_weight):
    channels, rows, cols = student_feats.shape
    hidden_size, classes = class_weight.shape
    pixel_count = float(rows * cols)
    student = student_feats.transpose(1, 0, 2)
    f32, bf16 = jnp.float32, jnp.bfloat16
    mid, up, down = share_rows(teacher_feats, teacher_probs, student)
    pre_act, stacked = row_call(
        convolve_kernel, rows, (student, conv_weight), [False] * 2,
        [
            jax.ShapeDtypeStruct((rows, hidden_size, cols), f32),
            jax.ShapeDtypeStruct((3 * hidden_size, 3 * channels), bf16),
        ],
        [True, False], [pltpu.VMEM((rows + 2, channels, cols), bf16)], 24, 9,
    )
    left, right = share_cols(mid, up, down, student)
    halo = (up, student, down, left, right)
    current, weights = refine(mid, up, down, left, right, teacher_feats.shape[0], classes)
    current_rows = pass_on(current[rows - EDGE_ROWS :], "row", 1), pass_on(current[:EDGE_ROWS], "row", -1)
    slope, hidden, guess = row_call(
        functools.partial(activate_kernel, skip=mid.shape[1]), rows,
        (up, down, left, right, stacked, class_weight.T, pre_act), [False] * 6 + [True],
        [
            jax.ShapeDtypeStruct((rows, hidden_size, cols), f32),
            jax.ShapeDtypeStruct((rows, hidden_size, cols), bf16),
            jax.ShapeDtypeStruct((rows, classes, cols), f32),
        ],
        [True] * 3,
        [pltpu.VMEM((hidden_size, 128), f32)] * 2 + [pltpu.VMEM((2, hidden_size, cols), f32)], 24, 7,
    )
    refined = finish(current, weights, cols, *current_rows)
    back, error = row_call(
        back_kernel, rows, (guess, refined, slope, class_weight), [True, True, True, False],
        [
            jax.ShapeDtypeStruct((rows, hidden_size, cols), bf16),
            jax.ShapeDtypeStruct((rows, classes, cols), bf16),
        ],
        [True] * 2, [], 24, 2,
    )
    back_up, back_down = unit_rows(back)
    core = lax.axis_index("core").astype(jnp.int32).reshape(1)
    chunks = jax.ShapeDtypeStruct((size_of(CHIPS), CHUNK_ROWS, 128), f32)
    keep, sent = row_call(
        grads_kernel, rows, (core,) + halo + (back, hidden, error), [False] * 6 + [True] * 3,
        [chunks, chunks], [False] * 2,
        [pltpu.VMEM((rows + 2, channels, cols), bf16)]
        + [pltpu.VMEM((hidden_size, 128), f32)] * 2
        + [pltpu.VMEM((3 * channels, 3 * hidden_size), f32), pltpu.VMEM((classes, hidden_size), f32)], 36, 9,
    )
    back_up, back_down, sent = lax.optimization_barrier((back_up, back_down, sent))
    other = lax.ppermute(sent, "core", PARTNER)
    back_left, back_right = unit_cols(back, back_up, back_down)
    packed = pack_half(keep + other)
    steps = rows // STEP_ROWS
    block = (STEP_ROWS, hidden_size, cols)
    feature_args = in_hbm(back_up, back, back_down) + (back_left, back_right) + in_hbm(conv_weight)
    feature_grad = pl.pallas_call(
        feature_kernel,
        grid=(steps,),
        in_specs=[
            whole(back_up),
            pl.BlockSpec(block, lambda i: (jnp.maximum(i - 1, 0), 0, 0)),
            pl.BlockSpec(block, lambda i: (i, 0, 0)),
            pl.BlockSpec(block, lambda i: (jnp.minimum(i + 1, steps - 1), 0, 0)),
            whole(back_down), whole(back_left), whole(back_right), whole(conv_weight),
        ],
        out_specs=by_rows((rows, channels, cols)),
        out_shape=jax.ShapeDtypeStruct((rows, channels, cols), bf16),
        scratch_shapes=[pltpu.VMEM((channels, 128), f32)] * 2
        + [pltpu.VMEM((3 * channels, 3 * hidden_size), bf16)],
        name="feature",
        compiler_params=vmem_of(24),
        cost_estimate=cost_of(8),
    )(feature_args[0], feature_args[1], feature_args[1], feature_args[1], *feature_args[2:])
    received = lax.all_to_all(packed, CHIPS, split_axis=0, concat_axis=0, tiled=True)
    total = jnp.sum(unpack_half(received), axis=0)
    total, feature_grad = lax.optimization_barrier((total, feature_grad))
    grad_conv, grad_class = gather_all(total, core, conv_weight.shape, class_weight.shape, 1.0 / pixel_count)
    return (refined.transpose(1, 0, 2), feature_grad.transpose(1, 0, 2), grad_conv, grad_class)


def solution(mesh):
    devices = mesh.devices
    mesh = Mesh(devices.reshape(devices.shape[0], -1, 2), ("row",) + COL)
    split = P(None, "row", COL)
    in_specs = (split, split, split, P(), P())
    out_specs = (split, split, P(), P())
    return jax.shard_map(local_step, mesh=mesh, in_specs=in_specs, out_specs=out_specs, check_vma=False)
```

```python
import functools
import math

import jax
import jax.numpy as jnp
from jax import lax
from jax.experimental import pallas as pl
from jax.experimental.pallas import tpu as pltpu
from jax.sharding import Mesh
from jax.sharding import PartitionSpec as P


EDGE_ROWS = 8
EDGE_COLS = 16
SPAN = 384
GROUP = 4
PAIR_TAPS = [tap for s in (1, 2, 4) for tap in ((0, s), (s, -s), (s, 0), (s, s))]


def shifted_by(cells, off_x):
    return cells if off_x == 0 else pltpu.roll(cells, (-off_x) % cells.shape[-1], cells.ndim - 1)


def vmem_of(mib):
    return pltpu.CompilerParams(vmem_limit_bytes=mib * 2**20)


def cost_of(micros):
    return pl.CostEstimate(flops=int(micros * 1e9), transcendentals=0, bytes_accessed=int(micros * 3e6))


def lane_of(shape):
    return lax.broadcasted_iota(jnp.int32, shape, len(shape) - 1)


def packed_row(ref, skip):
    return jnp.concatenate([ref[i, skip:, :] for i in range(EDGE_ROWS)], axis=0)


def edges_kernel(up_ref, mid_ref, down_ref, student_ref, left_ref, right_ref):
    rows, channels, _ = mid_ref.shape
    group = lane_of((channels, 128)) // EDGE_COLS
    groups = rows // 8 + 2
    for g in range(groups):
        source = up_ref if g == 0 else down_ref if g == groups - 1 else mid_ref.at[pl.ds(8 * (g - 1), 8)]
        left = jnp.zeros((channels, 128), jnp.float32)
        right = jnp.zeros((channels, 128), jnp.float32)
        for i in range(8):
            first = source[i, :channels, :128].astype(jnp.float32)
            last = source[i, :channels, -128:].astype(jnp.float32)
            left = jnp.where(group == i, pltpu.roll(first, EDGE_COLS * i, 1), left)
            right = jnp.where(group == i, pltpu.roll(last, (EDGE_COLS * (i + 1)) % 128, 1), right)
        left_ref[channels * g : channels * (g + 1)] = left.astype(left_ref.dtype)
        right_ref[channels * g : channels * (g + 1)] = right.astype(right_ref.dtype)
    up, down = packed_row(up_ref, channels), packed_row(down_ref, channels)
    left, right = border_cells([up] + [student_ref.at[i] for i in range(rows)] + [down], student_ref.shape[1:])
    left_ref[channels * groups :] = left.astype(left_ref.dtype)
    right_ref[channels * groups :] = right.astype(right_ref.dtype)


def border_cells(sources, shape):
    channels, cols = shape
    lanes = lane_of((channels, 128))
    left = jnp.zeros((channels, 128), jnp.float32)
    right = jnp.zeros((channels, 128), jnp.float32)
    for i, source in enumerate(sources):
        first = source[:, :128].astype(jnp.float32)
        last = source[:, cols - 128 :].astype(jnp.float32)
        left = jnp.where(lanes == i, pltpu.roll(first, i, 1), left)
        right = jnp.where(lanes == i, pltpu.roll(last, i + 1, 1), right)
    return left, right


def sweep_row(weights, center_row, read_row):
    total = weights(0) * read_row(center_row)
    for index, (off_y, off_x) in enumerate(PAIR_TAPS):
        total += weights(1 + index) * shifted_by(read_row(center_row + off_y), off_x)
        total += weights(13 + index) * shifted_by(read_row(center_row - off_y), -off_x)
    return total


def affinity_kernel(
    place_ref, up_ref, mid_ref, down_ref, left_ref, right_ref, current_ref, weights_ref,
    feats, probs, next_probs, pairs, squares, *, full_rows, full_cols, feat_channels, classes,
):
    rows = mid_ref.shape[0]
    cols = mid_ref.shape[2]
    tall = rows + 2 * EDGE_ROWS
    channels = mid_ref.shape[1]
    lanes = lane_of((channels, 128))

    def gather(i, carry):
        for g in range(tall // 8):
            if g == 0:
                body = up_ref[i, :channels]
            elif g == tall // 8 - 1:
                body = down_ref[i, :channels]
            else:
                body = mid_ref[8 * (g - 1) + i]
            from_right = pltpu.roll(right_ref[channels * g : channels * (g + 1)].astype(jnp.float32), (128 - EDGE_COLS * i) % 128, 1)
            from_left = pltpu.roll(left_ref[channels * g : channels * (g + 1)].astype(jnp.float32), (240 - EDGE_COLS * i) % 128, 1)
            side = jnp.where(lanes < EDGE_COLS, from_right, jnp.where(lanes >= 128 - EDGE_COLS, from_left, 0.0))
            body = body.astype(jnp.float32)
            row = 8 * g + i
            high, low = feat_channels, feat_channels + classes
            feats[row, :, :cols] = body[:high]
            feats[row, :, cols:] = side[:high]
            probs[row, :, :cols] = body[high:low] + body[low:]
            probs[row, :, cols:] = side[high:low] + side[low:]
        return carry

    lax.fori_loop(0, 8, gather, 0)
    pairs[:, tall - 8 :, :] = jnp.zeros((len(PAIR_TAPS), 8, SPAN), jnp.float32)

    for ring, radius in enumerate((1, 2, 4)):

        def products(step, carry, ring=ring, radius=radius):
            rows_at = [step * GROUP + g for g in range(GROUP)]
            sums = [[None] * 4 for _ in rows_at]
            for c in range(feat_channels // 8):
                for g, row in enumerate(rows_at):
                    here = feats[row, 8 * c : 8 * c + 8, :]
                    there = feats[row + radius, 8 * c : 8 * c + 8, :]
                    for k, (off_y, off_x) in enumerate(PAIR_TAPS[4 * ring : 4 * ring + 4]):
                        product = here * shifted_by(there if off_y else here, off_x)
                        sums[g][k] = product if c == 0 else sums[g][k] + product
            totals = [[jnp.sum(cells, axis=0, keepdims=True) for cells in row_sums] for row_sums in sums]
            for g, row in enumerate(rows_at):
                for k in range(4):
                    pairs[4 * ring + k, pl.ds(row, 1), :] = totals[g][k]
            return carry

        lax.fori_loop(0, (tall - 4) // GROUP, products, 0)

    def sizes(row, carry):
        cells = feats[row]
        squares[pl.ds(row, 1), :] = jnp.sum(cells * cells, axis=0, keepdims=True)
        return carry

    lax.fori_loop(0, tall, sizes, 0, unroll=4)
    squares[tall:, :] = jnp.zeros((8, SPAN), jnp.float32)

    shape = (tall, SPAN)
    lane = lane_of(shape)
    row_at = place_ref[0] - EDGE_ROWS + lax.broadcasted_iota(jnp.int32, shape, 0)
    col_at = place_ref[1] + jnp.where(lane < cols + EDGE_COLS, lane, lane - SPAN)

    def inside(off_y, off_x):
        y, x = row_at + off_y, col_at + off_x
        return (y >= 0) & (y < full_rows) & (x >= 0) & (x < full_cols)

    here_inside = inside(0, 0)
    for index, (off_y, off_x) in enumerate(PAIR_TAPS):
        present = here_inside & inside(off_y, off_x)
        both = squares[:tall, :] + shifted_by(squares[off_y : off_y + tall, :], off_x)
        distance = jnp.maximum(both - 2.0 * pairs[index], 0.0)
        pairs[index] = jnp.where(present, jnp.exp(distance * (-1.0 / feat_channels)), 0.0)
    wide = rows + EDGE_ROWS
    total = jnp.ones((wide, SPAN), jnp.float32)
    for index, (off_y, off_x) in enumerate(PAIR_TAPS):
        ahead = pairs[index, 4 : 4 + wide, :]
        behind = shifted_by(pairs[index, 4 - off_y : 4 - off_y + wide, :], -off_x)
        weights_ref[1 + index] = ahead
        weights_ref[13 + index] = behind
        total = total + (ahead + behind)
    scale = 1.0 / total
    weights_ref[0] = scale
    for index in range(1, 25):
        weights_ref[index] = weights_ref[index] * scale
    two_sweeps(weights_ref, lambda row: probs[row], next_probs, current_ref, rows)


def two_sweeps(weights_ref, read_row, middle, out_ref, rows):
    def first(row, carry):
        middle[row] = sweep_row(lambda o: weights_ref[o, pl.ds(row, 1), :], row + 4, read_row)
        return carry

    lax.fori_loop(0, rows + 8, first, 0, unroll=8)

    def second(row, carry):
        value = sweep_row(lambda o: weights_ref[o, pl.ds(row + 4, 1), :], row + 4, lambda r: middle[r])
        out_ref[row] = value[:, : out_ref.shape[2]]
        return carry

    lax.fori_loop(0, rows, second, 0, unroll=8)


def finish_kernel(weights_ref, up_ref, mid_ref, down_ref, out_ref, probs, next_probs):
    rows = mid_ref.shape[0]
    probs[:EDGE_ROWS] = up_ref[...]
    probs[EDGE_ROWS : EDGE_ROWS + rows] = mid_ref[...]
    probs[EDGE_ROWS + rows :] = down_ref[...]
    two_sweeps(weights_ref, lambda row: probs[row], next_probs, out_ref, rows)


COL = ("pair", "core")


def size_of(axes):
    return math.prod(lax.axis_size(a) for a in axes) if isinstance(axes, tuple) else lax.axis_size(axes)


def pass_on(cells, axis, step):
    ends = size_of(axis) - 1
    if step > 0:
        return lax.ppermute(cells, axis, [(i, i + 1) for i in range(ends)])
    return lax.ppermute(cells, axis, [(i + 1, i) for i in range(ends)])


def share_rows(teacher_feats, teacher_probs, student):
    rows = teacher_feats.shape[1]
    high = lax.reduce_precision(teacher_probs, 8, 7)
    low = teacher_probs - high
    mid = jnp.concatenate(
        [teacher_feats, high.astype(jnp.bfloat16), low.astype(jnp.bfloat16)], axis=0
    ).transpose(1, 0, 2)

    def message(first, row):
        return jnp.concatenate(
            [mid[first : first + EDGE_ROWS], student[row].reshape(EDGE_ROWS, -1, student.shape[2])], axis=1
        )

    up = pass_on(message(rows - EDGE_ROWS, rows - 1), "row", 1)
    down = pass_on(message(0, 0), "row", -1)
    return mid, up, down


def share_cols(mid, up, down, student):
    rows, channels, _ = mid.shape
    groups = rows // 8 + 2
    edge = jax.ShapeDtypeStruct((groups * channels + student.shape[1], 128), jnp.bfloat16)
    to_left, to_right = pl.pallas_call(
        edges_kernel, out_shape=(edge, edge), name="edges", compiler_params=vmem_of(16), cost_estimate=cost_of(2)
    )(up, mid, down, student)
    return pass_on(to_right, COL, 1), pass_on(to_left, COL, -1)


def refine(mid, up, down, left, right, feat_channels, classes):
    rows, _, cols = mid.shape
    place = jnp.stack([lax.axis_index("row") * rows, lax.axis_index(COL) * cols]).astype(jnp.int32)
    tall = rows + 2 * EDGE_ROWS
    vmem = pl.BlockSpec(memory_space=pltpu.VMEM)
    current, weights = pl.pallas_call(
        functools.partial(
            affinity_kernel,
            full_rows=rows * lax.axis_size("row"),
            full_cols=cols * size_of(COL),
            feat_channels=feat_channels,
            classes=classes,
        ),
        out_shape=(
            jax.ShapeDtypeStruct((rows, classes, SPAN), jnp.float32),
            jax.ShapeDtypeStruct((25, rows + EDGE_ROWS, SPAN), jnp.float32),
        ),
        in_specs=[pl.BlockSpec(memory_space=pltpu.SMEM)] + [vmem] * 5,
        out_specs=(vmem, vmem),
        scratch_shapes=[
            pltpu.VMEM((tall, feat_channels, SPAN), jnp.float32),
            pltpu.VMEM((tall, classes, SPAN), jnp.float32),
            pltpu.VMEM((rows + 8, classes, SPAN), jnp.float32),
            pltpu.VMEM((len(PAIR_TAPS), tall, SPAN), jnp.float32),
            pltpu.VMEM((tall + 8, SPAN), jnp.float32),
        ],
        name="affinity",
        compiler_params=vmem_of(20),
        cost_estimate=cost_of(12),
    )(place, *in_hbm(up, mid, down), left, right)
    return current, weights


def finish(current, weights, cols, up, down):
    rows, classes, _ = current.shape
    tall = rows + 2 * EDGE_ROWS
    refined = pl.pallas_call(
        finish_kernel,
        out_shape=jax.ShapeDtypeStruct((rows, classes, cols), jnp.float32),
        scratch_shapes=[
            pltpu.VMEM((tall, classes, SPAN), jnp.float32),
            pltpu.VMEM((rows + 8, classes, SPAN), jnp.float32),
        ],
        name="finish",
        compiler_params=vmem_of(12),
        cost_estimate=cost_of(4),
    )(weights, up, current, down)
    return refined


CHIPS = ("row", "pair")
PARTNER = [(0, 1), (1, 0)]
CLASS_ROW = 36
MARK_ROW = 37
CHUNK_ROWS = 40


def tile_places(n_tiles, chips):
    full = n_tiles // chips
    for tile in range(n_tiles):
        if tile < full * chips:
            yield tile, 0, 8, tile // full, 8 * (tile % full)
        else:
            share = 8 * (n_tiles - full * chips) // chips
            for part in range(8 // share):
                chip = (tile - full * chips) * (8 // share) + part
                yield tile, part * share, share, chip, 8 * full


def write_chunks(chunk_ref, conv_ref, class_ref, half):
    height, width = conv_ref.shape[0] // 2, conv_ref.shape[1]
    chips = chunk_ref.shape[0]
    first = pl.multiple_of(half * height, height)
    chunk_ref[:, CLASS_ROW:, :] = jnp.zeros((chips, CHUNK_ROWS - CLASS_ROW, 128), jnp.float32)
    for tile, skip, count, chip, row in tile_places(height * width // 1024, chips):
        block, lane = tile // (width // 128), tile % (width // 128)
        rows = conv_ref[pl.ds(pl.multiple_of(first + 8 * block, 8), 8), 128 * lane : 128 * (lane + 1)]
        chunk_ref[chip, row : row + count, :] = rows[skip : skip + count]
    sums = jnp.where(half == 0, class_ref[:, :128], class_ref[:, 128:])
    for k in range(class_ref.shape[0]):
        chunk_ref[k, CLASS_ROW : CLASS_ROW + 1, :] = sums[k : k + 1]


def read_chunks(core_ref, own_ref, other_ref, conv_ref, class_ref, *, scale):
    _, channels, hidden = conv_ref.shape
    width = 3 * hidden
    chips = own_ref.shape[0]
    for half in range(2):
        mine = core_ref[0] == half
        for tile, skip, count, chip, row in tile_places(3 * channels * width // 2048, chips):
            block, lane = tile // (width // 128), tile % (width // 128)
            top = half * 3 * channels // 2 + 8 * block
            a, b = top // channels, 128 * lane // hidden
            value = jnp.where(mine, own_ref[chip, row : row + count, :], other_ref[chip, row : row + count, :])
            conv_ref[
                3 * a + b, top % channels + skip : top % channels + skip + count,
                128 * lane % hidden : 128 * lane % hidden + 128,
            ] = value * scale
        for k in range(class_ref.shape[0]):
            value = jnp.where(
                mine, own_ref[k, CLASS_ROW : CLASS_ROW + 1, :], other_ref[k, CLASS_ROW : CLASS_ROW + 1, :]
            )
            class_ref[k : k + 1, 128 * half : 128 * (half + 1)] = value * scale


def pack_half(values):
    marks = lax.broadcasted_iota(jnp.int32, values.shape, values.ndim - 2) == MARK_ROW
    largest = jnp.max(jnp.where(marks, 0.0, jnp.abs(values)), axis=-2, keepdims=True)
    exponent = jnp.clip(jnp.ceil(jnp.log2(jnp.maximum(largest, 1e-30))), -100.0, 120.0)
    return jnp.where(marks, exponent, values * jnp.exp2(14.0 - exponent)).astype(jnp.float16)


def unpack_half(packed):
    exponent = packed[..., MARK_ROW : MARK_ROW + 1, :].astype(jnp.float32)
    return packed.astype(jnp.float32) * jnp.exp2(exponent - 14.0)


def gather_all(total, core, conv_shape, class_shape, scale):
    mine = pack_half(total)
    spread = jnp.broadcast_to(mine[None], (size_of(CHIPS),) + mine.shape)
    own = lax.all_to_all(spread, CHIPS, split_axis=0, concat_axis=0, tiled=True)
    other = lax.ppermute(own, "core", PARTNER)
    vmem = pl.BlockSpec(memory_space=pltpu.VMEM)
    conv, small = pl.pallas_call(
        functools.partial(read_chunks, scale=scale),
        out_shape=(
            jax.ShapeDtypeStruct(conv_shape, jnp.float32),
            jax.ShapeDtypeStruct(class_shape[::-1], jnp.float32),
        ),
        in_specs=[pl.BlockSpec(memory_space=pltpu.SMEM), vmem, vmem],
        out_specs=(vmem, vmem),
        name="place",
        compiler_params=vmem_of(12),
        cost_estimate=cost_of(2),
    )(core, unpack_half(own), unpack_half(other))
    return conv, small.T


def unit_edges_kernel(up_ref, mid_ref, down_ref, left_ref, right_ref):
    sources = [up_ref.at[0]] + [mid_ref.at[i] for i in range(mid_ref.shape[0])] + [down_ref.at[0]]
    left, right = border_cells(sources, mid_ref.shape[1:])
    left_ref[...] = left.astype(left_ref.dtype)
    right_ref[...] = right.astype(right_ref.dtype)


def side_sums(side, weights):
    side = side.astype(jnp.float32)
    moved = [pltpu.roll(side, (128 - a) % 128, 1).astype(jnp.bfloat16) for a in range(3)]
    return jnp.dot(weights, jnp.concatenate(moved, axis=0), preferred_element_type=jnp.float32)


STEP_ROWS = 8


def joined(parts, out):
    cols = parts.shape[1]
    lanes = lane_of((out, cols))
    before = jnp.where(lanes == 0, 0.0, pltpu.roll(parts[:out], 1, 1))
    after = jnp.where(lanes == cols - 1, 0.0, pltpu.roll(parts[2 * out :], cols - 1, 1))
    return parts[out : 2 * out] + (before + after)


def convolve_kernel(mid_ref, taps_ref, pre_ref, weights_ref, padded):
    rows, channels, cols = mid_ref.shape
    out = weights_ref.shape[0] // 3

    @pl.when(pl.program_id(0) == 0)
    def _():
        for b in range(3):
            for a in range(3):
                weights_ref[out * b : out * (b + 1), channels * a : channels * (a + 1)] = taps_ref[3 * a + b].T
        padded[0] = jnp.zeros((channels, cols), padded.dtype)
        padded[pl.ds(1, rows)] = mid_ref[...]
        padded[rows + 1] = jnp.zeros((channels, cols), padded.dtype)

    for k in range(STEP_ROWS):
        row = pl.program_id(0) * STEP_ROWS + k
        stack = jnp.concatenate([padded[row], padded[row + 1], padded[row + 2]], axis=0)
        pre_ref[k] = joined(jnp.dot(weights_ref[...], stack, preferred_element_type=jnp.float32), out)


def activate_kernel(
    up_ref, down_ref, left_ref, right_ref, weights_ref, class_ref, pre_ref,
    slope_ref, hidden_ref, guess_ref, left_sum, right_sum, borders, *, skip,
):
    out, channels = weights_ref.shape[0] // 3, weights_ref.shape[1] // 3
    step = pl.program_id(0)

    @pl.when(step == 0)
    def _():
        left_sum[...] = side_sums(left_ref[-channels:], weights_ref[:out])
        right_sum[...] = side_sums(right_ref[-channels:], weights_ref[2 * out :])
        for index, ref in enumerate((up_ref, down_ref)):
            taps = weights_ref[:, 2 * channels * index : 2 * channels * index + channels]
            parts = jnp.dot(taps, packed_row(ref, skip), preferred_element_type=jnp.float32)
            borders[index] = joined(parts, out)

    lanes = lane_of((out, 128))
    for k in range(STEP_ROWS):
        row = step * STEP_ROWS + k
        left = jnp.where(lanes == 0, pltpu.roll(left_sum[...], (128 - row) % 128, 1), 0.0)
        right = jnp.where(lanes == 127, pltpu.roll(right_sum[...], 127 - row, 1), 0.0)
        pre_act = pre_ref[k]
        pre_act = jnp.concatenate([pre_act[:, :128] + left, pre_act[:, 128:] + right], axis=1)
        if k == 0:
            pre_act = pre_act + jnp.where(step == 0, borders[0], 0.0)
        if k == STEP_ROWS - 1:
            pre_act = pre_act + jnp.where(step == pl.num_programs(0) - 1, borders[1], 0.0)
        logistic = 0.5 * jnp.tanh(0.5 * pre_act) + 0.5
        silu = pre_act * logistic
        slope_ref[k] = logistic + silu * (1.0 - logistic)
        hidden = silu.astype(jnp.bfloat16)
        hidden_ref[k] = hidden
        logit = jnp.dot(class_ref[...], hidden, preferred_element_type=jnp.float32)
        guess_ref[k] = 0.5 * jnp.tanh(0.5 * logit) + 0.5


def back_kernel(guess_ref, refined_ref, slope_ref, class_ref, back_ref, error_ref):
    for k in range(STEP_ROWS):
        error = (guess_ref[k] - refined_ref[k]).astype(jnp.bfloat16)
        error_ref[k] = error
        summed = jnp.dot(class_ref[...], error, preferred_element_type=jnp.float32)
        back_ref[k] = (summed * slope_ref[k]).astype(jnp.bfloat16)


CONTRACT_LAST = (((1,), (1,)), ((), ()))


def grads_kernel(
    core_ref, up_ref, mid_ref, down_ref, left_ref, right_ref, back_ref, hidden_ref, error_ref,
    keep_ref, send_ref, padded, first_cols, last_cols, conv_ref, class_ref,
):
    rows, channels, cols = mid_ref.shape
    step = pl.program_id(0)

    @pl.when(step == 0)
    def _():
        padded[0] = packed_row(up_ref, up_ref.shape[1] - channels // EDGE_ROWS)
        padded[pl.ds(1, rows)] = mid_ref[...]
        padded[rows + 1] = packed_row(down_ref, down_ref.shape[1] - channels // EDGE_ROWS)
        conv_ref[...] = jnp.zeros(conv_ref.shape, jnp.float32)
        class_ref[...] = jnp.zeros(class_ref.shape, jnp.float32)
        first_cols[...] = jnp.zeros(first_cols.shape, jnp.float32)
        last_cols[...] = jnp.zeros(last_cols.shape, jnp.float32)

    lanes = lane_of((back_ref.shape[1], cols))
    narrow = lane_of((back_ref.shape[1], 128))
    images, backs = [], []
    for k in range(STEP_ROWS):
        row = step * STEP_ROWS + k
        images.append(jnp.concatenate([padded[row], padded[row + 1], padded[row + 2]], axis=0))
        back = back_ref[k].astype(jnp.float32)
        first_cols[...] = jnp.where(narrow == row + 1, pltpu.roll(back[:, :128], row + 1, 1), first_cols[...])
        last_cols[...] = jnp.where(narrow == row + 1, pltpu.roll(back[:, cols - 128 :], row + 2, 1), last_cols[...])
        below = jnp.where(lanes == cols - 1, 0.0, pltpu.roll(back, cols - 1, 1))
        above = jnp.where(lanes == 0, 0.0, pltpu.roll(back, 1, 1))
        backs.append(
            jnp.concatenate([below.astype(jnp.bfloat16), back_ref[k], above.astype(jnp.bfloat16)], axis=0)
        )
        class_ref[...] += lax.dot_general(
            error_ref[k], hidden_ref[k], CONTRACT_LAST, preferred_element_type=jnp.float32
        )
    conv_ref[...] += lax.dot_general(
        jnp.concatenate(images, axis=1), jnp.concatenate(backs, axis=1), CONTRACT_LAST,
        preferred_element_type=jnp.float32,
    )

    @pl.when(step == pl.num_programs(0) - 1)
    def _():
        hidden = back_ref.shape[1]
        for side_ref, cells, place in ((left_ref, first_cols, 0), (right_ref, last_cols, 2 * hidden)):
            side = side_ref[-channels:].astype(jnp.float32)
            moved = [pltpu.roll(side, (1 - a) % 128, 1).astype(jnp.bfloat16) for a in range(3)]
            conv_ref[:, pl.ds(place, hidden)] += lax.dot_general(
                jnp.concatenate(moved, axis=0), cells[...].astype(jnp.bfloat16), CONTRACT_LAST,
                preferred_element_type=jnp.float32,
            )
        write_chunks(keep_ref, conv_ref, class_ref, core_ref[0])
        write_chunks(send_ref, conv_ref, class_ref, 1 - core_ref[0])


def feature_kernel(
    up_ref, above_ref, mid_ref, below_ref, down_ref, left_ref, right_ref, taps_ref, out_ref,
    left_sum, right_sum, weights_ref,
):
    out, channels = weights_ref.shape[0] // 3, weights_ref.shape[1] // 3
    cols = mid_ref.shape[2]
    step = pl.program_id(0)

    @pl.when(step == 0)
    def _():
        for b in range(3):
            for a in range(3):
                tap = taps_ref[3 * (2 - a) + (2 - b)]
                weights_ref[out * b : out * (b + 1), channels * a : channels * (a + 1)] = tap
        left_sum[...] = side_sums(left_ref[...], weights_ref[:out])
        right_sum[...] = side_sums(right_ref[...], weights_ref[2 * out :])

    above = jnp.where(step == 0, up_ref[0], above_ref[STEP_ROWS - 1])
    below = jnp.where(step == pl.num_programs(0) - 1, down_ref[0], below_ref[0])
    cells = [above] + [mid_ref[k] for k in range(STEP_ROWS)] + [below]
    lanes = lane_of((out, 128))
    for k in range(STEP_ROWS):
        row = step * STEP_ROWS + k
        parts = jnp.dot(
            weights_ref[...], jnp.concatenate(cells[k : k + 3], axis=0), preferred_element_type=jnp.float32
        )
        before = pltpu.roll(parts[:out], 1, 1)
        after = pltpu.roll(parts[2 * out :], cols - 1, 1)
        left = pltpu.roll(left_sum[...], (128 - row) % 128, 1)
        right = pltpu.roll(right_sum[...], 127 - row, 1)
        before = jnp.concatenate([jnp.where(lanes == 0, left, before[:, :128]), before[:, 128:]], axis=1)
        after = jnp.concatenate([after[:, :-128], jnp.where(lanes == 127, right, after[:, -128:])], axis=1)
        out_ref[k] = (parts[out : 2 * out] + (before + after)).astype(out_ref.dtype)


def in_hbm(*arrays):
    return tuple(pltpu.with_memory_space_constraint(a, pltpu.HBM) for a in arrays)


def whole(array):
    return pl.BlockSpec(array.shape, lambda i: (0,) * array.ndim, pipeline_mode=pl.Buffered(1))


def by_rows(shape):
    return pl.BlockSpec((STEP_ROWS,) + shape[1:], lambda i: (i, 0, 0))


def unit_rows(cells):
    return pass_on(cells[-1:], "row", 1), pass_on(cells[:1], "row", -1)


def unit_cols(cells, up, down):
    edge = jax.ShapeDtypeStruct((cells.shape[1], 128), cells.dtype)
    to_left, to_right = pl.pallas_call(
        unit_edges_kernel, out_shape=(edge, edge), name="unit_edges",
        compiler_params=vmem_of(40),
        cost_estimate=cost_of(1),
    )(up, cells, down)
    return pass_on(to_right, COL, 1), pass_on(to_left, COL, -1)


def row_call(kernel, rows, args, arg_rows, outs, out_rows, scratch, vmem, micros):
    return pl.pallas_call(
        kernel,
        grid=(rows // STEP_ROWS,),
        in_specs=[
            pl.BlockSpec(memory_space=pltpu.SMEM) if a.ndim == 1 else by_rows(a.shape) if split else whole(a)
            for a, split in zip(args, arg_rows)
        ],
        out_specs=tuple(by_rows(o.shape) if split else whole(o) for o, split in zip(outs, out_rows)),
        out_shape=tuple(outs),
        scratch_shapes=scratch,
        compiler_params=vmem_of(vmem),
        cost_estimate=cost_of(micros),
    )(*args)


def local_step(teacher_feats, teacher_probs, student_feats, conv_weight, class_weight):
    channels, rows, cols = student_feats.shape
    hidden_size, classes = class_weight.shape
    pixel_count = float(rows * cols)
    student = student_feats.transpose(1, 0, 2)
    f32, bf16 = jnp.float32, jnp.bfloat16
    mid, up, down = share_rows(teacher_feats, teacher_probs, student)
    pre_act, stacked = row_call(
        convolve_kernel, rows, (student, conv_weight), [False] * 2,
        [
            jax.ShapeDtypeStruct((rows, hidden_size, cols), f32),
            jax.ShapeDtypeStruct((3 * hidden_size, 3 * channels), bf16),
        ],
        [True, False], [pltpu.VMEM((rows + 2, channels, cols), bf16)], 44, 9,
    )
    left, right = share_cols(mid, up, down, student)
    halo = (up, student, down, left, right)
    current, weights = refine(mid, up, down, left, right, teacher_feats.shape[0], classes)
    current_rows = pass_on(current[rows - EDGE_ROWS :], "row", 1), pass_on(current[:EDGE_ROWS], "row", -1)
    slope, hidden, guess = row_call(
        functools.partial(activate_kernel, skip=mid.shape[1]), rows,
        (up, down, left, right, stacked, class_weight.T, pre_act), [False] * 6 + [True],
        [
            jax.ShapeDtypeStruct((rows, hidden_size, cols), f32),
            jax.ShapeDtypeStruct((rows, hidden_size, cols), bf16),
            jax.ShapeDtypeStruct((rows, classes, cols), f32),
        ],
        [True] * 3,
        [pltpu.VMEM((hidden_size, 128), f32)] * 2 + [pltpu.VMEM((2, hidden_size, cols), f32)], 48, 7,
    )
    refined = finish(current, weights, cols, *current_rows)
    back, error = row_call(
        back_kernel, rows, (guess, refined, slope, class_weight), [True, True, True, False],
        [
            jax.ShapeDtypeStruct((rows, hidden_size, cols), bf16),
            jax.ShapeDtypeStruct((rows, classes, cols), bf16),
        ],
        [True] * 2, [], 40, 2,
    )
    back_up, back_down = unit_rows(back)
    core = lax.axis_index("core").astype(jnp.int32).reshape(1)
    chunks = jax.ShapeDtypeStruct((size_of(CHIPS), CHUNK_ROWS, 128), f32)
    keep, sent = row_call(
        grads_kernel, rows, (core,) + halo + (back, hidden, error), [False] * 6 + [True] * 3,
        [chunks, chunks], [False] * 2,
        [pltpu.VMEM((rows + 2, channels, cols), bf16)]
        + [pltpu.VMEM((hidden_size, 128), f32)] * 2
        + [pltpu.VMEM((3 * channels, 3 * hidden_size), f32), pltpu.VMEM((classes, hidden_size), f32)], 56, 9,
    )
    back_up, back_down, sent = lax.optimization_barrier((back_up, back_down, sent))
    other = lax.ppermute(sent, "core", PARTNER)
    back_left, back_right = unit_cols(back, back_up, back_down)
    packed = pack_half(keep + other)
    steps = rows // STEP_ROWS
    block = (STEP_ROWS, hidden_size, cols)
    feature_args = in_hbm(back_up, back, back_down) + (back_left, back_right) + in_hbm(conv_weight)
    feature_grad = pl.pallas_call(
        feature_kernel,
        grid=(steps,),
        in_specs=[
            whole(back_up),
            pl.BlockSpec(block, lambda i: (jnp.maximum(i - 1, 0), 0, 0)),
            pl.BlockSpec(block, lambda i: (i, 0, 0)),
            pl.BlockSpec(block, lambda i: (jnp.minimum(i + 1, steps - 1), 0, 0)),
            whole(back_down), whole(back_left), whole(back_right), whole(conv_weight),
        ],
        out_specs=by_rows((rows, channels, cols)),
        out_shape=jax.ShapeDtypeStruct((rows, channels, cols), bf16),
        scratch_shapes=[pltpu.VMEM((channels, 128), f32)] * 2
        + [pltpu.VMEM((3 * channels, 3 * hidden_size), bf16)],
        name="feature",
        compiler_params=vmem_of(40),
        cost_estimate=cost_of(8),
    )(feature_args[0], feature_args[1], feature_args[1], feature_args[1], *feature_args[2:])
    received = lax.all_to_all(packed, CHIPS, split_axis=0, concat_axis=0, tiled=True)
    total = jnp.sum(unpack_half(received), axis=0)
    total, feature_grad = lax.optimization_barrier((total, feature_grad))
    grad_conv, grad_class = gather_all(total, core, conv_weight.shape, class_weight.shape, 1.0 / pixel_count)
    return (refined.transpose(1, 0, 2), feature_grad.transpose(1, 0, 2), grad_conv, grad_class)


def solution(mesh):
    devices = mesh.devices
    mesh = Mesh(devices.reshape(devices.shape[0], -1, 2), ("row",) + COL)
    split = P(None, "row", COL)
    in_specs = (split, split, split, P(), P())
    out_specs = (split, split, P(), P())
    return jax.shard_map(local_step, mesh=mesh, in_specs=in_specs, out_specs=out_specs, check_vma=False)
```
